32 devices in a mesh: section: 2 (over x), patch: 16 (over z, y, core).
Axes of the slice: x: 2, y: 2, z: 4, core: 2. Of those that a mesh axis runs over, the one named last changes fastest.
Arguments:
- latent: bfloat16 [2, 320, 48, 128], P('section', None, 'patch'), may hold values from -20 to 20
- conv_weight: bfloat16 [2, 3, 320, 3, 320], P('section'), may hold values from -0.109375 to 0.109375
- norm_gain: bfloat16 [2, 320], P('section'), may hold values from 0.25 to 1.75
- norm_shift: bfloat16 [2, 320], P('section'), may hold values from -3 to 3
- step_bias: bfloat16 [2, 2, 320], P('section'), may hold values from -3 to 3
- patch_rows: int32 [16], replicated, may hold values from 1 to 3, 40 in all
Outputs:
- section_out: bfloat16 [2, 2, 320, 48, 128], P('section', None, None, 'patch')
The draws below stay inside these ranges and needn't reach their ends.
Inputs may be any that keep to these rules, and one draw needn't show every extreme that they name: `patch_rows`: patch heights in window order; they sum to 40 and the tallest is exactly 3.
All inputs are finite; a program needn't handle non-finite values.
Results may differ from the reference program's by a relative error of at most 0.0045.
Values may be sent and summed in bfloat16 or wider, within the bound.
A program may use at most 64 MiB of HBM per device.

```python
import math
import jax
import jax.numpy as jnp
import numpy as np
from jax import lax

C = 320
GROUPS = 32
COLS = 128
CAP = 3
SAMPLES = 2
ROWS_ALL = 40
PROWS = 48
N_SECTION = 2
N_PATCH = 16


def draw_latent(key, part):
    key_noise, key_cols, key_chan, key_off, key_scale, key_row = jax.random.split(key, 6)
    full_shape = (SAMPLES, C, PROWS, COLS)
    per_group = C // GROUPS
    patch_off = jax.random.uniform(key_off, (N_PATCH, GROUPS), jnp.float32, -2.0, 2.0)
    patch_scale = jnp.exp(jax.random.uniform(key_scale, (N_PATCH, GROUPS), jnp.float32, 0.0, jnp.log(4.0)))
    row_scale = jnp.exp(jax.random.uniform(key_row, (PROWS,), jnp.float32, 0.0, jnp.log(2.0)))
    col_scale = jnp.exp(jax.random.uniform(key_cols, (COLS,), jnp.float32, 0.0, jnp.log(3.0)))
    chan_off = jax.random.uniform(key_chan, (C,), jnp.float32, -0.5, 0.5)
    off_table = jnp.repeat(jnp.repeat(patch_off, CAP, axis=0), per_group, axis=1).T
    scale_table = jnp.repeat(jnp.repeat(patch_scale, CAP, axis=0), per_group, axis=1).T
    offsets = off_table + chan_off[:, None]
    scales = scale_table * row_scale[None, :]
    noise = jnp.clip(jax.random.normal(key_noise, full_shape, jnp.float32), -4.0, 4.0)
    values = (noise + offsets[None, :, :, None]) * scales[None, :, :, None] * col_scale[None, None, None, :] / 8.0
    return values.astype(jnp.bfloat16)


def levels(stream_key, dims, cuts, least, top_value):
    factor_of = 1.0
    for axis_at, parts in cuts:
        draws = jax.random.uniform(jax.random.fold_in(jax.random.fold_in(stream_key, 6), axis_at), (parts,), jnp.float32, least / len(cuts), top_value / len(cuts))
        factor_of = factor_of * jnp.repeat(jnp.exp(draws), dims[axis_at] // parts).reshape((-1,) + (1,) * (len(dims) - 1 - axis_at))
    return factor_of


def split_up(count, total, most, skew):
    portions = [(1 << 20) // math.isqrt(rank ** skew) + 1 for rank in range(2, count + 1)]
    rest, holding = total - most - (count - 1), [1] * (count - 1)
    while rest > 0:
        movable = [i for i in range(count - 1) if holding[i] < most]
        mass, remaining = sum([portions[i] for i in movable]), rest
        for i in movable:
            addition = min(most - holding[i], max(1, remaining * portions[i] // mass), rest)
            holding[i] = holding[i] + addition
            rest = rest - addition
    return np.array([most] + holding)


def ragged(rng, number_of, total, limit, lean):
    if number_of == 2:
        one = jax.random.randint(rng, (), max(1, total - limit), min(limit, total - 1) + 1)
        return jnp.stack([one, total - one])
    lengths = jnp.asarray(split_up(number_of, total, limit, lean), jnp.int32)
    twos = (number_of - 1) // 2
    giver, taker = lengths[1:1 + 2 * twos:2], lengths[2:2 + 2 * twos:2]
    margin = jnp.minimum(giver - 1, limit - taker)
    shifted = jax.random.randint(jax.random.fold_in(rng, 1), (twos,), 0, 1 << 20) % (margin + 1)
    lengths = lengths.at[1:1 + 2 * twos:2].set(giver - shifted).at[2:2 + 2 * twos:2].set(taker + shifted)
    return lengths[jax.random.permutation(jax.random.fold_in(rng, 2), number_of)]


def centred(key, shape, spread, reach, shards=(), kind=jnp.bfloat16):
    level = levels(key, shape, shards, -0.22, 0.18) if shards else 1.0
    drawn = jax.random.normal(key, shape, jnp.float32) * spread * level
    return jnp.minimum(jnp.maximum(drawn, -reach), reach).astype(kind)


def setup_inputs(seed: int = 0) -> dict:
    arg_keys = jax.random.split(jax.random.key(seed), 7)
    return {
        "latent": draw_latent(jax.random.fold_in(arg_keys[6], 71), 0),
        "conv_weight": centred(arg_keys[1], (N_SECTION, 3, C, 3, C), (9 * C) ** -0.5, 0.109375, ((0, 2),)),
        "norm_gain": jnp.clip(1.0 + 0.15 * jax.random.normal(arg_keys[2], (N_SECTION, C), jnp.float32), 0.25, 1.75).astype(jnp.bfloat16),
        "norm_shift": centred(arg_keys[3], (N_SECTION, C), 0.5, 3.0, ((0, 2),)),
        "step_bias": centred(arg_keys[4], (N_SECTION, SAMPLES, C), 0.5, 3.0, ((0, 2),)),
        "patch_rows": ragged(arg_keys[5], N_PATCH, ROWS_ALL, CAP, 2).astype(jnp.int32),
    }


eps = 1e-05

def run_block(current, block_in, is_odd, weight, norm_gain, norm_shift, chan_bias):
    values = current.astype(jnp.float32)
    samples, channels, height, columns = values.shape
    grouped = values.reshape(samples, GROUPS, channels // GROUPS, height * columns)
    group_mean = lax.optimization_barrier(jnp.mean(grouped, axis=(2, 3), keepdims=True))
    centered = grouped - group_mean
    group_var = lax.optimization_barrier(jnp.mean(centered * centered, axis=(2, 3), keepdims=True))
    normed = (centered * lax.rsqrt(group_var + eps)).reshape(samples, channels, height, columns)
    normed = normed * norm_gain.astype(jnp.float32)[None, :, None, None] + norm_shift.astype(jnp.float32)[None, :, None, None]
    activated = jax.nn.silu(normed).astype(jnp.bfloat16)
    padded = jnp.pad(activated.astype(jnp.float32), ((0, 0), (0, 0), (1, 1), (1, 1)))
    conv_out = jnp.zeros((samples, channels, height, columns), jnp.float32)
    for row_off in range(3):
        for col_off in range(3):
            conv_out = conv_out + jnp.einsum('oi,sirc->sorc', weight[col_off, :, row_off, :].astype(jnp.float32), padded[:, :, row_off:row_off + height, col_off:col_off + columns], precision=lax.Precision.HIGHEST)
    conv_out = conv_out + chan_bias.astype(jnp.float32)[:, :, None, None]
    if is_odd:
        return (block_in.astype(jnp.float32) + conv_out).astype(jnp.bfloat16)
    return conv_out.astype(jnp.bfloat16)

def reference(latent, conv_weight, norm_gain, norm_shift, step_bias, patch_rows):
    row_ends = jnp.cumsum(patch_rows).astype(jnp.int32)
    row_starts = (row_ends - patch_rows).astype(jnp.int32)
    window = jnp.arange(ROWS_ALL, dtype=jnp.int32)
    owner_patch = lax.optimization_barrier(jnp.sum((row_ends[None, :] <= window[:, None]).astype(jnp.int32), axis=1)).astype(jnp.int32)
    patch_ids = jnp.arange(N_PATCH, dtype=jnp.int32)
    owner_start = lax.optimization_barrier(jnp.sum(jnp.where(patch_ids[None, :] == owner_patch[:, None], row_starts[None, :], 0), axis=1)).astype(jnp.int32)
    slot_rows = (owner_patch * CAP + window - owner_start).astype(jnp.int32)
    current = jnp.take(latent, slot_rows, axis=2)
    block_in = current
    section_list = []
    for section_index in range(N_SECTION):
        is_odd = section_index % 2 == 1
        if not is_odd:
            block_in = current
        current = run_block(current, block_in, is_odd, conv_weight[section_index], norm_gain[section_index], norm_shift[section_index], step_bias[section_index])
        placed = jnp.zeros((SAMPLES, C, PROWS, COLS), jnp.bfloat16).at[:, :, slot_rows, :].set(current)
        section_list.append(placed)
    return jnp.stack(section_list, axis=0)
```

```python
import functools

import jax
import jax.numpy as jnp
from jax import lax
from jax.experimental import pallas as pl
from jax.experimental.pallas import tpu as pltpu
from jax.sharding import PartitionSpec as P

GROUPS = 32
EPS = 1e-05
MESH = pl.DeviceIdType.MESH
ROWS_OUT = 64


def kernel(
    sections,
    patches,
    heights_in,
    latent_ref,
    weight_ref,
    gain_ref,
    shift_ref,
    bias_ref,
    out_ref,
    lat,
    weights,
    wall,
    xbuf,
    skip,
    obuf,
    edge_lat,
    edge_out,
    heights_ref,
    gain_v,
    shift_v,
    bias_v,
    stat_lat,
    stat_out,
    stat_in,
    gain_b,
    shift_b,
    bias_b,
    ybuf,
    tbuf,
    sum_b,
    sq_b,
    local_sem,
    first_sem,
    ends_rs,
    mid_rs,
    up_rs,
    low_rs,
    stat_rs,
    skip_rs,
    ends_ss,
    mid_ss,
    up_ss,
    low_ss,
    stat_ss,
    skip_ss,
    out_sem,
    sweep,
):
    k = lax.axis_index("section")
    p = lax.axis_index("patch")
    height, channels, columns = lat.shape
    per_group = channels // GROUPS
    is_odd = lax.rem(k, 2) == 1
    last = k == sections - 1
    has_far = jnp.logical_and(is_odd, k + 2 < sections)

    load_lat = pltpu.make_async_copy(latent_ref, lat, local_sem.at[0])
    load_w = pltpu.make_async_copy(weight_ref, weights, local_sem.at[1])
    load_h = pltpu.make_async_copy(heights_in, heights_ref, local_sem.at[2])
    load_g = pltpu.make_async_copy(gain_ref, gain_v, local_sem.at[3])
    load_s = pltpu.make_async_copy(shift_ref, shift_v, local_sem.at[4])
    load_b = pltpu.make_async_copy(bias_ref, bias_v, local_sem.at[5])
    load_h.start()
    load_lat.start()
    load_g.start()
    load_s.start()
    load_b.start()
    load_w.start()

    barrier = pltpu.get_barrier_semaphore()

    def signal(s, q):
        pl.semaphore_signal(barrier, inc=1, device_id=(s, q), device_id_type=MESH)

    near = sections == 2 and patches % 4 == 0
    host, place = p // 4, lax.rem(p, 4)
    hosts = patches // 4
    has_below, has_above = host > 0, host < hosts - 1
    if near:
        for i in range(4):
            q = host * 4 + lax.rem(place + i, 4)
            signal(1 - k, q)
            if i > 0:
                signal(k, q)

        @pl.when(has_below)
        def _():
            signal(k, p - 4)

        @pl.when(has_above)
        def _():
            signal(k, p + 4)
    else:
        @pl.when(k == 0)
        def _():
            def step(i, c):
                q = lax.rem(p + i, patches)
                for s in range(sections):
                    if s == 0:
                        @pl.when(i > 0)
                        def _():
                            signal(0, q)
                    else:
                        signal(s, q)
                return c

            lax.fori_loop(0, patches, step, 0)

        @pl.when(k > 0)
        def _():
            def step(i, c):
                signal(k - 1, lax.rem(p + i, patches))
                return c

            lax.fori_loop(0, patches, step, 0)

            @pl.when(p > 0)
            def _():
                signal(k, p - 1)

            @pl.when(p < patches - 1)
            def _():
                signal(k, p + 1)

        if sections > 2:
            @pl.when(k == 1)
            def _():
                for s in range(2, sections):
                    signal(s, p)

            @pl.when(jnp.logical_and(is_odd, k >= 3))
            def _():
                signal(k - 2, p)

    load_h.wait()
    height_own = heights_ref[p]
    window_rows = heights_ref[0]
    for i in range(1, patches):
        window_rows = window_rows + heights_ref[i]
    inv_count = 1.0 / (
        jnp.full((1, 128), window_rows, jnp.int32).astype(jnp.float32)
        * (per_group * columns)
    )

    chan = lax.broadcasted_iota(jnp.int32, (channels, 128), 0)
    first = lax.broadcasted_iota(jnp.int32, (channels, 128), 1) * per_group
    group_mask = jnp.where(
        jnp.logical_and(chan >= first, chan < first + per_group), 1.0, 0.0
    ).astype(jnp.float32)

    def to_groups(per_chan):
        total = jnp.sum(per_chan, axis=1, keepdims=True)
        return jnp.sum(total * group_mask, axis=0, keepdims=True)

    def to_channels(per_group_row):
        return jnp.sum(per_group_row * group_mask, axis=1, keepdims=True)

    def write_stats(ref, sums, squares):
        ref[...] = to_groups(sums) + pltpu.roll(to_groups(squares), GROUPS, 1)

    load_lat.wait()
    rows = [
        jnp.where(r < height_own, lat[r].astype(jnp.float32), 0.0) for r in range(height)
    ]
    sums, squares, edge = rows[0], rows[0] * rows[0], lat[0]
    for r in range(1, height):
        sums = sums + rows[r]
        squares = squares + rows[r] * rows[r]
        edge = jnp.where(height_own == r + 1, lat[r], edge)
    edge_lat[...] = edge
    write_stats(stat_lat, sums, squares)

    if near:
        pl.semaphore_wait(barrier, 7 + has_below.astype(jnp.int32) + has_above.astype(jnp.int32))
    else:
        sends_to = (
            patches
            - (k == 0).astype(jnp.int32)
            + jnp.where(last, 0, patches)
            + jnp.where(k > 0, (p > 0).astype(jnp.int32) + (p < patches - 1).astype(jnp.int32), 0)
            + (k >= 2).astype(jnp.int32)
            + has_far.astype(jnp.int32)
        )
        pl.semaphore_wait(barrier, sends_to)

    def remote(src, dst, ssem, rsem, s, q):
        return pltpu.make_async_remote_copy(
            src_ref=src, dst_ref=dst, send_sem=ssem, recv_sem=rsem,
            device_id=(s, q), device_id_type=MESH,
        )

    def send_stats(m, s, stat, ssem, own):
        def step(i, c):
            q = lax.rem(p + i, patches)
            remote(stat, stat_in.at[m, p], ssem, stat_rs.at[m], s, q).start()
            return c

        if own is None:
            lax.fori_loop(0, patches, step, 0)
        else:
            lax.fori_loop(1, patches, step, 0)

            @pl.when(own)
            def _():
                pltpu.make_async_copy(stat, stat_in.at[m, p], stat_rs.at[m]).start()

            @pl.when(jnp.logical_not(own))
            def _():
                step(0, 0)

    def send_rows(m, s, head, tail, mid, ssem_ends, ssem_mid):
        remote(head, xbuf.at[m, 1], ssem_ends, ends_rs.at[m], s, p).start()
        remote(tail, xbuf.at[m, 2], ssem_ends, ends_rs.at[m], s, p).start()
        remote(mid, xbuf.at[m, 3], ssem_mid, mid_rs.at[m], s, p).start()

    def pass_on(m, head, tail):
        @pl.when(p < patches - 1)
        def _():
            remote(tail, xbuf.at[m, 0], up_ss.at[m], up_rs.at[m], k, p + 1).start()

        @pl.when(p > 0)
        def _():
            remote(head, xbuf.at[m, 4], low_ss.at[m], low_rs.at[m], k, p - 1).start()

    def first_rows():
        @pl.when(k > 0)
        def _():
            send_rows(k, 0, lat.at[0], edge_lat, lat.at[1], first_sem.at[1], first_sem.at[2])

        @pl.when(k == 1)
        def _():
            pltpu.make_async_copy(lat, skip.at[1], skip_rs.at[1]).start()

        @pl.when(k != 1)
        def _():
            remote(lat, skip.at[k], first_sem.at[3], skip_rs.at[k], 1, p).start()

    if near:
        first_rows()

        def greet(i, q):
            pl.semaphore_signal(sweep.at[i], inc=1, device_id=(k, q), device_id_type=MESH)

        @pl.when(has_below)
        def _():
            pl.semaphore_wait(sweep.at[0], 1)

        @pl.when(has_above)
        def _():
            greet(0, p + 4)
            pl.semaphore_wait(sweep.at[1], 1)

        @pl.when(has_below)
        def _():
            greet(1, p - 4)

    send_stats(k, 0, stat_lat, first_sem.at[0], k == 0)

    @pl.when(k == 0)
    def _():
        pass_on(0, lat.at[0], edge_lat)
        pltpu.make_async_copy(lat.at[0], xbuf.at[0, 1], ends_rs.at[0]).start()
        pltpu.make_async_copy(edge_lat, xbuf.at[0, 2], ends_rs.at[0]).start()
        pltpu.make_async_copy(lat.at[1], xbuf.at[0, 3], mid_rs.at[0]).start()

    if not near:
        first_rows()

    eye = jnp.where(
        lax.broadcasted_iota(jnp.int32, (channels, channels), 0)
        == lax.broadcasted_iota(jnp.int32, (channels, channels), 1),
        1.0,
        0.0,
    ).astype(jnp.bfloat16)

    def spread(row):
        wide = jnp.broadcast_to(row.astype(jnp.float32), (128, channels)).astype(jnp.bfloat16)
        return lax.dot_general(
            eye, wide, (((1,), (1,)), ((), ())), preferred_element_type=jnp.float32
        )

    load_g.wait()
    gain_b[...] = spread(gain_v[...])
    load_s.wait()
    shift_b[...] = spread(shift_v[...])
    load_b.wait()
    for m in range(sections):
        bias_b[m] = spread(bias_v[m : m + 1, :])

    load_w.wait()
    for b in range(3):
        for a in range(3):
            wall[b * channels : (b + 1) * channels, a * channels : (a + 1) * channels] = weights[b, a]

    def wait_for(ref, sem):
        pltpu.make_async_copy(ref, ref, sem).wait()

    lane = lax.broadcasted_iota(jnp.int32, (ROWS_OUT, columns), 1)

    def sample(m, carry):
        wait_for(xbuf.at[m, pl.ds(1, 2)], ends_rs.at[m])

        @pl.when(jnp.logical_or(k > 0, m > 0))
        def _():
            pass_on(m, xbuf.at[m, 1], xbuf.at[m, 2])

        wait_for(stat_in.at[m], stat_rs.at[m])
        total = jnp.sum(stat_in[m], axis=0)
        mean = total * inv_count
        var = pltpu.roll(mean, 128 - GROUPS, 1) - mean * mean
        inv = lax.rsqrt(jnp.maximum(var, 0.0) + EPS)
        scale = to_channels(inv) * gain_b[...]
        offset = shift_b[...] - to_channels(mean) * scale

        def activate(values):
            v = values.astype(jnp.float32) * scale + offset
            half = 0.5 * v
            return half + half * jnp.tanh(half)

        def put(j, value):
            value = value.astype(jnp.bfloat16)
            for a in range(3):
                r = j - a
                if 0 <= r < height:
                    ybuf[a * channels : (a + 1) * channels, r * columns : (r + 1) * columns] = value

        put(1, activate(xbuf[m, 1]))
        tail = activate(xbuf[m, 2])
        wait_for(xbuf.at[m, 3], mid_rs.at[m])
        mid = activate(xbuf[m, 3])

        @pl.when(p > 0)
        def _():
            wait_for(xbuf.at[m, 0], up_rs.at[m])

        @pl.when(p < patches - 1)
        def _():
            wait_for(xbuf.at[m, 4], low_rs.at[m])

        put(0, jnp.where(p > 0, activate(xbuf[m, 0]), 0.0))
        below = jnp.where(p < patches - 1, activate(xbuf[m, 4]), 0.0)
        one, two = height_own == 1, height_own == 2
        put(2, jnp.where(one, below, jnp.where(two, tail, mid)))
        put(3, jnp.where(one, 0.0, jnp.where(two, below, tail)))
        put(4, jnp.where(height_own == 3, below, 0.0))

        tbuf[...] = jnp.dot(wall[...], ybuf[...], preferred_element_type=jnp.float32)

        @pl.when(is_odd)
        def _():
            wait_for(skip.at[m], skip_rs.at[m])

        for c0 in range(0, channels, ROWS_OUT):
            cs = slice(c0, c0 + ROWS_OUT)
            sums = jnp.zeros((ROWS_OUT, columns), jnp.float32)
            squares = sums
            edge = None
            for r in range(height):
                ls = slice(r * columns, (r + 1) * columns)
                left = pltpu.roll(tbuf[c0 : c0 + ROWS_OUT, ls], 1, 1)
                mid = tbuf[channels + c0 : channels + c0 + ROWS_OUT, ls]
                right = pltpu.roll(
                    tbuf[2 * channels + c0 : 2 * channels + c0 + ROWS_OUT, ls], columns - 1, 1
                )
                z = (
                    jnp.where(lane > 0, left, 0.0)
                    + mid
                    + jnp.where(lane < columns - 1, right, 0.0)
                    + bias_b[m, cs]
                )
                z = jnp.where(is_odd, skip[m, r, cs].astype(jnp.float32) + z, z)
                value = jnp.where(r < height_own, z, 0.0).astype(jnp.bfloat16)
                obuf[m, r, cs] = value
                wide = value.astype(jnp.float32)
                sums = sums + wide
                squares = squares + wide * wide
                edge = value if r == 0 else jnp.where(height_own == r + 1, value, edge)
            edge_out[m, cs] = edge
            sum_b[cs] = sums
            sq_b[cs] = squares

        @pl.when(jnp.logical_not(last))
        def _():
            send_rows(
                m, k + 1, obuf.at[m, 0], edge_out.at[m], obuf.at[m, 1], ends_ss.at[m], mid_ss.at[m]
            )
            write_stats(stat_out.at[m], sum_b[...], sq_b[...])
            send_stats(m, k + 1, stat_out.at[m], stat_ss.at[m], None)

        if sections > 2:
            @pl.when(has_far)
            def _():
                remote(obuf.at[m], skip.at[m], skip_ss.at[m], skip_rs.at[m], k + 2, p).start()

        pltpu.make_async_copy(obuf.at[m], out_ref.at[m], out_sem.at[m]).start()
        return carry

    lax.fori_loop(0, sections, sample, 0)

    wait_for(stat_in.at[0, pl.ds(1, patches - 1)], first_sem.at[0])

    @pl.when(k > 0)
    def _():
        wait_for(stat_lat, first_sem.at[0])
        wait_for(xbuf.at[0, pl.ds(0, 2)], first_sem.at[1])
        wait_for(edge_lat, first_sem.at[2])

    @pl.when(k != 1)
    def _():
        wait_for(lat, first_sem.at[3])

    def drain(m, carry):
        @pl.when(p < patches - 1)
        def _():
            wait_for(edge_lat, up_ss.at[m])

        @pl.when(p > 0)
        def _():
            wait_for(edge_lat, low_ss.at[m])

        @pl.when(jnp.logical_not(last))
        def _():
            wait_for(xbuf.at[m, pl.ds(0, 2)], ends_ss.at[m])
            wait_for(edge_lat, mid_ss.at[m])
            wait_for(stat_in.at[m], stat_ss.at[m])

        if sections > 2:
            @pl.when(has_far)
            def _():
                wait_for(obuf.at[m], skip_ss.at[m])

        wait_for(obuf.at[m], out_sem.at[m])
        return carry

    lax.fori_loop(0, sections, drain, 0)


def per_device(sections, patches, latent, conv_weight, norm_gain, norm_shift, step_bias, patch_rows):
    latent = jnp.transpose(latent[0], (1, 0, 2))
    weight = jnp.transpose(conv_weight[0], (0, 2, 1, 3))
    height, channels, columns = latent.shape
    bf16, f32 = jnp.bfloat16, jnp.float32
    hbm = pl.BlockSpec(memory_space=pltpu.HBM)
    dma = pltpu.SemaphoreType.DMA
    out = pl.pallas_call(
        functools.partial(kernel, sections, patches),
        out_shape=jax.ShapeDtypeStruct((sections, height, channels, columns), bf16),
        in_specs=[hbm] * 6,
        out_specs=pl.BlockSpec(memory_space=pl.ANY),
        scratch_shapes=[
            pltpu.VMEM((height, channels, columns), bf16),
            pltpu.VMEM((3, 3, channels, channels), bf16),
            pltpu.VMEM((3 * channels, 3 * channels), bf16),
            pltpu.VMEM((sections, height + 2, channels, columns), bf16),
            pltpu.VMEM((sections, height, channels, columns), bf16),
            pltpu.VMEM((sections, height, channels, columns), bf16),
            pltpu.VMEM((channels, columns), bf16),
            pltpu.VMEM((sections, channels, columns), bf16),
            pltpu.SMEM((patches,), jnp.int32),
            pltpu.VMEM((1, channels), bf16),
            pltpu.VMEM((1, channels), bf16),
            pltpu.VMEM((sections, channels), bf16),
            pltpu.VMEM((1, 128), f32),
            pltpu.VMEM((sections, 1, 128), f32),
            pltpu.VMEM((sections, patches, 1, 128), f32),
            pltpu.VMEM((channels, 128), f32),
            pltpu.VMEM((channels, 128), f32),
            pltpu.VMEM((sections, channels, 128), f32),
            pltpu.VMEM((3 * channels, height * columns), bf16),
            pltpu.VMEM((3 * channels, height * columns), f32),
            pltpu.VMEM((channels, columns), f32),
            pltpu.VMEM((channels, columns), f32),
            dma((6,)),
            dma((4,)),
        ]
        + [dma((sections,)) for _ in range(13)]
        + [pltpu.SemaphoreType.REGULAR((2,))],
        compiler_params=pltpu.CompilerParams(
            collective_id=0, has_side_effects=True, vmem_limit_bytes=48 * 1024 * 1024
        ),
    )(
        *[
            pltpu.with_memory_space_constraint(array, pltpu.HBM)
            for array in (patch_rows, latent, weight, norm_gain, norm_shift, step_bias[0])
        ]
    )
    return jnp.transpose(out, (0, 2, 1, 3))[None]


def solution(mesh):
    placed = (
        P("section", None, "patch", None),
        P("section", None, None, None, None),
        P("section", None),
        P("section", None),
        P("section", None, None),
        P(),
    )
    return jax.shard_map(
        functools.partial(per_device, mesh.shape["section"], mesh.shape["patch"]),
        mesh=mesh,
        in_specs=placed,
        out_specs=P("section", None, None, "patch", None),
        check_vma=False,
    )
```

```python
import functools

import jax
import jax.numpy as jnp
from jax import lax
from jax.experimental import pallas as pl
from jax.experimental.pallas import tpu as pltpu
from jax.sharding import PartitionSpec as P

GROUPS = 32
EPS = 1e-05
MESH = pl.DeviceIdType.MESH
ROWS_OUT = 64
SUB = 3


def kernel(
    sections,
    patches,
    heights_in,
    latent_ref,
    weight_ref,
    gain_ref,
    shift_ref,
    bias_ref,
    out_ref,
    lat,
    weights,
    wall,
    xbuf,
    skip,
    obuf,
    edge_lat,
    edge_out,
    heights_ref,
    gain_v,
    shift_v,
    bias_v,
    stat_lat,
    stat_out,
    stat_in,
    gain_b,
    shift_b,
    bias_b,
    ybuf,
    tbuf,
    sum_b,
    sq_b,
    local_sem,
    first_sem,
    ends_rs,
    mid_rs,
    up_rs,
    low_rs,
    stat_rs,
    skip_rs,
    ends_ss,
    mid_ss,
    up_ss,
    low_ss,
    stat_ss,
    skip_ss,
    out_sem,
):
    k = lax.axis_index("section")
    p = lax.axis_index("patch")
    height, channels, columns = lat.shape
    per_group = channels // GROUPS
    is_odd = lax.rem(k, 2) == 1
    last = k == sections - 1
    has_far = jnp.logical_and(is_odd, k + 2 < sections)

    load_lat = pltpu.make_async_copy(latent_ref, lat, local_sem.at[0])
    load_w = pltpu.make_async_copy(weight_ref, weights, local_sem.at[1])
    load_h = pltpu.make_async_copy(heights_in, heights_ref, local_sem.at[2])
    load_g = pltpu.make_async_copy(gain_ref, gain_v, local_sem.at[3])
    load_s = pltpu.make_async_copy(shift_ref, shift_v, local_sem.at[4])
    load_b = pltpu.make_async_copy(bias_ref, bias_v, local_sem.at[5])
    load_h.start()
    load_lat.start()
    load_g.start()
    load_s.start()
    load_b.start()
    load_w.start()

    barrier = pltpu.get_barrier_semaphore()

    def signal(s, q):
        pl.semaphore_signal(barrier, inc=1, device_id=(s, q), device_id_type=MESH)

    @pl.when(k == 0)
    def _():
        def step(i, c):
            q = lax.rem(p + i, patches)
            for s in range(sections):
                if s == 0:
                    @pl.when(i > 0)
                    def _():
                        signal(0, q)
                else:
                    signal(s, q)
            return c

        lax.fori_loop(0, patches, step, 0)

    @pl.when(k > 0)
    def _():
        def step(i, c):
            signal(k - 1, lax.rem(p + i, patches))
            return c

        lax.fori_loop(0, patches, step, 0)

        @pl.when(p > 0)
        def _():
            signal(k, p - 1)

        @pl.when(p < patches - 1)
        def _():
            signal(k, p + 1)

    if sections > 2:
        @pl.when(k == 1)
        def _():
            for s in range(2, sections):
                signal(s, p)

        @pl.when(jnp.logical_and(is_odd, k >= 3))
        def _():
            signal(k - 2, p)

    load_h.wait()
    height_own = heights_ref[p]
    window_rows = heights_ref[0]
    for i in range(1, patches):
        window_rows = window_rows + heights_ref[i]
    inv_count = 1.0 / (
        jnp.full((1, 128), window_rows, jnp.int32).astype(jnp.float32)
        * (per_group * columns)
    )

    chan = lax.broadcasted_iota(jnp.int32, (channels, 128), 0)
    first = lax.broadcasted_iota(jnp.int32, (channels, 128), 1) * per_group
    group_mask = jnp.where(
        jnp.logical_and(chan >= first, chan < first + per_group), 1.0, 0.0
    ).astype(jnp.float32)

    def to_groups(per_chan):
        total = jnp.sum(per_chan, axis=1, keepdims=True)
        return jnp.sum(total * group_mask, axis=0, keepdims=True)

    def to_channels(per_group_row):
        return jnp.sum(per_group_row * group_mask, axis=1, keepdims=True)

    def write_stats(ref, sums, squares):
        ref[...] = to_groups(sums) + pltpu.roll(to_groups(squares), GROUPS, 1)

    load_lat.wait()
    rows = [
        jnp.where(r < height_own, lat[r].astype(jnp.float32), 0.0) for r in range(height)
    ]
    sums, squares, edge = rows[0], rows[0] * rows[0], lat[0]
    for r in range(1, height):
        sums = sums + rows[r]
        squares = squares + rows[r] * rows[r]
        edge = jnp.where(height_own == r + 1, lat[r], edge)
    edge_lat[...] = edge
    write_stats(stat_lat, sums, squares)

    sends_to = (
        patches
        - (k == 0).astype(jnp.int32)
        + jnp.where(last, 0, patches)
        + jnp.where(k > 0, (p > 0).astype(jnp.int32) + (p < patches - 1).astype(jnp.int32), 0)
        + (k >= 2).astype(jnp.int32)
        + has_far.astype(jnp.int32)
    )
    pl.semaphore_wait(barrier, sends_to)

    def remote(src, dst, ssem, rsem, s, q):
        return pltpu.make_async_remote_copy(
            src_ref=src, dst_ref=dst, send_sem=ssem, recv_sem=rsem,
            device_id=(s, q), device_id_type=MESH,
        )

    def send_stats(m, s, stat, ssem, own):
        def step(i, c):
            q = lax.rem(p + i, patches)
            remote(stat, stat_in.at[m, p], ssem, stat_rs.at[m], s, q).start()
            return c

        if own is None:
            lax.fori_loop(0, patches, step, 0)
        else:
            lax.fori_loop(1, patches, step, 0)

            @pl.when(own)
            def _():
                pltpu.make_async_copy(stat, stat_in.at[m, p], stat_rs.at[m]).start()

            @pl.when(jnp.logical_not(own))
            def _():
                step(0, 0)

    def send_rows(m, s, head, tail, mid, ssem_ends, ssem_mid):
        remote(head, xbuf.at[m, 1], ssem_ends, ends_rs.at[m], s, p).start()
        remote(tail, xbuf.at[m, 2], ssem_ends, ends_rs.at[m], s, p).start()
        remote(mid, xbuf.at[m, 3], ssem_mid, mid_rs.at[m], s, p).start()

    def pass_on(m, head, tail):
        @pl.when(p < patches - 1)
        def _():
            remote(tail, xbuf.at[m, 0], up_ss.at[m], up_rs.at[m], k, p + 1).start()

        @pl.when(p > 0)
        def _():
            remote(head, xbuf.at[m, 4], low_ss.at[m], low_rs.at[m], k, p - 1).start()

    send_stats(k, 0, stat_lat, first_sem.at[0], k == 0)

    @pl.when(k == 0)
    def _():
        pass_on(0, lat.at[0], edge_lat)
        pltpu.make_async_copy(lat.at[0], xbuf.at[0, 1], ends_rs.at[0]).start()
        pltpu.make_async_copy(edge_lat, xbuf.at[0, 2], ends_rs.at[0]).start()
        pltpu.make_async_copy(lat.at[1], xbuf.at[0, 3], mid_rs.at[0]).start()

    @pl.when(k > 0)
    def _():
        send_rows(k, 0, lat.at[0], edge_lat, lat.at[1], first_sem.at[1], first_sem.at[2])

    @pl.when(k == 1)
    def _():
        pltpu.make_async_copy(lat, skip.at[1], skip_rs.at[1]).start()

    @pl.when(k != 1)
    def _():
        remote(lat, skip.at[k], first_sem.at[3], skip_rs.at[k], 1, p).start()

    eye = jnp.where(
        lax.broadcasted_iota(jnp.int32, (channels, channels), 0)
        == lax.broadcasted_iota(jnp.int32, (channels, channels), 1),
        1.0,
        0.0,
    ).astype(jnp.bfloat16)

    def spread(row):
        wide = jnp.broadcast_to(row.astype(jnp.float32), (128, channels)).astype(jnp.bfloat16)
        return lax.dot_general(
            eye, wide, (((1,), (1,)), ((), ())), preferred_element_type=jnp.float32
        )

    load_g.wait()
    gain_b[...] = spread(gain_v[...])
    load_s.wait()
    shift_b[...] = spread(shift_v[...])
    load_b.wait()
    for m in range(sections):
        bias_b[m] = spread(bias_v[m : m + 1, :])

    load_w.wait()
    for b in range(3):
        for a in range(3):
            wall[b * channels : (b + 1) * channels, a * channels : (a + 1) * channels] = weights[b, a]

    def wait_for(ref, sem):
        pltpu.make_async_copy(ref, ref, sem).wait()

    lane = lax.broadcasted_iota(jnp.int32, (ROWS_OUT, columns), 1)

    def sample(m, carry):
        wait_for(xbuf.at[m, pl.ds(1, 2)], ends_rs.at[m])

        @pl.when(jnp.logical_or(k > 0, m > 0))
        def _():
            pass_on(m, xbuf.at[m, 1], xbuf.at[m, 2])

        wait_for(stat_in.at[m], stat_rs.at[m])
        total = jnp.sum(stat_in[m], axis=0)
        mean = total * inv_count
        var = pltpu.roll(mean, 128 - GROUPS, 1) - mean * mean
        inv = lax.rsqrt(jnp.maximum(var, 0.0) + EPS)
        scale = to_channels(inv) * gain_b[...]
        offset = shift_b[...] - to_channels(mean) * scale

        def activate(values):
            v = values.astype(jnp.float32) * scale + offset
            half = 0.5 * v
            return half + half * jnp.tanh(half)

        def put(j, value):
            value = value.astype(jnp.bfloat16)
            for a in range(3):
                r = j - a
                if 0 <= r < height:
                    ybuf[a * channels : (a + 1) * channels, r * columns : (r + 1) * columns] = value

        put(1, activate(xbuf[m, 1]))
        tail = activate(xbuf[m, 2])
        wait_for(xbuf.at[m, 3], mid_rs.at[m])
        mid = activate(xbuf[m, 3])

        @pl.when(p > 0)
        def _():
            wait_for(xbuf.at[m, 0], up_rs.at[m])

        @pl.when(p < patches - 1)
        def _():
            wait_for(xbuf.at[m, 4], low_rs.at[m])

        put(0, jnp.where(p > 0, activate(xbuf[m, 0]), 0.0))
        below = jnp.where(p < patches - 1, activate(xbuf[m, 4]), 0.0)
        one, two = height_own == 1, height_own == 2
        put(2, jnp.where(one, below, jnp.where(two, tail, mid)))
        put(3, jnp.where(one, 0.0, jnp.where(two, below, tail)))
        put(4, jnp.where(height_own == 3, below, 0.0))

        tbuf[...] = jnp.dot(wall[...], ybuf[...], preferred_element_type=jnp.float32)

        @pl.when(is_odd)
        def _():
            wait_for(skip.at[m], skip_rs.at[m])

        for c0 in range(0, channels, ROWS_OUT):
            cs = slice(c0, c0 + ROWS_OUT)
            sums = jnp.zeros((ROWS_OUT, columns), jnp.float32)
            squares = sums
            edge = None
            for r in range(height):
                ls = slice(r * columns, (r + 1) * columns)
                left = pltpu.roll(tbuf[c0 : c0 + ROWS_OUT, ls], 1, 1)
                mid = tbuf[channels + c0 : channels + c0 + ROWS_OUT, ls]
                right = pltpu.roll(
                    tbuf[2 * channels + c0 : 2 * channels + c0 + ROWS_OUT, ls], columns - 1, 1
                )
                z = (
                    jnp.where(lane > 0, left, 0.0)
                    + mid
                    + jnp.where(lane < columns - 1, right, 0.0)
                    + bias_b[m, cs]
                )
                z = jnp.where(is_odd, skip[m, r, cs].astype(jnp.float32) + z, z)
                value = jnp.where(r < height_own, z, 0.0).astype(jnp.bfloat16)
                obuf[m, r, cs] = value
                wide = value.astype(jnp.float32)
                sums = sums + wide
                squares = squares + wide * wide
                edge = value if r == 0 else jnp.where(height_own == r + 1, value, edge)
            edge_out[m, cs] = edge
            sum_b[cs] = sums
            sq_b[cs] = squares

        @pl.when(jnp.logical_not(last))
        def _():
            send_rows(
                m, k + 1, obuf.at[m, 0], edge_out.at[m], obuf.at[m, 1], ends_ss.at[m], mid_ss.at[m]
            )
            write_stats(stat_out.at[m], sum_b[...], sq_b[...])
            send_stats(m, k + 1, stat_out.at[m], stat_ss.at[m], None)

        if sections > 2:
            @pl.when(has_far)
            def _():
                remote(obuf.at[m], skip.at[m], skip_ss.at[m], skip_rs.at[m], k + 2, p).start()

        pltpu.make_async_copy(obuf.at[m], out_ref.at[m], out_sem.at[m]).start()
        return carry

    lax.fori_loop(0, sections, sample, 0)

    wait_for(stat_in.at[0, pl.ds(1, patches - 1)], first_sem.at[0])

    @pl.when(k > 0)
    def _():
        wait_for(stat_lat, first_sem.at[0])
        wait_for(xbuf.at[0, pl.ds(0, 2)], first_sem.at[1])
        wait_for(edge_lat, first_sem.at[2])

    @pl.when(k != 1)
    def _():
        wait_for(lat, first_sem.at[3])

    def drain(m, carry):
        @pl.when(p < patches - 1)
        def _():
            wait_for(edge_lat, up_ss.at[m])

        @pl.when(p > 0)
        def _():
            wait_for(edge_lat, low_ss.at[m])

        @pl.when(jnp.logical_not(last))
        def _():
            wait_for(xbuf.at[m, pl.ds(0, 2)], ends_ss.at[m])
            wait_for(edge_lat, mid_ss.at[m])
            wait_for(stat_in.at[m], stat_ss.at[m])

        if sections > 2:
            @pl.when(has_far)
            def _():
                wait_for(obuf.at[m], skip_ss.at[m])

        wait_for(obuf.at[m], out_sem.at[m])
        return carry

    lax.fori_loop(0, sections, drain, 0)


def paired_kernel(
    patches,
    local,
    heights_in,
    latent_ref,
    weight_ref,
    gain_ref,
    shift_ref,
    bias_ref,
    out_ref,
    lat,
    weights,
    wall,
    part,
    xin,
    xmid,
    obuf,
    ends,
    heights_ref,
    gain_v,
    shift_v,
    bias_v,
    params,
    params_in,
    stat_lat,
    stat_own,
    stat_all,
    total_out,
    total_in,
    stat_mid,
    stat_mid_all,
    gain_b,
    shift_b,
    bias_b,
    ybuf,
    tbuf,
    sum_b,
    sq_b,
    load_sem,
    ready,
    small_rs,
    small_ss,
    row_rs,
    row_ss,
    edge_rs,
    edge_ss,
    seed_rs,
    seed_ss,
    share_rs,
    share_ss,
    core_rs,
    core_ss,
    mid_rs,
    mid_ss,
    own_edge_rs,
    own_edge_ss,
    far_edge_rs,
    far_edge_ss,
    stat_rs,
    stat_ss,
    out_sem,
):
    k = lax.axis_index("section")
    p = lax.axis_index("patch")
    height, channels, columns = lat.shape
    per_group = channels // GROUPS
    rest = channels - local
    piece = part.shape[0] // (8 * SUB)

    core = lax.rem(p, 2)
    mate = p + 1 - 2 * core
    across = p - 1 + 2 * core
    has_across = jnp.logical_and(across >= 0, across < patches)
    member = lax.rem(p, 8)
    turn_y = 2 - 4 * lax.rem(member // 2, 2)
    turn_z = 4 - 8 * (member // 4)
    friends = (p + turn_y, p + turn_z, p + turn_y + turn_z)

    load_h = pltpu.make_async_copy(heights_in, heights_ref, load_sem.at[0])
    load_lat = pltpu.make_async_copy(latent_ref, lat, load_sem.at[1])
    load_g = pltpu.make_async_copy(gain_ref, gain_v, load_sem.at[2])
    load_s = pltpu.make_async_copy(shift_ref, shift_v, load_sem.at[3])
    load_b = pltpu.make_async_copy(bias_ref, bias_v, load_sem.at[4])
    load_w = pltpu.make_async_copy(weight_ref, weights, load_sem.at[5])
    for load in (load_h, load_lat, load_g, load_s, load_b, load_w):
        load.start()

    barrier = pltpu.get_barrier_semaphore()

    def signal(s, q):
        pl.semaphore_signal(barrier, inc=1, device_id=(s, q), device_id_type=MESH)

    @pl.when(k == 0)
    def _():
        signal(1, p)

        def step(i, carry):
            signal(0, lax.rem(p + i, patches))
            return carry

        lax.fori_loop(1, patches, step, 0)

    @pl.when(k == 1)
    def _():
        for q in (mate, *friends):
            signal(1, q)

        @pl.when(has_across)
        def _():
            signal(1, across)

    def remote(src, dst, ssem, rsem, s, q):
        return pltpu.make_async_remote_copy(
            src_ref=src, dst_ref=dst, send_sem=ssem, recv_sem=rsem,
            device_id=(s, q), device_id_type=MESH,
        )

    def wait_for(ref, sem):
        pltpu.make_async_copy(ref, ref, sem).wait()

    load_h.wait()
    height_own = heights_ref[p]
    window_rows = heights_ref[0]
    for i in range(1, patches):
        window_rows = window_rows + heights_ref[i]
    inv_count = 1.0 / (
        jnp.full((1, 128), window_rows, jnp.int32).astype(jnp.float32)
        * (per_group * columns)
    )

    chan = lax.broadcasted_iota(jnp.int32, (channels, 128), 0)
    first = lax.broadcasted_iota(jnp.int32, (channels, 128), 1) * per_group
    group_mask = jnp.where(
        jnp.logical_and(chan >= first, chan < first + per_group), 1.0, 0.0
    ).astype(jnp.float32)

    def to_groups(per_chan):
        total = jnp.sum(per_chan, axis=1, keepdims=True)
        return jnp.sum(total * group_mask, axis=0, keepdims=True)

    def to_channels(per_group_row):
        return jnp.sum(per_group_row * group_mask, axis=1, keepdims=True)

    def both(sums, squares):
        return to_groups(sums) + pltpu.roll(to_groups(squares), GROUPS, 1)

    load_lat.wait()
    rows = [
        jnp.where(r < height_own, lat[r].astype(jnp.float32), 0.0) for r in range(height)
    ]
    sums, squares, edge = rows[0], rows[0] * rows[0], lat[0]
    for r in range(1, height):
        sums = sums + rows[r]
        squares = squares + rows[r] * rows[r]
        edge = jnp.where(height_own == r + 1, lat[r], edge)
    xin[k, 1] = lat[0]
    xin[k, 2] = edge
    xin[k, 3] = lat[1]
    stat_lat[...] = both(sums, squares)

    load_g.wait()
    load_s.wait()
    load_b.wait()
    params[0:1] = gain_v[...].astype(jnp.float32)
    params[1:2] = shift_v[...].astype(jnp.float32)
    params[2:4] = bias_v[...].astype(jnp.float32)

    eye = jnp.where(
        lax.broadcasted_iota(jnp.int32, (channels, channels), 0)
        == lax.broadcasted_iota(jnp.int32, (channels, channels), 1),
        1.0,
        0.0,
    ).astype(jnp.bfloat16)

    def spread(row):
        wide = jnp.broadcast_to(row, (128, channels)).astype(jnp.bfloat16)
        return lax.dot_general(
            eye, wide, (((1,), (1,)), ((), ())), preferred_element_type=jnp.float32
        )

    def spread_params(at, source):
        gain_b[at] = spread(source[0:1])
        shift_b[at] = spread(source[1:2])
        for m in range(2):
            bias_b[at, m] = spread(source[2 + m : 3 + m])

    spread_params(0, params)

    load_w.wait()
    for b in range(3):
        for a in range(3):
            cols = slice(a * channels, (a + 1) * channels)
            wall[b * local : (b + 1) * local, cols] = weights[b, a, :local]
            start = 3 * local + b * rest
            wall[start : start + rest, cols] = weights[b, a, local:]

    cross_slot, other_slot = 1 + core, 2 - core

    def send_rows():
        for i, slot in enumerate((cross_slot, other_slot, 3)):
            remote(xin.at[k, slot], xin.at[k, slot], row_ss.at[i], row_rs.at[i], 1 - k, p).start()

    def wait_row(i):
        wait_for(lat.at[0], row_rs.at[i])

    def send_edge(kind, ref, m, span, ssem, rsem):
        src_slot = cross_slot if kind == 0 else other_slot
        dst_slot = 4 - 4 * core if kind == 0 else 4 * core
        q = across if kind == 0 else mate

        def go():
            remote(
                ref.at[m, src_slot, span], ref.at[m, dst_slot, span],
                ssem.at[m, kind], rsem.at[m, kind], k, q,
            ).start()

        if kind == 0:
            pl.when(has_across)(go)
        else:
            go()

    def wait_edge(kind, ref, sem, m):
        if kind == 0:
            @pl.when(has_across)
            def _():
                wait_for(ref, sem.at[m, kind])
        else:
            wait_for(ref, sem.at[m, kind])

    whole = pl.ds(0, channels)
    head_part = pl.ds(0, local)
    tail_part = pl.ds(local, rest)

    def pass_in(kind, m):
        send_edge(kind, xin, m, whole, edge_ss, edge_rs)

    def coefficients(total, at):
        mean = total * inv_count
        var = pltpu.roll(mean, 128 - GROUPS, 1) - mean * mean
        inv = lax.rsqrt(jnp.maximum(var, 0.0) + EPS)
        scale = to_channels(inv) * gain_b[at]
        return scale, shift_b[at] - to_channels(mean) * scale

    def fill(rows_of, m, scale, offset, before_edges):
        def activate(values):
            v = values.astype(jnp.float32) * scale + offset
            half = 0.5 * v
            return half + half * jnp.tanh(half)

        def put(j, value):
            value = value.astype(jnp.bfloat16)
            for a in range(3):
                r = j - a
                if 0 <= r < height:
                    at = (m * height + r) * columns
                    ybuf[a * channels : (a + 1) * channels, at : at + columns] = value

        put(1, activate(rows_of[m, 1]))
        tail = activate(rows_of[m, 2])
        mid = activate(rows_of[m, 3])
        before_edges()
        put(0, jnp.where(p > 0, activate(rows_of[m, 0]), 0.0))
        below = jnp.where(p < patches - 1, activate(rows_of[m, 4]), 0.0)
        one, two = height_own == 1, height_own == 2
        put(2, jnp.where(one, below, jnp.where(two, tail, mid)))
        put(3, jnp.where(one, 0.0, jnp.where(two, below, tail)))
        put(4, jnp.where(height_own == 3, below, 0.0))

    lane = lax.broadcasted_iota(jnp.int32, (ROWS_OUT, columns), 1)

    def conv_row(m, r, c0, count, bias):
        at = (m * height + r) * columns
        ls = slice(at, at + columns)

        def block(b):
            start = b * local + c0 if c0 < local else 3 * local + b * rest + c0 - local
            return tbuf[start : start + count, ls]

        return (
            jnp.where(lane > 0, pltpu.roll(block(0), 1, 1), 0.0)
            + block(1)
            + jnp.where(lane < columns - 1, pltpu.roll(block(2), columns - 1, 1), 0.0)
            + bias
        )

    def send_mid(i, m):
        src = (ends.at[m, core], ends.at[m, 1 - core], obuf.at[m, 1])[i]
        slot = (cross_slot, other_slot, 3)[i]
        remote(
            src.at[tail_part], xmid.at[m, slot, tail_part], mid_ss.at[m, i], mid_rs.at[m, i], 1, p
        ).start()

    def multiply(count, m0, samples):
        cols = slice(m0 * height * columns, (m0 + samples) * height * columns)
        tbuf[:count, cols] = jnp.dot(
            wall[...] if count > 3 * local else part[...],
            ybuf[:, cols],
            preferred_element_type=jnp.float32,
        )

    @pl.when(k == 1)
    def _():
        pl.semaphore_wait(barrier, 5 + has_across.astype(jnp.int32))
        pl.semaphore_signal(ready, inc=1, device_id=(0, p), device_id_type=MESH)
        remote(stat_lat, stat_own.at[1], small_ss.at[1], small_rs.at[1], 0, p).start()
        send_rows()
        pass_in(0, 1)
        pass_in(1, 1)

    @pl.when(k == 0)
    def _():
        stat_own[0] = stat_lat[...]
        pl.semaphore_wait(ready, 1)
        remote(params, params_in, small_ss.at[0], small_rs.at[0], 1, p).start()
        for i in range(SUB):
            at = pl.ds((member * SUB + i) * piece, piece)
            remote(wall.at[at], part.at[at], seed_ss.at[i], seed_rs.at[i], 1, p).start()
        send_rows()

        wait_for(stat_lat, small_rs.at[1])
        pl.semaphore_wait(barrier, patches - 1)

        def step(i, carry):
            q = lax.rem(p + i, patches)
            remote(stat_own, stat_all.at[p], small_ss.at[2], small_rs.at[2], 0, q).start()
            return carry

        lax.fori_loop(1, patches, step, 0)
        stat_all[p] = stat_own[...]
        pass_in(0, 0)
        pass_in(1, 0)
        wait_row(0)
        pass_in(0, 1)
        wait_for(stat_all.at[pl.ds(0, patches - 1)], small_rs.at[2])
        totals = jnp.sum(stat_all[...], axis=0)
        total_out[...] = totals
        remote(total_out, total_in, small_ss.at[3], small_rs.at[3], 1, p).start()

        for m in range(2):
            scale, offset = coefficients(totals[m], 0)

            def before_edges():
                if m == 0:
                    wait_row(1)
                    pass_in(1, 1)
                for kind in range(2):
                    wait_edge(kind, lat.at[0], edge_rs, m)

            if m == 1:
                wait_row(2)
            fill(xin, m, scale, offset, before_edges)
            multiply(3 * channels, m, 1)
            for c0 in range(0, channels, ROWS_OUT):
                cs = slice(c0, c0 + ROWS_OUT)
                sums = jnp.zeros((ROWS_OUT, columns), jnp.float32)
                squares = sums
                edge = None
                for r in range(height):
                    z = conv_row(m, r, c0, ROWS_OUT, bias_b[0, m, cs])
                    value = jnp.where(r < height_own, z, 0.0).astype(jnp.bfloat16)
                    obuf[m, r, cs] = value
                    wide = value.astype(jnp.float32)
                    sums = sums + wide
                    squares = squares + wide * wide
                    edge = value if r == 0 else jnp.where(height_own == r + 1, value, edge)
                    if r == 0:
                        ends[m, 0, cs] = value
                ends[m, 1, cs] = edge
                sum_b[cs] = sums
                sq_b[cs] = squares
            stat_mid[m] = both(sum_b[...], sq_b[...])

            def step(i, carry):
                q = lax.rem(p + i, patches)
                remote(stat_mid.at[m], stat_mid_all.at[m, p], stat_ss.at[m], stat_rs.at[m], 1, q).start()
                return carry

            lax.fori_loop(0, patches, step, 0)
            send_mid(0, m)
            send_mid(1, m)
            pltpu.make_async_copy(obuf.at[m], out_ref.at[m], out_sem.at[m]).start()
        send_mid(2, 0)
        send_mid(2, 1)

        wait_for(params, small_ss.at[0])
        wait_for(stat_all.at[pl.ds(0, patches - 1)], small_ss.at[2])
        wait_for(total_out, small_ss.at[3])
        for i in range(SUB):
            wait_for(part.at[pl.ds(0, piece)], seed_ss.at[i])
        for m in range(2):
            wait_for(stat_mid_all.at[m], stat_ss.at[m])
            for i in range(3):
                wait_for(obuf.at[m, 1, tail_part], mid_ss.at[m, i])

    @pl.when(k == 1)
    def _():
        def to_mate(index, sem):
            at = pl.ds(index * piece, piece)
            remote(part.at[at], part.at[at], core_ss.at[sem], core_rs.at[0], 1, mate).start()

        def seed(i, carry):
            index = member * SUB + i
            at = pl.ds(index * piece, piece)
            wait_for(part.at[pl.ds(0, piece)], seed_rs.at[i])
            for j in range(3):
                remote(
                    part.at[at], part.at[at], share_ss.at[j, i], share_rs.at[j, i], 1, friends[j]
                ).start()
            to_mate(index, i)
            return carry

        lax.fori_loop(0, SUB, seed, 0)
        wait_for(params, small_rs.at[0])
        spread_params(1, params_in)
        wait_row(0)
        pass_in(0, 0)

        def shared(i, carry):
            for j in range(3):
                wait_for(part.at[pl.ds(0, piece)], share_rs.at[j, i])
                to_mate(lax.rem(friends[j], 8) * SUB + i, (1 + j) * SUB + i)
            return carry

        lax.fori_loop(0, SUB, shared, 0)
        wait_row(1)
        pass_in(1, 0)
        wait_for(total_out, small_rs.at[3])
        totals = total_in[...]
        for m in (1, 0):
            scale, offset = coefficients(totals[m], 1)

            def before_edges():
                for kind in range(2):
                    wait_edge(kind, lat.at[0], edge_rs, m)

            if m == 0:
                wait_row(2)
            fill(xin, m, scale, offset, before_edges)
        wait_for(part.at[pl.ds(0, 4 * SUB * piece)], core_rs.at[0])
        multiply(3 * local, 0, 2)
        for m in (0, 1):
            for c0 in range(0, local, ROWS_OUT):
                cs = slice(c0, c0 + ROWS_OUT)
                edge = None
                for r in range(height):
                    value = conv_row(m, r, c0, ROWS_OUT, bias_b[1, m, cs]).astype(jnp.bfloat16)
                    edge = value if r == 0 else jnp.where(height_own == r + 1, value, edge)
                    if r == 0:
                        xmid[m, 1, cs] = value
                    if r == 1:
                        xmid[m, 3, cs] = value
                xmid[m, 2, cs] = edge
            for kind in range(2):
                send_edge(kind, xmid, m, head_part, own_edge_ss, own_edge_rs)
        for m in range(2):
            for kind in range(2):
                wait_for(obuf.at[m, 1, tail_part], mid_rs.at[m, kind])
                send_edge(kind, xmid, m, tail_part, far_edge_ss, far_edge_rs)

        for m in range(2):
            wait_for(stat_mid_all.at[m], stat_rs.at[m])
            scale, offset = coefficients(jnp.sum(stat_mid_all[m], axis=0), 0)
            wait_for(obuf.at[m, 1, tail_part], mid_rs.at[m, 2])

            def before_edges():
                for kind in range(2):
                    wait_edge(kind, lat.at[0, head_part], own_edge_rs, m)
                    wait_edge(kind, lat.at[0, tail_part], far_edge_rs, m)

            fill(xmid, m, scale, offset, before_edges)
            multiply(3 * channels, m, 1)
            for c0 in range(0, channels, ROWS_OUT):
                cs = slice(c0, c0 + ROWS_OUT)
                for r in range(height):
                    z = conv_row(m, r, c0, ROWS_OUT, bias_b[0, m, cs])
                    z = xin[m, (1, 3, 2)[r], cs].astype(jnp.float32) + z
                    obuf[m, r, cs] = jnp.where(r < height_own, z, 0.0).astype(jnp.bfloat16)
            pltpu.make_async_copy(obuf.at[m], out_ref.at[m], out_sem.at[m]).start()

        wait_for(stat_lat, small_ss.at[1])
        for i in range(SUB):
            for j in range(3):
                wait_for(part.at[pl.ds(0, piece)], share_ss.at[j, i])
        for i in range(4 * SUB):
            wait_for(part.at[pl.ds(0, piece)], core_ss.at[i])
        for m in range(2):
            for kind in range(2):
                wait_edge(kind, lat.at[0, head_part], own_edge_ss, m)
                wait_edge(kind, lat.at[0, tail_part], far_edge_ss, m)

    for i in range(3):
        wait_for(lat.at[0], row_ss.at[i])
    for m in range(2):
        for kind in range(2):
            wait_edge(kind, lat.at[0], edge_ss, m)
        wait_for(obuf.at[m], out_sem.at[m])


def paired_call(patches, operands, height, channels, columns):
    bf16, f32 = jnp.bfloat16, jnp.float32
    local = channels * 2 // 5
    hbm = pl.BlockSpec(memory_space=pltpu.HBM)
    dma = pltpu.SemaphoreType.DMA
    return pl.pallas_call(
        functools.partial(paired_kernel, patches, local),
        out_shape=jax.ShapeDtypeStruct((2, height, channels, columns), bf16),
        in_specs=[hbm] * 6,
        out_specs=pl.BlockSpec(memory_space=pl.ANY),
        scratch_shapes=[
            pltpu.VMEM((height, channels, columns), bf16),
            pltpu.VMEM((3, 3, channels, channels), bf16),
            pltpu.VMEM((3 * channels, 3 * channels), bf16),
            pltpu.VMEM((3 * local, 3 * channels), bf16),
            pltpu.VMEM((2, height + 2, channels, columns), bf16),
            pltpu.VMEM((2, height + 2, channels, columns), bf16),
            pltpu.VMEM((2, height, channels, columns), bf16),
            pltpu.VMEM((2, 2, channels, columns), bf16),
            pltpu.SMEM((patches,), jnp.int32),
            pltpu.VMEM((1, channels), bf16),
            pltpu.VMEM((1, channels), bf16),
            pltpu.VMEM((2, channels), bf16),
            pltpu.VMEM((8, channels), f32),
            pltpu.VMEM((8, channels), f32),
            pltpu.VMEM((1, 128), f32),
            pltpu.VMEM((2, 1, 128), f32),
            pltpu.VMEM((patches, 2, 1, 128), f32),
            pltpu.VMEM((2, 1, 128), f32),
            pltpu.VMEM((2, 1, 128), f32),
            pltpu.VMEM((2, 1, 128), f32),
            pltpu.VMEM((2, patches, 1, 128), f32),
            pltpu.VMEM((2, channels, 128), f32),
            pltpu.VMEM((2, channels, 128), f32),
            pltpu.VMEM((2, 2, channels, 128), f32),
            pltpu.VMEM((3 * channels, 2 * height * columns), bf16),
            pltpu.VMEM((3 * channels, 2 * height * columns), f32),
            pltpu.VMEM((channels, columns), f32),
            pltpu.VMEM((channels, columns), f32),
            dma((6,)),
            pltpu.SemaphoreType.REGULAR,
            dma((4,)),
            dma((4,)),
            dma((3,)),
            dma((3,)),
            dma((2, 2)),
            dma((2, 2)),
            dma((SUB,)),
            dma((SUB,)),
            dma((3, SUB)),
            dma((3, SUB)),
            dma((1,)),
            dma((4 * SUB,)),
            dma((2, 3)),
            dma((2, 3)),
            dma((2, 2)),
            dma((2, 2)),
            dma((2, 2)),
            dma((2, 2)),
            dma((2,)),
            dma((2,)),
            dma((2,)),
        ],
        compiler_params=pltpu.CompilerParams(
            collective_id=0, has_side_effects=True, vmem_limit_bytes=48 * 1024 * 1024
        ),
    )(*operands)


def per_device(sections, patches, latent, conv_weight, norm_gain, norm_shift, step_bias, patch_rows):
    latent = jnp.transpose(latent[0], (1, 0, 2))
    weight = jnp.transpose(conv_weight[0], (0, 2, 1, 3))
    height, channels, columns = latent.shape
    bf16, f32 = jnp.bfloat16, jnp.float32
    hbm = pl.BlockSpec(memory_space=pltpu.HBM)
    dma = pltpu.SemaphoreType.DMA
    operands = [
        pltpu.with_memory_space_constraint(array, pltpu.HBM)
        for array in (patch_rows, latent, weight, norm_gain, norm_shift, step_bias[0])
    ]
    if sections == 2 and patches % 8 == 0:
        out = paired_call(patches, operands, height, channels, columns)
        return jnp.transpose(out, (0, 2, 1, 3))[None]
    out = pl.pallas_call(
        functools.partial(kernel, sections, patches),
        out_shape=jax.ShapeDtypeStruct((sections, height, channels, columns), bf16),
        in_specs=[hbm] * 6,
        out_specs=pl.BlockSpec(memory_space=pl.ANY),
        scratch_shapes=[
            pltpu.VMEM((height, channels, columns), bf16),
            pltpu.VMEM((3, 3, channels, channels), bf16),
            pltpu.VMEM((3 * channels, 3 * channels), bf16),
            pltpu.VMEM((sections, height + 2, channels, columns), bf16),
            pltpu.VMEM((sections, height, channels, columns), bf16),
            pltpu.VMEM((sections, height, channels, columns), bf16),
            pltpu.VMEM((channels, columns), bf16),
            pltpu.VMEM((sections, channels, columns), bf16),
            pltpu.SMEM((patches,), jnp.int32),
            pltpu.VMEM((1, channels), bf16),
            pltpu.VMEM((1, channels), bf16),
            pltpu.VMEM((sections, channels), bf16),
            pltpu.VMEM((1, 128), f32),
            pltpu.VMEM((sections, 1, 128), f32),
            pltpu.VMEM((sections, patches, 1, 128), f32),
            pltpu.VMEM((channels, 128), f32),
            pltpu.VMEM((channels, 128), f32),
            pltpu.VMEM((sections, channels, 128), f32),
            pltpu.VMEM((3 * channels, height * columns), bf16),
            pltpu.VMEM((3 * channels, height * columns), f32),
            pltpu.VMEM((channels, columns), f32),
            pltpu.VMEM((channels, columns), f32),
            dma((6,)),
            dma((4,)),
        ]
        + [dma((sections,)) for _ in range(13)],
        compiler_params=pltpu.CompilerParams(
            collective_id=0, has_side_effects=True, vmem_limit_bytes=48 * 1024 * 1024
        ),
    )(*operands)
    return jnp.transpose(out, (0, 2, 1, 3))[None]


def solution(mesh):
    placed = (
        P("section", None, "patch", None),
        P("section", None, None, None, None),
        P("section", None),
        P("section", None),
        P("section", None, None),
        P(),
    )
    return jax.shard_map(
        functools.partial(per_device, mesh.shape["section"], mesh.shape["patch"]),
        mesh=mesh,
        in_specs=placed,
        out_specs=P("section", None, None, "patch", None),
        check_vma=False,
    )
```

```python
import functools

import jax
import jax.numpy as jnp
from jax import lax
from jax.experimental import pallas as pl
from jax.experimental.pallas import tpu as pltpu
from jax.sharding import PartitionSpec as P

GROUPS = 32
EPS = 1e-05
MESH = pl.DeviceIdType.MESH
ROWS_OUT = 64
SUB = 3


def kernel(
    sections,
    patches,
    heights_in,
    latent_ref,
    weight_ref,
    gain_ref,
    shift_ref,
    bias_ref,
    out_ref,
    lat,
    weights,
    wall,
    xbuf,
    skip,
    obuf,
    edge_lat,
    edge_out,
    heights_ref,
    gain_v,
    shift_v,
    bias_v,
    stat_lat,
    stat_out,
    stat_in,
    gain_b,
    shift_b,
    bias_b,
    ybuf,
    tbuf,
    sum_b,
    sq_b,
    local_sem,
    first_sem,
    ends_rs,
    mid_rs,
    up_rs,
    low_rs,
    stat_rs,
    skip_rs,
    ends_ss,
    mid_ss,
    up_ss,
    low_ss,
    stat_ss,
    skip_ss,
    out_sem,
):
    k = lax.axis_index("section")
    p = lax.axis_index("patch")
    height, channels, columns = lat.shape
    per_group = channels // GROUPS
    is_odd = lax.rem(k, 2) == 1
    last = k == sections - 1
    has_far = jnp.logical_and(is_odd, k + 2 < sections)

    load_lat = pltpu.make_async_copy(latent_ref, lat, local_sem.at[0])
    load_w = pltpu.make_async_copy(weight_ref, weights, local_sem.at[1])
    load_h = pltpu.make_async_copy(heights_in, heights_ref, local_sem.at[2])
    load_g = pltpu.make_async_copy(gain_ref, gain_v, local_sem.at[3])
    load_s = pltpu.make_async_copy(shift_ref, shift_v, local_sem.at[4])
    load_b = pltpu.make_async_copy(bias_ref, bias_v, local_sem.at[5])
    load_h.start()
    load_lat.start()
    load_g.start()
    load_s.start()
    load_b.start()
    load_w.start()

    barrier = pltpu.get_barrier_semaphore()

    def signal(s, q):
        pl.semaphore_signal(barrier, inc=1, device_id=(s, q), device_id_type=MESH)

    @pl.when(k == 0)
    def _():
        def step(i, c):
            q = lax.rem(p + i, patches)
            for s in range(sections):
                if s == 0:
                    @pl.when(i > 0)
                    def _():
                        signal(0, q)
                else:
                    signal(s, q)
            return c

        lax.fori_loop(0, patches, step, 0)

    @pl.when(k > 0)
    def _():
        def step(i, c):
            signal(k - 1, lax.rem(p + i, patches))
            return c

        lax.fori_loop(0, patches, step, 0)

        @pl.when(p > 0)
        def _():
            signal(k, p - 1)

        @pl.when(p < patches - 1)
        def _():
            signal(k, p + 1)

    if sections > 2:
        @pl.when(k == 1)
        def _():
            for s in range(2, sections):
                signal(s, p)

        @pl.when(jnp.logical_and(is_odd, k >= 3))
        def _():
            signal(k - 2, p)

    load_h.wait()
    height_own = heights_ref[p]
    window_rows = heights_ref[0]
    for i in range(1, patches):
        window_rows = window_rows + heights_ref[i]
    inv_count = 1.0 / (
        jnp.full((1, 128), window_rows, jnp.int32).astype(jnp.float32)
        * (per_group * columns)
    )

    chan = lax.broadcasted_iota(jnp.int32, (channels, 128), 0)
    first = lax.broadcasted_iota(jnp.int32, (channels, 128), 1) * per_group
    group_mask = jnp.where(
        jnp.logical_and(chan >= first, chan < first + per_group), 1.0, 0.0
    ).astype(jnp.float32)

    def to_groups(per_chan):
        total = jnp.sum(per_chan, axis=1, keepdims=True)
        return jnp.sum(total * group_mask, axis=0, keepdims=True)

    def to_channels(per_group_row):
        return jnp.sum(per_group_row * group_mask, axis=1, keepdims=True)

    def write_stats(ref, sums, squares):
        ref[...] = to_groups(sums) + pltpu.roll(to_groups(squares), GROUPS, 1)

    load_lat.wait()
    rows = [
        jnp.where(r < height_own, lat[r].astype(jnp.float32), 0.0) for r in range(height)
    ]
    sums, squares, edge = rows[0], rows[0] * rows[0], lat[0]
    for r in range(1, height):
        sums = sums + rows[r]
        squares = squares + rows[r] * rows[r]
        edge = jnp.where(height_own == r + 1, lat[r], edge)
    edge_lat[...] = edge
    write_stats(stat_lat, sums, squares)

    sends_to = (
        patches
        - (k == 0).astype(jnp.int32)
        + jnp.where(last, 0, patches)
        + jnp.where(k > 0, (p > 0).astype(jnp.int32) + (p < patches - 1).astype(jnp.int32), 0)
        + (k >= 2).astype(jnp.int32)
        + has_far.astype(jnp.int32)
    )
    pl.semaphore_wait(barrier, sends_to)

    def remote(src, dst, ssem, rsem, s, q):
        return pltpu.make_async_remote_copy(
            src_ref=src, dst_ref=dst, send_sem=ssem, recv_sem=rsem,
            device_id=(s, q), device_id_type=MESH,
        )

    def send_stats(m, s, stat, ssem, own):
        def step(i, c):
            q = lax.rem(p + i, patches)
            remote(stat, stat_in.at[m, p], ssem, stat_rs.at[m], s, q).start()
            return c

        if own is None:
            lax.fori_loop(0, patches, step, 0)
        else:
            lax.fori_loop(1, patches, step, 0)

            @pl.when(own)
            def _():
                pltpu.make_async_copy(stat, stat_in.at[m, p], stat_rs.at[m]).start()

            @pl.when(jnp.logical_not(own))
            def _():
                step(0, 0)

    def send_rows(m, s, head, tail, mid, ssem_ends, ssem_mid):
        remote(head, xbuf.at[m, 1], ssem_ends, ends_rs.at[m], s, p).start()
        remote(tail, xbuf.at[m, 2], ssem_ends, ends_rs.at[m], s, p).start()
        remote(mid, xbuf.at[m, 3], ssem_mid, mid_rs.at[m], s, p).start()

    def pass_on(m, head, tail):
        @pl.when(p < patches - 1)
        def _():
            remote(tail, xbuf.at[m, 0], up_ss.at[m], up_rs.at[m], k, p + 1).start()

        @pl.when(p > 0)
        def _():
            remote(head, xbuf.at[m, 4], low_ss.at[m], low_rs.at[m], k, p - 1).start()

    send_stats(k, 0, stat_lat, first_sem.at[0], k == 0)

    @pl.when(k == 0)
    def _():
        pass_on(0, lat.at[0], edge_lat)
        pltpu.make_async_copy(lat.at[0], xbuf.at[0, 1], ends_rs.at[0]).start()
        pltpu.make_async_copy(edge_lat, xbuf.at[0, 2], ends_rs.at[0]).start()
        pltpu.make_async_copy(lat.at[1], xbuf.at[0, 3], mid_rs.at[0]).start()

    @pl.when(k > 0)
    def _():
        send_rows(k, 0, lat.at[0], edge_lat, lat.at[1], first_sem.at[1], first_sem.at[2])

    @pl.when(k == 1)
    def _():
        pltpu.make_async_copy(lat, skip.at[1], skip_rs.at[1]).start()

    @pl.when(k != 1)
    def _():
        remote(lat, skip.at[k], first_sem.at[3], skip_rs.at[k], 1, p).start()

    eye = jnp.where(
        lax.broadcasted_iota(jnp.int32, (channels, channels), 0)
        == lax.broadcasted_iota(jnp.int32, (channels, channels), 1),
        1.0,
        0.0,
    ).astype(jnp.bfloat16)

    def spread(row):
        wide = jnp.broadcast_to(row.astype(jnp.float32), (128, channels)).astype(jnp.bfloat16)
        return lax.dot_general(
            eye, wide, (((1,), (1,)), ((), ())), preferred_element_type=jnp.float32
        )

    load_g.wait()
    gain_b[...] = spread(gain_v[...])
    load_s.wait()
    shift_b[...] = spread(shift_v[...])
    load_b.wait()
    for m in range(sections):
        bias_b[m] = spread(bias_v[m : m + 1, :])

    load_w.wait()
    for b in range(3):
        for a in range(3):
            wall[b * channels : (b + 1) * channels, a * channels : (a + 1) * channels] = weights[b, a]

    def wait_for(ref, sem):
        pltpu.make_async_copy(ref, ref, sem).wait()

    lane = lax.broadcasted_iota(jnp.int32, (ROWS_OUT, columns), 1)

    def sample(m, carry):
        wait_for(xbuf.at[m, pl.ds(1, 2)], ends_rs.at[m])

        @pl.when(jnp.logical_or(k > 0, m > 0))
        def _():
            pass_on(m, xbuf.at[m, 1], xbuf.at[m, 2])

        wait_for(stat_in.at[m], stat_rs.at[m])
        total = jnp.sum(stat_in[m], axis=0)
        mean = total * inv_count
        var = pltpu.roll(mean, 128 - GROUPS, 1) - mean * mean
        inv = lax.rsqrt(jnp.maximum(var, 0.0) + EPS)
        scale = to_channels(inv) * gain_b[...]
        offset = shift_b[...] - to_channels(mean) * scale

        def activate(values):
            v = values.astype(jnp.float32) * scale + offset
            half = 0.5 * v
            return half + half * jnp.tanh(half)

        def put(j, value):
            value = value.astype(jnp.bfloat16)
            for a in range(3):
                r = j - a
                if 0 <= r < height:
                    ybuf[a * channels : (a + 1) * channels, r * columns : (r + 1) * columns] = value

        put(1, activate(xbuf[m, 1]))
        tail = activate(xbuf[m, 2])
        wait_for(xbuf.at[m, 3], mid_rs.at[m])
        mid = activate(xbuf[m, 3])

        @pl.when(p > 0)
        def _():
            wait_for(xbuf.at[m, 0], up_rs.at[m])

        @pl.when(p < patches - 1)
        def _():
            wait_for(xbuf.at[m, 4], low_rs.at[m])

        put(0, jnp.where(p > 0, activate(xbuf[m, 0]), 0.0))
        below = jnp.where(p < patches - 1, activate(xbuf[m, 4]), 0.0)
        one, two = height_own == 1, height_own == 2
        put(2, jnp.where(one, below, jnp.where(two, tail, mid)))
        put(3, jnp.where(one, 0.0, jnp.where(two, below, tail)))
        put(4, jnp.where(height_own == 3, below, 0.0))

        tbuf[...] = jnp.dot(wall[...], ybuf[...], preferred_element_type=jnp.float32)

        @pl.when(is_odd)
        def _():
            wait_for(skip.at[m], skip_rs.at[m])

        for c0 in range(0, channels, ROWS_OUT):
            cs = slice(c0, c0 + ROWS_OUT)
            sums = jnp.zeros((ROWS_OUT, columns), jnp.float32)
            squares = sums
            edge = None
            for r in range(height):
                ls = slice(r * columns, (r + 1) * columns)
                left = pltpu.roll(tbuf[c0 : c0 + ROWS_OUT, ls], 1, 1)
                mid = tbuf[channels + c0 : channels + c0 + ROWS_OUT, ls]
                right = pltpu.roll(
                    tbuf[2 * channels + c0 : 2 * channels + c0 + ROWS_OUT, ls], columns - 1, 1
                )
                z = (
                    jnp.where(lane > 0, left, 0.0)
                    + mid
                    + jnp.where(lane < columns - 1, right, 0.0)
                    + bias_b[m, cs]
                )
                z = jnp.where(is_odd, skip[m, r, cs].astype(jnp.float32) + z, z)
                value = jnp.where(r < height_own, z, 0.0).astype(jnp.bfloat16)
                obuf[m, r, cs] = value
                wide = value.astype(jnp.float32)
                sums = sums + wide
                squares = squares + wide * wide
                edge = value if r == 0 else jnp.where(height_own == r + 1, value, edge)
            edge_out[m, cs] = edge
            sum_b[cs] = sums
            sq_b[cs] = squares

        @pl.when(jnp.logical_not(last))
        def _():
            send_rows(
                m, k + 1, obuf.at[m, 0], edge_out.at[m], obuf.at[m, 1], ends_ss.at[m], mid_ss.at[m]
            )
            write_stats(stat_out.at[m], sum_b[...], sq_b[...])
            send_stats(m, k + 1, stat_out.at[m], stat_ss.at[m], None)

        if sections > 2:
            @pl.when(has_far)
            def _():
                remote(obuf.at[m], skip.at[m], skip_ss.at[m], skip_rs.at[m], k + 2, p).start()

        pltpu.make_async_copy(obuf.at[m], out_ref.at[m], out_sem.at[m]).start()
        return carry

    lax.fori_loop(0, sections, sample, 0)

    wait_for(stat_in.at[0, pl.ds(1, patches - 1)], first_sem.at[0])

    @pl.when(k > 0)
    def _():
        wait_for(stat_lat, first_sem.at[0])
        wait_for(xbuf.at[0, pl.ds(0, 2)], first_sem.at[1])
        wait_for(edge_lat, first_sem.at[2])

    @pl.when(k != 1)
    def _():
        wait_for(lat, first_sem.at[3])

    def drain(m, carry):
        @pl.when(p < patches - 1)
        def _():
            wait_for(edge_lat, up_ss.at[m])

        @pl.when(p > 0)
        def _():
            wait_for(edge_lat, low_ss.at[m])

        @pl.when(jnp.logical_not(last))
        def _():
            wait_for(xbuf.at[m, pl.ds(0, 2)], ends_ss.at[m])
            wait_for(edge_lat, mid_ss.at[m])
            wait_for(stat_in.at[m], stat_ss.at[m])

        if sections > 2:
            @pl.when(has_far)
            def _():
                wait_for(obuf.at[m], skip_ss.at[m])

        wait_for(obuf.at[m], out_sem.at[m])
        return carry

    lax.fori_loop(0, sections, drain, 0)


def paired_kernel(
    patches,
    local,
    heights_in,
    latent_ref,
    weight_ref,
    gain_ref,
    shift_ref,
    bias_ref,
    out_ref,
    lat,
    weights,
    wall,
    part,
    xin,
    xmid,
    obuf,
    ends,
    heights_ref,
    gain_v,
    shift_v,
    bias_v,
    params,
    params_in,
    stat_lat,
    stat_mate,
    stat_all,
    total_out,
    total_in,
    stat_mid,
    stat_mid_all,
    gain_b,
    shift_b,
    bias_b,
    ybuf,
    tbuf,
    sum_b,
    sq_b,
    load_sem,
    ready,
    small_rs,
    small_ss,
    row_rs,
    row_ss,
    edge_rs,
    edge_ss,
    seed_rs,
    seed_ss,
    share_rs,
    share_ss,
    core_rs,
    core_ss,
    mid_rs,
    mid_ss,
    own_edge_rs,
    own_edge_ss,
    far_edge_rs,
    far_edge_ss,
    stat_rs,
    stat_ss,
    out_sem,
):
    k = lax.axis_index("section")
    p = lax.axis_index("patch")
    height, channels, columns = lat.shape
    per_group = channels // GROUPS
    rest = channels - local
    piece = part.shape[0] // (8 * SUB)

    core = lax.rem(p, 2)
    mate = p + 1 - 2 * core
    across = p - 1 + 2 * core
    has_across = jnp.logical_and(across >= 0, across < patches)
    member = lax.rem(p, 8)
    turn_y = 2 - 4 * lax.rem(member // 2, 2)
    turn_z = 4 - 8 * (member // 4)
    friends = (p + turn_y, p + turn_z, p + turn_y + turn_z)

    load_h = pltpu.make_async_copy(heights_in, heights_ref, load_sem.at[0])
    load_lat = pltpu.make_async_copy(latent_ref, lat, load_sem.at[1])
    load_g = pltpu.make_async_copy(gain_ref, gain_v, load_sem.at[2])
    load_s = pltpu.make_async_copy(shift_ref, shift_v, load_sem.at[3])
    load_b = pltpu.make_async_copy(bias_ref, bias_v, load_sem.at[4])
    load_w = pltpu.make_async_copy(weight_ref, weights, load_sem.at[5])
    for load in (load_h, load_lat, load_g, load_s, load_b, load_w):
        load.start()

    barrier = pltpu.get_barrier_semaphore()

    def signal(s, q):
        pl.semaphore_signal(barrier, inc=1, device_id=(s, q), device_id_type=MESH)

    @pl.when(k == 0)
    def _():
        signal(1, p)

        def step(i, carry):
            signal(0, lax.rem(p + i, patches))
            return carry

        lax.fori_loop(1, patches, step, 0)

    @pl.when(k == 1)
    def _():
        for q in (mate, *friends):
            signal(1, q)

        @pl.when(has_across)
        def _():
            signal(1, across)

    def remote(src, dst, ssem, rsem, s, q):
        return pltpu.make_async_remote_copy(
            src_ref=src, dst_ref=dst, send_sem=ssem, recv_sem=rsem,
            device_id=(s, q), device_id_type=MESH,
        )

    def wait_for(ref, sem):
        pltpu.make_async_copy(ref, ref, sem).wait()

    load_h.wait()
    height_own = heights_ref[p]
    window_rows = heights_ref[0]
    for i in range(1, patches):
        window_rows = window_rows + heights_ref[i]
    inv_count = 1.0 / (
        jnp.full((1, 128), window_rows, jnp.int32).astype(jnp.float32)
        * (per_group * columns)
    )

    chan = lax.broadcasted_iota(jnp.int32, (channels, 128), 0)
    first = lax.broadcasted_iota(jnp.int32, (channels, 128), 1) * per_group
    group_mask = jnp.where(
        jnp.logical_and(chan >= first, chan < first + per_group), 1.0, 0.0
    ).astype(jnp.float32)

    def to_groups(per_chan):
        total = jnp.sum(per_chan, axis=1, keepdims=True)
        return jnp.sum(total * group_mask, axis=0, keepdims=True)

    def to_channels(per_group_row):
        return jnp.sum(per_group_row * group_mask, axis=1, keepdims=True)

    def both(sums, squares):
        return to_groups(sums) + pltpu.roll(to_groups(squares), GROUPS, 1)

    load_lat.wait()
    rows = [
        jnp.where(r < height_own, lat[r].astype(jnp.float32), 0.0) for r in range(height)
    ]
    sums, squares, edge = rows[0], rows[0] * rows[0], lat[0]
    for r in range(1, height):
        sums = sums + rows[r]
        squares = squares + rows[r] * rows[r]
        edge = jnp.where(height_own == r + 1, lat[r], edge)
    xin[k, 1] = lat[0]
    xin[k, 2] = edge
    xin[k, 3] = lat[1]
    stat_lat[...] = both(sums, squares)

    def take_params():
        load_g.wait()
        load_s.wait()
        load_b.wait()
        params[0:1] = gain_v[...].astype(jnp.float32)
        params[1:2] = shift_v[...].astype(jnp.float32)
        params[2:4] = bias_v[...].astype(jnp.float32)

    eye = jnp.where(
        lax.broadcasted_iota(jnp.int32, (channels, channels), 0)
        == lax.broadcasted_iota(jnp.int32, (channels, channels), 1),
        1.0,
        0.0,
    ).astype(jnp.bfloat16)

    def spread(row):
        wide = jnp.broadcast_to(row, (128, channels)).astype(jnp.bfloat16)
        return lax.dot_general(
            eye, wide, (((1,), (1,)), ((), ())), preferred_element_type=jnp.float32
        )

    def spread_params(at, source):
        gain_b[at] = spread(source[0:1])
        shift_b[at] = spread(source[1:2])
        for m in range(2):
            bias_b[at, m] = spread(source[2 + m : 3 + m])

    def build(is_rest):
        for b in range(3):
            for a in range(3):
                cols = slice(a * channels, (a + 1) * channels)
                if is_rest:
                    start = 3 * local + b * rest
                    wall[start : start + rest, cols] = weights[b, a, local:]
                else:
                    wall[b * local : (b + 1) * local, cols] = weights[b, a, :local]

    cross_slot, other_slot = 1 + core, 2 - core

    def send_rows():
        for i, slot in enumerate((cross_slot, other_slot, 3)):
            remote(xin.at[k, slot], xin.at[k, slot], row_ss.at[i], row_rs.at[i], 1 - k, p).start()

    def wait_row(i):
        wait_for(lat.at[0], row_rs.at[i])

    def send_edge(kind, ref, m, span, ssem, rsem):
        src_slot = cross_slot if kind == 0 else other_slot
        dst_slot = 4 - 4 * core if kind == 0 else 4 * core
        q = across if kind == 0 else mate

        def go():
            remote(
                ref.at[m, src_slot, span], ref.at[m, dst_slot, span],
                ssem.at[m, kind], rsem.at[m, kind], k, q,
            ).start()

        if kind == 0:
            pl.when(has_across)(go)
        else:
            go()

    def wait_edge(kind, ref, sem, m):
        if kind == 0:
            @pl.when(has_across)
            def _():
                wait_for(ref, sem.at[m, kind])
        else:
            wait_for(ref, sem.at[m, kind])

    whole = pl.ds(0, channels)
    head_part = pl.ds(0, local)
    tail_part = pl.ds(local, rest)

    def pass_in(kind, m):
        send_edge(kind, xin, m, whole, edge_ss, edge_rs)

    def coefficients(total, at):
        mean = total * inv_count
        var = pltpu.roll(mean, 128 - GROUPS, 1) - mean * mean
        inv = lax.rsqrt(jnp.maximum(var, 0.0) + EPS)
        scale = to_channels(inv) * gain_b[at]
        return scale, shift_b[at] - to_channels(mean) * scale

    def fill(rows_of, m, scale, offset, before_edges):
        def activate(values):
            v = values.astype(jnp.float32) * scale + offset
            half = 0.5 * v
            return half + half * jnp.tanh(half)

        def put(j, value):
            value = value.astype(jnp.bfloat16)
            for a in range(3):
                r = j - a
                if 0 <= r < height:
                    at = (m * height + r) * columns
                    ybuf[a * channels : (a + 1) * channels, at : at + columns] = value

        put(1, activate(rows_of[m, 1]))
        tail = activate(rows_of[m, 2])
        mid = activate(rows_of[m, 3])
        before_edges()
        put(0, jnp.where(p > 0, activate(rows_of[m, 0]), 0.0))
        below = jnp.where(p < patches - 1, activate(rows_of[m, 4]), 0.0)
        one, two = height_own == 1, height_own == 2
        put(2, jnp.where(one, below, jnp.where(two, tail, mid)))
        put(3, jnp.where(one, 0.0, jnp.where(two, below, tail)))
        put(4, jnp.where(height_own == 3, below, 0.0))

    lane = lax.broadcasted_iota(jnp.int32, (ROWS_OUT, columns), 1)

    def conv_row(m, r, c0, count, bias):
        at = (m * height + r) * columns
        ls = slice(at, at + columns)

        def block(b):
            start = b * local + c0 if c0 < local else 3 * local + b * rest + c0 - local
            return tbuf[start : start + count, ls]

        return (
            jnp.where(lane > 0, pltpu.roll(block(0), 1, 1), 0.0)
            + block(1)
            + jnp.where(lane < columns - 1, pltpu.roll(block(2), columns - 1, 1), 0.0)
            + bias
        )

    def send_mid(i, m):
        src = (ends.at[m, core], ends.at[m, 1 - core], obuf.at[m, 1])[i]
        slot = (cross_slot, other_slot, 3)[i]
        remote(
            src.at[tail_part], xmid.at[m, slot, tail_part], mid_ss.at[m, i], mid_rs.at[m, i], 1, p
        ).start()

    def multiply(count, m0, samples):
        cols = slice(m0 * height * columns, (m0 + samples) * height * columns)
        tbuf[:count, cols] = jnp.dot(
            wall[...] if count > 3 * local else part[...],
            ybuf[:, cols],
            preferred_element_type=jnp.float32,
        )

    @pl.when(k == 1)
    def _():
        pl.semaphore_wait(barrier, 5 + has_across.astype(jnp.int32))
        pl.semaphore_signal(ready, inc=1, device_id=(0, p), device_id_type=MESH)
        remote(stat_lat, stat_mate, small_ss.at[1], small_rs.at[1], 0, p).start()
        send_rows()
        pass_in(0, 1)
        pass_in(1, 1)
        take_params()
        spread_params(0, params)
        load_w.wait()
        build(False)
        build(True)

    @pl.when(k == 0)
    def _():
        take_params()
        load_w.wait()
        build(False)
        pl.semaphore_wait(ready, 1)
        remote(params, params_in, small_ss.at[0], small_rs.at[0], 1, p).start()
        for i in range(SUB):
            at = pl.ds((member * SUB + i) * piece, piece)
            remote(wall.at[at], part.at[at], seed_ss.at[i], seed_rs.at[i], 1, p).start()
        send_rows()
        pl.semaphore_wait(barrier, patches - 1)

        def share_stats(m, source):
            def step(i, carry):
                q = lax.rem(p + i, patches)
                remote(
                    source, stat_all.at[m, p], small_ss.at[2 + m], small_rs.at[2 + m], 0, q
                ).start()
                return carry

            lax.fori_loop(1, patches, step, 0)
            stat_all[m, p] = source[...]

        def total_of(m):
            wait_for(stat_all.at[m, pl.ds(0, patches - 1)], small_rs.at[2 + m])
            total = jnp.sum(stat_all[m], axis=0)
            total_out[m] = total
            remote(
                total_out.at[m], total_in.at[m], small_ss.at[4 + m], small_rs.at[4 + m], 1, p
            ).start()
            return total

        share_stats(0, stat_lat)
        pass_in(0, 0)
        pass_in(1, 0)
        spread_params(0, params)
        build(True)
        wait_for(stat_lat, small_rs.at[1])
        share_stats(1, stat_mate)
        wait_row(0)
        pass_in(0, 1)

        for m in range(2):
            scale, offset = coefficients(total_of(m), 0)

            def before_edges():
                if m == 0:
                    wait_row(1)
                    pass_in(1, 1)
                for kind in range(2):
                    wait_edge(kind, lat.at[0], edge_rs, m)

            if m == 1:
                wait_row(2)
            fill(xin, m, scale, offset, before_edges)
            multiply(3 * channels, m, 1)
            for c0 in range(0, channels, ROWS_OUT):
                cs = slice(c0, c0 + ROWS_OUT)
                sums = jnp.zeros((ROWS_OUT, columns), jnp.float32)
                squares = sums
                edge = None
                for r in range(height):
                    z = conv_row(m, r, c0, ROWS_OUT, bias_b[0, m, cs])
                    value = jnp.where(r < height_own, z, 0.0).astype(jnp.bfloat16)
                    obuf[m, r, cs] = value
                    wide = value.astype(jnp.float32)
                    sums = sums + wide
                    squares = squares + wide * wide
                    edge = value if r == 0 else jnp.where(height_own == r + 1, value, edge)
                    if r == 0:
                        ends[m, 0, cs] = value
                ends[m, 1, cs] = edge
                sum_b[cs] = sums
                sq_b[cs] = squares
            stat_mid[m] = both(sum_b[...], sq_b[...])

            def step(i, carry):
                q = lax.rem(p + i, patches)
                remote(stat_mid.at[m], stat_mid_all.at[m, p], stat_ss.at[m], stat_rs.at[m], 1, q).start()
                return carry

            send_mid(0, m)
            if m == 0:
                send_mid(1, 0)
            lax.fori_loop(0, patches, step, 0)
            pltpu.make_async_copy(obuf.at[m], out_ref.at[m], out_sem.at[m]).start()
        send_mid(2, 0)
        send_mid(1, 1)
        send_mid(2, 1)

        wait_for(params, small_ss.at[0])
        for m in range(2):
            wait_for(stat_all.at[m, pl.ds(0, patches - 1)], small_ss.at[2 + m])
            wait_for(total_out.at[m], small_ss.at[4 + m])
        for i in range(SUB):
            wait_for(part.at[pl.ds(0, piece)], seed_ss.at[i])
        for m in range(2):
            wait_for(stat_mid_all.at[m], stat_ss.at[m])
            for i in range(3):
                wait_for(obuf.at[m, 1, tail_part], mid_ss.at[m, i])

    @pl.when(k == 1)
    def _():
        def to_mate(index, sem):
            at = pl.ds(index * piece, piece)
            remote(part.at[at], part.at[at], core_ss.at[sem], core_rs.at[0], 1, mate).start()

        def seed(i, carry):
            index = member * SUB + i
            at = pl.ds(index * piece, piece)
            wait_for(part.at[pl.ds(0, piece)], seed_rs.at[i])
            for j in range(3):
                remote(
                    part.at[at], part.at[at], share_ss.at[j, i], share_rs.at[j, i], 1, friends[j]
                ).start()
            to_mate(index, i)
            return carry

        lax.fori_loop(0, SUB, seed, 0)
        wait_for(params, small_rs.at[0])
        spread_params(1, params_in)
        wait_row(0)
        pass_in(0, 0)

        def shared(i, carry):
            for j in range(3):
                wait_for(part.at[pl.ds(0, piece)], share_rs.at[j, i])
                to_mate(lax.rem(friends[j], 8) * SUB + i, (1 + j) * SUB + i)
            return carry

        lax.fori_loop(0, SUB, shared, 0)
        wait_row(1)
        pass_in(1, 0)
        wait_row(2)

        def pass_far(kind, m):
            wait_for(obuf.at[m, 1, tail_part], mid_rs.at[m, kind])
            send_edge(kind, xmid, m, tail_part, far_edge_ss, far_edge_rs)

        for m in range(2):
            wait_for(total_out.at[m], small_rs.at[4 + m])
            scale, offset = coefficients(total_in[m], 1)

            def before_edges():
                for kind in range(2):
                    wait_edge(kind, lat.at[0], edge_rs, m)

            fill(xin, m, scale, offset, before_edges)
            if m == 0:
                wait_for(part.at[pl.ds(0, 4 * SUB * piece)], core_rs.at[0])
            multiply(3 * local, m, 1)
            for c0 in range(0, local, ROWS_OUT):
                cs = slice(c0, c0 + ROWS_OUT)
                edge = None
                for r in range(height):
                    value = conv_row(m, r, c0, ROWS_OUT, bias_b[1, m, cs]).astype(jnp.bfloat16)
                    edge = value if r == 0 else jnp.where(height_own == r + 1, value, edge)
                    if r == 0:
                        xmid[m, 1, cs] = value
                    if r == 1:
                        xmid[m, 3, cs] = value
                xmid[m, 2, cs] = edge
            for kind in range(2):
                send_edge(kind, xmid, m, head_part, own_edge_ss, own_edge_rs)
            pass_far(0, m)
            if m == 0:
                pass_far(1, 0)

        for m in range(2):
            wait_for(stat_mid_all.at[m], stat_rs.at[m])
            scale, offset = coefficients(jnp.sum(stat_mid_all[m], axis=0), 0)
            wait_for(obuf.at[m, 1, tail_part], mid_rs.at[m, 2])

            def before_edges():
                for kind in range(2):
                    wait_edge(kind, lat.at[0, head_part], own_edge_rs, m)
                    wait_edge(kind, lat.at[0, tail_part], far_edge_rs, m)

            fill(xmid, m, scale, offset, before_edges)
            multiply(3 * channels, m, 1)
            if m == 0:
                pass_far(1, 1)
            for c0 in range(0, channels, ROWS_OUT):
                cs = slice(c0, c0 + ROWS_OUT)
                for r in range(height):
                    z = conv_row(m, r, c0, ROWS_OUT, bias_b[0, m, cs])
                    z = xin[m, (1, 3, 2)[r], cs].astype(jnp.float32) + z
                    obuf[m, r, cs] = jnp.where(r < height_own, z, 0.0).astype(jnp.bfloat16)
            pltpu.make_async_copy(obuf.at[m], out_ref.at[m], out_sem.at[m]).start()

        wait_for(stat_lat, small_ss.at[1])
        for i in range(SUB):
            for j in range(3):
                wait_for(part.at[pl.ds(0, piece)], share_ss.at[j, i])
        for i in range(4 * SUB):
            wait_for(part.at[pl.ds(0, piece)], core_ss.at[i])
        for m in range(2):
            for kind in range(2):
                wait_edge(kind, lat.at[0, head_part], own_edge_ss, m)
                wait_edge(kind, lat.at[0, tail_part], far_edge_ss, m)

    for i in range(3):
        wait_for(lat.at[0], row_ss.at[i])
    for m in range(2):
        for kind in range(2):
            wait_edge(kind, lat.at[0], edge_ss, m)
        wait_for(obuf.at[m], out_sem.at[m])


def paired_call(patches, operands, height, channels, columns):
    bf16, f32 = jnp.bfloat16, jnp.float32
    local = channels * 2 // 5
    hbm = pl.BlockSpec(memory_space=pltpu.HBM)
    dma = pltpu.SemaphoreType.DMA
    return pl.pallas_call(
        functools.partial(paired_kernel, patches, local),
        out_shape=jax.ShapeDtypeStruct((2, height, channels, columns), bf16),
        in_specs=[hbm] * 6,
        out_specs=pl.BlockSpec(memory_space=pl.ANY),
        scratch_shapes=[
            pltpu.VMEM((height, channels, columns), bf16),
            pltpu.VMEM((3, 3, channels, channels), bf16),
            pltpu.VMEM((3 * channels, 3 * channels), bf16),
            pltpu.VMEM((3 * local, 3 * channels), bf16),
            pltpu.VMEM((2, height + 2, channels, columns), bf16),
            pltpu.VMEM((2, height + 2, channels, columns), bf16),
            pltpu.VMEM((2, height, channels, columns), bf16),
            pltpu.VMEM((2, 2, channels, columns), bf16),
            pltpu.SMEM((patches,), jnp.int32),
            pltpu.VMEM((1, channels), bf16),
            pltpu.VMEM((1, channels), bf16),
            pltpu.VMEM((2, channels), bf16),
            pltpu.VMEM((8, channels), f32),
            pltpu.VMEM((8, channels), f32),
            pltpu.VMEM((1, 128), f32),
            pltpu.VMEM((1, 128), f32),
            pltpu.VMEM((2, patches, 1, 128), f32),
            pltpu.VMEM((2, 1, 128), f32),
            pltpu.VMEM((2, 1, 128), f32),
            pltpu.VMEM((2, 1, 128), f32),
            pltpu.VMEM((2, patches, 1, 128), f32),
            pltpu.VMEM((2, channels, 128), f32),
            pltpu.VMEM((2, channels, 128), f32),
            pltpu.VMEM((2, 2, channels, 128), f32),
            pltpu.VMEM((3 * channels, 2 * height * columns), bf16),
            pltpu.VMEM((3 * channels, 2 * height * columns), f32),
            pltpu.VMEM((channels, columns), f32),
            pltpu.VMEM((channels, columns), f32),
            dma((6,)),
            pltpu.SemaphoreType.REGULAR,
            dma((6,)),
            dma((6,)),
            dma((3,)),
            dma((3,)),
            dma((2, 2)),
            dma((2, 2)),
            dma((SUB,)),
            dma((SUB,)),
            dma((3, SUB)),
            dma((3, SUB)),
            dma((1,)),
            dma((4 * SUB,)),
            dma((2, 3)),
            dma((2, 3)),
            dma((2, 2)),
            dma((2, 2)),
            dma((2, 2)),
            dma((2, 2)),
            dma((2,)),
            dma((2,)),
            dma((2,)),
        ],
        compiler_params=pltpu.CompilerParams(
            collective_id=0, has_side_effects=True, vmem_limit_bytes=48 * 1024 * 1024
        ),
    )(*operands)


def per_device(sections, patches, latent, conv_weight, norm_gain, norm_shift, step_bias, patch_rows):
    latent = jnp.transpose(latent[0], (1, 0, 2))
    weight = jnp.transpose(conv_weight[0], (0, 2, 1, 3))
    height, channels, columns = latent.shape
    bf16, f32 = jnp.bfloat16, jnp.float32
    hbm = pl.BlockSpec(memory_space=pltpu.HBM)
    dma = pltpu.SemaphoreType.DMA
    operands = [
        pltpu.with_memory_space_constraint(array, pltpu.HBM)
        for array in (patch_rows, latent, weight, norm_gain, norm_shift, step_bias[0])
    ]
    if sections == 2 and patches % 8 == 0:
        out = paired_call(patches, operands, height, channels, columns)
        return jnp.transpose(out, (0, 2, 1, 3))[None]
    out = pl.pallas_call(
        functools.partial(kernel, sections, patches),
        out_shape=jax.ShapeDtypeStruct((sections, height, channels, columns), bf16),
        in_specs=[hbm] * 6,
        out_specs=pl.BlockSpec(memory_space=pl.ANY),
        scratch_shapes=[
            pltpu.VMEM((height, channels, columns), bf16),
            pltpu.VMEM((3, 3, channels, channels), bf16),
            pltpu.VMEM((3 * channels, 3 * channels), bf16),
            pltpu.VMEM((sections, height + 2, channels, columns), bf16),
            pltpu.VMEM((sections, height, channels, columns), bf16),
            pltpu.VMEM((sections, height, channels, columns), bf16),
            pltpu.VMEM((channels, columns), bf16),
            pltpu.VMEM((sections, channels, columns), bf16),
            pltpu.SMEM((patches,), jnp.int32),
            pltpu.VMEM((1, channels), bf16),
            pltpu.VMEM((1, channels), bf16),
            pltpu.VMEM((sections, channels), bf16),
            pltpu.VMEM((1, 128), f32),
            pltpu.VMEM((sections, 1, 128), f32),
            pltpu.VMEM((sections, patches, 1, 128), f32),
            pltpu.VMEM((channels, 128), f32),
            pltpu.VMEM((channels, 128), f32),
            pltpu.VMEM((sections, channels, 128), f32),
            pltpu.VMEM((3 * channels, height * columns), bf16),
            pltpu.VMEM((3 * channels, height * columns), f32),
            pltpu.VMEM((channels, columns), f32),
            pltpu.VMEM((channels, columns), f32),
            dma((6,)),
            dma((4,)),
        ]
        + [dma((sections,)) for _ in range(13)],
        compiler_params=pltpu.CompilerParams(
            collective_id=0, has_side_effects=True, vmem_limit_bytes=48 * 1024 * 1024
        ),
    )(*operands)
    return jnp.transpose(out, (0, 2, 1, 3))[None]


def solution(mesh):
    placed = (
        P("section", None, "patch", None),
        P("section", None, None, None, None),
        P("section", None),
        P("section", None),
        P("section", None, None),
        P(),
    )
    return jax.shard_map(
        functools.partial(per_device, mesh.shape["section"], mesh.shape["patch"]),
        mesh=mesh,
        in_specs=placed,
        out_specs=P("section", None, None, "patch", None),
        check_vma=False,
    )
```

```python
import functools

import jax
import jax.numpy as jnp
from jax import lax
from jax.experimental import pallas as pl
from jax.experimental.pallas import tpu as pltpu
from jax.sharding import PartitionSpec as P

GROUPS = 32
EPS = 1e-05
MESH = pl.DeviceIdType.MESH
ROWS_OUT = 64
SUB = 3


def kernel(
    sections,
    patches,
    heights_in,
    latent_ref,
    weight_ref,
    gain_ref,
    shift_ref,
    bias_ref,
    out_ref,
    lat,
    weights,
    wall,
    xbuf,
    skip,
    obuf,
    edge_lat,
    edge_out,
    heights_ref,
    gain_v,
    shift_v,
    bias_v,
    stat_lat,
    stat_out,
    stat_in,
    gain_b,
    shift_b,
    bias_b,
    ybuf,
    tbuf,
    sum_b,
    sq_b,
    local_sem,
    first_sem,
    ends_rs,
    mid_rs,
    up_rs,
    low_rs,
    stat_rs,
    skip_rs,
    ends_ss,
    mid_ss,
    up_ss,
    low_ss,
    stat_ss,
    skip_ss,
    out_sem,
):
    k = lax.axis_index("section")
    p = lax.axis_index("patch")
    height, channels, columns = lat.shape
    per_group = channels // GROUPS
    is_odd = lax.rem(k, 2) == 1
    last = k == sections - 1
    has_far = jnp.logical_and(is_odd, k + 2 < sections)

    load_lat = pltpu.make_async_copy(latent_ref, lat, local_sem.at[0])
    load_w = pltpu.make_async_copy(weight_ref, weights, local_sem.at[1])
    load_h = pltpu.make_async_copy(heights_in, heights_ref, local_sem.at[2])
    load_g = pltpu.make_async_copy(gain_ref, gain_v, local_sem.at[3])
    load_s = pltpu.make_async_copy(shift_ref, shift_v, local_sem.at[4])
    load_b = pltpu.make_async_copy(bias_ref, bias_v, local_sem.at[5])
    load_h.start()
    load_lat.start()
    load_g.start()
    load_s.start()
    load_b.start()
    load_w.start()

    barrier = pltpu.get_barrier_semaphore()

    def signal(s, q):
        pl.semaphore_signal(barrier, inc=1, device_id=(s, q), device_id_type=MESH)

    @pl.when(k == 0)
    def _():
        def step(i, c):
            q = lax.rem(p + i, patches)
            for s in range(sections):
                if s == 0:
                    @pl.when(i > 0)
                    def _():
                        signal(0, q)
                else:
                    signal(s, q)
            return c

        lax.fori_loop(0, patches, step, 0)

    @pl.when(k > 0)
    def _():
        def step(i, c):
            signal(k - 1, lax.rem(p + i, patches))
            return c

        lax.fori_loop(0, patches, step, 0)

        @pl.when(p > 0)
        def _():
            signal(k, p - 1)

        @pl.when(p < patches - 1)
        def _():
            signal(k, p + 1)

    if sections > 2:
        @pl.when(k == 1)
        def _():
            for s in range(2, sections):
                signal(s, p)

        @pl.when(jnp.logical_and(is_odd, k >= 3))
        def _():
            signal(k - 2, p)

    load_h.wait()
    height_own = heights_ref[p]
    window_rows = heights_ref[0]
    for i in range(1, patches):
        window_rows = window_rows + heights_ref[i]
    inv_count = 1.0 / (
        jnp.full((1, 128), window_rows, jnp.int32).astype(jnp.float32)
        * (per_group * columns)
    )

    chan = lax.broadcasted_iota(jnp.int32, (channels, 128), 0)
    first = lax.broadcasted_iota(jnp.int32, (channels, 128), 1) * per_group
    group_mask = jnp.where(
        jnp.logical_and(chan >= first, chan < first + per_group), 1.0, 0.0
    ).astype(jnp.float32)

    def to_groups(per_chan):
        total = jnp.sum(per_chan, axis=1, keepdims=True)
        return jnp.sum(total * group_mask, axis=0, keepdims=True)

    def to_channels(per_group_row):
        return jnp.sum(per_group_row * group_mask, axis=1, keepdims=True)

    def write_stats(ref, sums, squares):
        ref[...] = to_groups(sums) + pltpu.roll(to_groups(squares), GROUPS, 1)

    load_lat.wait()
    rows = [
        jnp.where(r < height_own, lat[r].astype(jnp.float32), 0.0) for r in range(height)
    ]
    sums, squares, edge = rows[0], rows[0] * rows[0], lat[0]
    for r in range(1, height):
        sums = sums + rows[r]
        squares = squares + rows[r] * rows[r]
        edge = jnp.where(height_own == r + 1, lat[r], edge)
    edge_lat[...] = edge
    write_stats(stat_lat, sums, squares)

    sends_to = (
        patches
        - (k == 0).astype(jnp.int32)
        + jnp.where(last, 0, patches)
        + jnp.where(k > 0, (p > 0).astype(jnp.int32) + (p < patches - 1).astype(jnp.int32), 0)
        + (k >= 2).astype(jnp.int32)
        + has_far.astype(jnp.int32)
    )
    pl.semaphore_wait(barrier, sends_to)

    def remote(src, dst, ssem, rsem, s, q):
        return pltpu.make_async_remote_copy(
            src_ref=src, dst_ref=dst, send_sem=ssem, recv_sem=rsem,
            device_id=(s, q), device_id_type=MESH,
        )

    def send_stats(m, s, stat, ssem, own):
        def step(i, c):
            q = lax.rem(p + i, patches)
            remote(stat, stat_in.at[m, p], ssem, stat_rs.at[m], s, q).start()
            return c

        if own is None:
            lax.fori_loop(0, patches, step, 0)
        else:
            lax.fori_loop(1, patches, step, 0)

            @pl.when(own)
            def _():
                pltpu.make_async_copy(stat, stat_in.at[m, p], stat_rs.at[m]).start()

            @pl.when(jnp.logical_not(own))
            def _():
                step(0, 0)

    def send_rows(m, s, head, tail, mid, ssem_ends, ssem_mid):
        remote(head, xbuf.at[m, 1], ssem_ends, ends_rs.at[m], s, p).start()
        remote(tail, xbuf.at[m, 2], ssem_ends, ends_rs.at[m], s, p).start()
        remote(mid, xbuf.at[m, 3], ssem_mid, mid_rs.at[m], s, p).start()

    def pass_on(m, head, tail):
        @pl.when(p < patches - 1)
        def _():
            remote(tail, xbuf.at[m, 0], up_ss.at[m], up_rs.at[m], k, p + 1).start()

        @pl.when(p > 0)
        def _():
            remote(head, xbuf.at[m, 4], low_ss.at[m], low_rs.at[m], k, p - 1).start()

    send_stats(k, 0, stat_lat, first_sem.at[0], k == 0)

    @pl.when(k == 0)
    def _():
        pass_on(0, lat.at[0], edge_lat)
        pltpu.make_async_copy(lat.at[0], xbuf.at[0, 1], ends_rs.at[0]).start()
        pltpu.make_async_copy(edge_lat, xbuf.at[0, 2], ends_rs.at[0]).start()
        pltpu.make_async_copy(lat.at[1], xbuf.at[0, 3], mid_rs.at[0]).start()

    @pl.when(k > 0)
    def _():
        send_rows(k, 0, lat.at[0], edge_lat, lat.at[1], first_sem.at[1], first_sem.at[2])

    @pl.when(k == 1)
    def _():
        pltpu.make_async_copy(lat, skip.at[1], skip_rs.at[1]).start()

    @pl.when(k != 1)
    def _():
        remote(lat, skip.at[k], first_sem.at[3], skip_rs.at[k], 1, p).start()

    eye = jnp.where(
        lax.broadcasted_iota(jnp.int32, (channels, channels), 0)
        == lax.broadcasted_iota(jnp.int32, (channels, channels), 1),
        1.0,
        0.0,
    ).astype(jnp.bfloat16)

    def spread(row):
        wide = jnp.broadcast_to(row.astype(jnp.float32), (128, channels)).astype(jnp.bfloat16)
        return lax.dot_general(
            eye, wide, (((1,), (1,)), ((), ())), preferred_element_type=jnp.float32
        )

    load_g.wait()
    gain_b[...] = spread(gain_v[...])
    load_s.wait()
    shift_b[...] = spread(shift_v[...])
    load_b.wait()
    for m in range(sections):
        bias_b[m] = spread(bias_v[m : m + 1, :])

    load_w.wait()
    for b in range(3):
        for a in range(3):
            wall[b * channels : (b + 1) * channels, a * channels : (a + 1) * channels] = weights[b, a]

    def wait_for(ref, sem):
        pltpu.make_async_copy(ref, ref, sem).wait()

    lane = lax.broadcasted_iota(jnp.int32, (ROWS_OUT, columns), 1)

    def sample(m, carry):
        wait_for(xbuf.at[m, pl.ds(1, 2)], ends_rs.at[m])

        @pl.when(jnp.logical_or(k > 0, m > 0))
        def _():
            pass_on(m, xbuf.at[m, 1], xbuf.at[m, 2])

        wait_for(stat_in.at[m], stat_rs.at[m])
        total = jnp.sum(stat_in[m], axis=0)
        mean = total * inv_count
        var = pltpu.roll(mean, 128 - GROUPS, 1) - mean * mean
        inv = lax.rsqrt(jnp.maximum(var, 0.0) + EPS)
        scale = to_channels(inv) * gain_b[...]
        offset = shift_b[...] - to_channels(mean) * scale

        def activate(values):
            v = values.astype(jnp.float32) * scale + offset
            half = 0.5 * v
            return half + half * jnp.tanh(half)

        def put(j, value):
            value = value.astype(jnp.bfloat16)
            for a in range(3):
                r = j - a
                if 0 <= r < height:
                    ybuf[a * channels : (a + 1) * channels, r * columns : (r + 1) * columns] = value

        put(1, activate(xbuf[m, 1]))
        tail = activate(xbuf[m, 2])
        wait_for(xbuf.at[m, 3], mid_rs.at[m])
        mid = activate(xbuf[m, 3])

        @pl.when(p > 0)
        def _():
            wait_for(xbuf.at[m, 0], up_rs.at[m])

        @pl.when(p < patches - 1)
        def _():
            wait_for(xbuf.at[m, 4], low_rs.at[m])

        put(0, jnp.where(p > 0, activate(xbuf[m, 0]), 0.0))
        below = jnp.where(p < patches - 1, activate(xbuf[m, 4]), 0.0)
        one, two = height_own == 1, height_own == 2
        put(2, jnp.where(one, below, jnp.where(two, tail, mid)))
        put(3, jnp.where(one, 0.0, jnp.where(two, below, tail)))
        put(4, jnp.where(height_own == 3, below, 0.0))

        tbuf[...] = jnp.dot(wall[...], ybuf[...], preferred_element_type=jnp.float32)

        @pl.when(is_odd)
        def _():
            wait_for(skip.at[m], skip_rs.at[m])

        for c0 in range(0, channels, ROWS_OUT):
            cs = slice(c0, c0 + ROWS_OUT)
            sums = jnp.zeros((ROWS_OUT, columns), jnp.float32)
            squares = sums
            edge = None
            for r in range(height):
                ls = slice(r * columns, (r + 1) * columns)
                left = pltpu.roll(tbuf[c0 : c0 + ROWS_OUT, ls], 1, 1)
                mid = tbuf[channels + c0 : channels + c0 + ROWS_OUT, ls]
                right = pltpu.roll(
                    tbuf[2 * channels + c0 : 2 * channels + c0 + ROWS_OUT, ls], columns - 1, 1
                )
                z = (
                    jnp.where(lane > 0, left, 0.0)
                    + mid
                    + jnp.where(lane < columns - 1, right, 0.0)
                    + bias_b[m, cs]
                )
                z = jnp.where(is_odd, skip[m, r, cs].astype(jnp.float32) + z, z)
                value = jnp.where(r < height_own, z, 0.0).astype(jnp.bfloat16)
                obuf[m, r, cs] = value
                wide = value.astype(jnp.float32)
                sums = sums + wide
                squares = squares + wide * wide
                edge = value if r == 0 else jnp.where(height_own == r + 1, value, edge)
            edge_out[m, cs] = edge
            sum_b[cs] = sums
            sq_b[cs] = squares

        @pl.when(jnp.logical_not(last))
        def _():
            send_rows(
                m, k + 1, obuf.at[m, 0], edge_out.at[m], obuf.at[m, 1], ends_ss.at[m], mid_ss.at[m]
            )
            write_stats(stat_out.at[m], sum_b[...], sq_b[...])
            send_stats(m, k + 1, stat_out.at[m], stat_ss.at[m], None)

        if sections > 2:
            @pl.when(has_far)
            def _():
                remote(obuf.at[m], skip.at[m], skip_ss.at[m], skip_rs.at[m], k + 2, p).start()

        pltpu.make_async_copy(obuf.at[m], out_ref.at[m], out_sem.at[m]).start()
        return carry

    lax.fori_loop(0, sections, sample, 0)

    wait_for(stat_in.at[0, pl.ds(1, patches - 1)], first_sem.at[0])

    @pl.when(k > 0)
    def _():
        wait_for(stat_lat, first_sem.at[0])
        wait_for(xbuf.at[0, pl.ds(0, 2)], first_sem.at[1])
        wait_for(edge_lat, first_sem.at[2])

    @pl.when(k != 1)
    def _():
        wait_for(lat, first_sem.at[3])

    def drain(m, carry):
        @pl.when(p < patches - 1)
        def _():
            wait_for(edge_lat, up_ss.at[m])

        @pl.when(p > 0)
        def _():
            wait_for(edge_lat, low_ss.at[m])

        @pl.when(jnp.logical_not(last))
        def _():
            wait_for(xbuf.at[m, pl.ds(0, 2)], ends_ss.at[m])
            wait_for(edge_lat, mid_ss.at[m])
            wait_for(stat_in.at[m], stat_ss.at[m])

        if sections > 2:
            @pl.when(has_far)
            def _():
                wait_for(obuf.at[m], skip_ss.at[m])

        wait_for(obuf.at[m], out_sem.at[m])
        return carry

    lax.fori_loop(0, sections, drain, 0)


def paired_kernel(
    patches,
    local,
    heights_in,
    latent_ref,
    weight_ref,
    gain_ref,
    shift_ref,
    bias_ref,
    out_ref,
    lat,
    weights,
    wall,
    part,
    xin,
    xmid,
    ends,
    heights_ref,
    gain_v,
    shift_v,
    bias_v,
    params,
    params_in,
    stat_lat,
    stat_mate,
    stat_all,
    total_out,
    total_in,
    stat_mid,
    stat_mid_all,
    gain_b,
    shift_b,
    bias_b,
    ybuf,
    tbuf,
    sum_b,
    sq_b,
    load_sem,
    ready,
    small_rs,
    small_ss,
    row_rs,
    row_ss,
    edge_rs,
    edge_ss,
    seed_rs,
    seed_ss,
    share_rs,
    share_ss,
    core_rs,
    core_ss,
    mid_rs,
    mid_ss,
    own_edge_rs,
    own_edge_ss,
    far_edge_rs,
    far_edge_ss,
    stat_rs,
    stat_ss,
):
    k = lax.axis_index("section")
    p = lax.axis_index("patch")
    height, channels, columns = lat.shape
    per_group = channels // GROUPS
    rest = channels - local
    piece = part.shape[0] // (8 * SUB)

    core = lax.rem(p, 2)
    mate = p + 1 - 2 * core
    across = p - 1 + 2 * core
    has_across = jnp.logical_and(across >= 0, across < patches)
    member = lax.rem(p, 8)
    turn_y = 2 - 4 * lax.rem(member // 2, 2)
    turn_z = 4 - 8 * (member // 4)
    friends = (p + turn_y, p + turn_z, p + turn_y + turn_z)

    load_h = pltpu.make_async_copy(heights_in, heights_ref, load_sem.at[0])
    load_lat = pltpu.make_async_copy(latent_ref, lat, load_sem.at[1])
    load_g = pltpu.make_async_copy(gain_ref, gain_v, load_sem.at[2])
    load_s = pltpu.make_async_copy(shift_ref, shift_v, load_sem.at[3])
    load_b = pltpu.make_async_copy(bias_ref, bias_v, load_sem.at[4])
    load_w = pltpu.make_async_copy(weight_ref, weights, load_sem.at[5])
    for load in (load_h, load_lat, load_g, load_s, load_b, load_w):
        load.start()

    barrier = pltpu.get_barrier_semaphore()

    def signal(s, q):
        pl.semaphore_signal(barrier, inc=1, device_id=(s, q), device_id_type=MESH)

    @pl.when(k == 0)
    def _():
        signal(1, p)

        def step(i, carry):
            signal(0, lax.rem(p + i, patches))
            return carry

        lax.fori_loop(1, patches, step, 0)

    @pl.when(k == 1)
    def _():
        for q in (mate, *friends):
            signal(1, q)

        @pl.when(has_across)
        def _():
            signal(1, across)

    def remote(src, dst, ssem, rsem, s, q):
        return pltpu.make_async_remote_copy(
            src_ref=src, dst_ref=dst, send_sem=ssem, recv_sem=rsem,
            device_id=(s, q), device_id_type=MESH,
        )

    def wait_for(ref, sem):
        pltpu.make_async_copy(ref, ref, sem).wait()

    load_h.wait()
    height_own = heights_ref[p]
    window_rows = heights_ref[0]
    for i in range(1, patches):
        window_rows = window_rows + heights_ref[i]
    inv_count = 1.0 / (
        jnp.full((1, 128), window_rows, jnp.int32).astype(jnp.float32)
        * (per_group * columns)
    )

    chan = lax.broadcasted_iota(jnp.int32, (channels, 128), 0)
    first = lax.broadcasted_iota(jnp.int32, (channels, 128), 1) * per_group
    group_mask = jnp.where(
        jnp.logical_and(chan >= first, chan < first + per_group), 1.0, 0.0
    ).astype(jnp.float32)

    def to_groups(per_chan):
        total = jnp.sum(per_chan, axis=1, keepdims=True)
        return jnp.sum(total * group_mask, axis=0, keepdims=True)

    def to_channels(per_group_row):
        return jnp.sum(per_group_row * group_mask, axis=1, keepdims=True)

    def both(sums, squares):
        return to_groups(sums) + pltpu.roll(to_groups(squares), GROUPS, 1)

    load_lat.wait()
    rows = [
        jnp.where(r < height_own, lat[r].astype(jnp.float32), 0.0) for r in range(height)
    ]
    sums, squares, edge = rows[0], rows[0] * rows[0], lat[0]
    for r in range(1, height):
        sums = sums + rows[r]
        squares = squares + rows[r] * rows[r]
        edge = jnp.where(height_own == r + 1, lat[r], edge)
    xin[k, 1] = lat[0]
    xin[k, 2] = edge
    xin[k, 3] = lat[1]
    stat_lat[...] = both(sums, squares)

    def take_params():
        load_g.wait()
        load_s.wait()
        load_b.wait()
        params[0:1] = gain_v[...].astype(jnp.float32)
        params[1:2] = shift_v[...].astype(jnp.float32)
        params[2:4] = bias_v[...].astype(jnp.float32)

    eye = jnp.where(
        lax.broadcasted_iota(jnp.int32, (channels, channels), 0)
        == lax.broadcasted_iota(jnp.int32, (channels, channels), 1),
        1.0,
        0.0,
    ).astype(jnp.bfloat16)

    def spread(row):
        wide = jnp.broadcast_to(row, (128, channels)).astype(jnp.bfloat16)
        return lax.dot_general(
            eye, wide, (((1,), (1,)), ((), ())), preferred_element_type=jnp.float32
        )

    def spread_params(at, source):
        gain_b[at] = spread(source[0:1])
        shift_b[at] = spread(source[1:2])
        for m in range(2):
            bias_b[at, m] = spread(source[2 + m : 3 + m])

    def build(is_rest):
        for b in range(3):
            for a in range(3):
                cols = slice(a * channels, (a + 1) * channels)
                if is_rest:
                    start = 3 * local + b * rest
                    wall[start : start + rest, cols] = weights[b, a, local:]
                else:
                    wall[b * local : (b + 1) * local, cols] = weights[b, a, :local]

    cross_slot, other_slot = 1 + core, 2 - core

    def send_rows():
        for i, slot in enumerate((cross_slot, other_slot, 3)):
            remote(xin.at[k, slot], xin.at[k, slot], row_ss.at[i], row_rs.at[i], 1 - k, p).start()

    def wait_row(i):
        wait_for(lat.at[0], row_rs.at[i])

    def send_edge(kind, ref, m, span, ssem, rsem):
        src_slot = cross_slot if kind == 0 else other_slot
        dst_slot = 4 - 4 * core if kind == 0 else 4 * core
        q = across if kind == 0 else mate

        def go():
            remote(
                ref.at[m, src_slot, span], ref.at[m, dst_slot, span],
                ssem.at[m, kind], rsem.at[m, kind], k, q,
            ).start()

        if kind == 0:
            pl.when(has_across)(go)
        else:
            go()

    def wait_edge(kind, ref, sem, m):
        if kind == 0:
            @pl.when(has_across)
            def _():
                wait_for(ref, sem.at[m, kind])
        else:
            wait_for(ref, sem.at[m, kind])

    whole = pl.ds(0, channels)
    head_part = pl.ds(0, local)
    tail_part = pl.ds(local, rest)

    def pass_in(kind, m):
        send_edge(kind, xin, m, whole, edge_ss, edge_rs)

    def coefficients(total, at):
        mean = total * inv_count
        var = pltpu.roll(mean, 128 - GROUPS, 1) - mean * mean
        inv = lax.rsqrt(jnp.maximum(var, 0.0) + EPS)
        scale = to_channels(inv) * gain_b[at]
        return scale, shift_b[at] - to_channels(mean) * scale

    def fill(rows_of, m, scale, offset, before_edges):
        def activate(values):
            v = values.astype(jnp.float32) * scale + offset
            half = 0.5 * v
            return half + half * jnp.tanh(half)

        def put(j, value):
            value = value.astype(jnp.bfloat16)
            for a in range(3):
                r = j - a
                if 0 <= r < height:
                    at = (m * height + r) * columns
                    ybuf[a * channels : (a + 1) * channels, at : at + columns] = value

        put(1, activate(rows_of[m, 1]))
        tail = activate(rows_of[m, 2])
        mid = activate(rows_of[m, 3])
        before_edges()
        put(0, jnp.where(p > 0, activate(rows_of[m, 0]), 0.0))
        below = jnp.where(p < patches - 1, activate(rows_of[m, 4]), 0.0)
        one, two = height_own == 1, height_own == 2
        put(2, jnp.where(one, below, jnp.where(two, tail, mid)))
        put(3, jnp.where(one, 0.0, jnp.where(two, below, tail)))
        put(4, jnp.where(height_own == 3, below, 0.0))

    lane = lax.broadcasted_iota(jnp.int32, (ROWS_OUT, columns), 1)

    def conv_row(m, r, c0, count, bias):
        at = (m * height + r) * columns
        ls = slice(at, at + columns)

        def block(b):
            start = b * local + c0 if c0 < local else 3 * local + b * rest + c0 - local
            return tbuf[start : start + count, ls]

        return (
            jnp.where(lane > 0, pltpu.roll(block(0), 1, 1), 0.0)
            + block(1)
            + jnp.where(lane < columns - 1, pltpu.roll(block(2), columns - 1, 1), 0.0)
            + bias
        )

    def send_mid(i, m):
        src = (ends.at[m, core], ends.at[m, 1 - core], out_ref.at[m, 1])[i]
        slot = (cross_slot, other_slot, 3)[i]
        remote(
            src.at[tail_part], xmid.at[m, slot, tail_part], mid_ss.at[m, i], mid_rs.at[m, i], 1, p
        ).start()

    def multiply(count, m0, samples):
        cols = slice(m0 * height * columns, (m0 + samples) * height * columns)
        tbuf[:count, cols] = jnp.dot(
            wall[...] if count > 3 * local else part[...],
            ybuf[:, cols],
            preferred_element_type=jnp.float32,
        )

    @pl.when(k == 1)
    def _():
        pl.semaphore_wait(barrier, 5 + has_across.astype(jnp.int32))
        pl.semaphore_signal(ready, inc=1, device_id=(0, p), device_id_type=MESH)
        remote(stat_lat, stat_mate, small_ss.at[1], small_rs.at[1], 0, p).start()
        send_rows()
        pass_in(0, 1)
        pass_in(1, 1)
        take_params()
        spread_params(0, params)
        load_w.wait()
        build(False)
        build(True)

    @pl.when(k == 0)
    def _():
        take_params()
        load_w.wait()
        build(False)
        pl.semaphore_wait(ready, 1)
        remote(params, params_in, small_ss.at[0], small_rs.at[0], 1, p).start()
        for i in range(SUB):
            at = pl.ds((member * SUB + i) * piece, piece)
            remote(wall.at[at], part.at[at], seed_ss.at[i], seed_rs.at[i], 1, p).start()
        send_rows()
        pl.semaphore_wait(barrier, patches - 1)

        def share_stats(m, source):
            def step(i, carry):
                q = lax.rem(p + i, patches)
                remote(
                    source, stat_all.at[m, p], small_ss.at[2 + m], small_rs.at[2 + m], 0, q
                ).start()
                return carry

            lax.fori_loop(1, patches, step, 0)
            stat_all[m, p] = source[...]

        def total_of(m):
            wait_for(stat_all.at[m, pl.ds(0, patches - 1)], small_rs.at[2 + m])
            total = jnp.sum(stat_all[m], axis=0)
            total_out[m] = total
            remote(
                total_out.at[m], total_in.at[m], small_ss.at[4 + m], small_rs.at[4 + m], 1, p
            ).start()
            return total

        share_stats(0, stat_lat)
        pass_in(0, 0)
        pass_in(1, 0)
        spread_params(0, params)
        build(True)
        wait_for(stat_lat, small_rs.at[1])
        share_stats(1, stat_mate)
        wait_row(0)
        pass_in(0, 1)

        for m in range(2):
            scale, offset = coefficients(total_of(m), 0)

            def before_edges():
                if m == 0:
                    wait_row(1)
                    pass_in(1, 1)
                for kind in range(2):
                    wait_edge(kind, lat.at[0], edge_rs, m)

            if m == 1:
                wait_row(2)
            fill(xin, m, scale, offset, before_edges)
            multiply(3 * channels, m, 1)
            for c0 in range(0, channels, ROWS_OUT):
                cs = slice(c0, c0 + ROWS_OUT)
                sums = jnp.zeros((ROWS_OUT, columns), jnp.float32)
                squares = sums
                edge = None
                for r in range(height):
                    z = conv_row(m, r, c0, ROWS_OUT, bias_b[0, m, cs])
                    value = jnp.where(r < height_own, z, 0.0).astype(jnp.bfloat16)
                    out_ref[m, r, cs] = value
                    wide = value.astype(jnp.float32)
                    sums = sums + wide
                    squares = squares + wide * wide
                    edge = value if r == 0 else jnp.where(height_own == r + 1, value, edge)
                    if r == 0:
                        ends[m, 0, cs] = value
                ends[m, 1, cs] = edge
                sum_b[cs] = sums
                sq_b[cs] = squares
            stat_mid[m] = both(sum_b[...], sq_b[...])

            def step(i, carry):
                q = lax.rem(p + i, patches)
                remote(stat_mid.at[m], stat_mid_all.at[m, p], stat_ss.at[m], stat_rs.at[m], 1, q).start()
                return carry

            send_mid(0, m)
            if m == 0:
                send_mid(1, 0)
            lax.fori_loop(0, patches, step, 0)
        send_mid(2, 0)
        send_mid(1, 1)
        send_mid(2, 1)

        wait_for(params, small_ss.at[0])
        for m in range(2):
            wait_for(stat_all.at[m, pl.ds(0, patches - 1)], small_ss.at[2 + m])
            wait_for(total_out.at[m], small_ss.at[4 + m])
        for i in range(SUB):
            wait_for(part.at[pl.ds(0, piece)], seed_ss.at[i])
        for m in range(2):
            wait_for(stat_mid_all.at[m], stat_ss.at[m])
            for i in range(3):
                wait_for(out_ref.at[m, 1, tail_part], mid_ss.at[m, i])

    @pl.when(k == 1)
    def _():
        def to_mate(index, sem):
            at = pl.ds(index * piece, piece)
            remote(part.at[at], part.at[at], core_ss.at[sem], core_rs.at[0], 1, mate).start()

        def seed(i, carry):
            index = member * SUB + i
            at = pl.ds(index * piece, piece)
            wait_for(part.at[pl.ds(0, piece)], seed_rs.at[i])
            for j in range(3):
                remote(
                    part.at[at], part.at[at], share_ss.at[j, i], share_rs.at[j, i], 1, friends[j]
                ).start()
            to_mate(index, i)
            return carry

        lax.fori_loop(0, SUB, seed, 0)
        wait_for(params, small_rs.at[0])
        spread_params(1, params_in)
        wait_row(0)
        pass_in(0, 0)

        def shared(i, carry):
            for j in range(3):
                wait_for(part.at[pl.ds(0, piece)], share_rs.at[j, i])
                to_mate(lax.rem(friends[j], 8) * SUB + i, (1 + j) * SUB + i)
            return carry

        lax.fori_loop(0, SUB, shared, 0)
        wait_row(1)
        pass_in(1, 0)
        wait_row(2)

        def pass_far(kind, m):
            wait_for(out_ref.at[m, 1, tail_part], mid_rs.at[m, kind])
            send_edge(kind, xmid, m, tail_part, far_edge_ss, far_edge_rs)

        for m in range(2):
            pass_far(0, m)
            wait_for(total_out.at[m], small_rs.at[4 + m])
            scale, offset = coefficients(total_in[m], 1)

            def before_edges():
                for kind in range(2):
                    wait_edge(kind, lat.at[0], edge_rs, m)

            fill(xin, m, scale, offset, before_edges)
            if m == 0:
                wait_for(part.at[pl.ds(0, 4 * SUB * piece)], core_rs.at[0])
            multiply(3 * local, m, 1)
            for c0 in range(0, local, ROWS_OUT):
                cs = slice(c0, c0 + ROWS_OUT)
                edge = None
                for r in range(height):
                    value = conv_row(m, r, c0, ROWS_OUT, bias_b[1, m, cs]).astype(jnp.bfloat16)
                    edge = value if r == 0 else jnp.where(height_own == r + 1, value, edge)
                    if r == 0:
                        xmid[m, 1, cs] = value
                    if r == 1:
                        xmid[m, 3, cs] = value
                xmid[m, 2, cs] = edge
            for kind in range(2):
                send_edge(kind, xmid, m, head_part, own_edge_ss, own_edge_rs)
            pass_far(1, m)

        for m in range(2):
            wait_for(stat_mid_all.at[m], stat_rs.at[m])
            scale, offset = coefficients(jnp.sum(stat_mid_all[m], axis=0), 0)
            wait_for(out_ref.at[m, 1, tail_part], mid_rs.at[m, 2])

            def before_edges():
                for kind in range(2):
                    wait_edge(kind, lat.at[0, head_part], own_edge_rs, m)
                    wait_edge(kind, lat.at[0, tail_part], far_edge_rs, m)

            fill(xmid, m, scale, offset, before_edges)
            multiply(3 * channels, m, 1)
            for c0 in range(0, channels, ROWS_OUT):
                cs = slice(c0, c0 + ROWS_OUT)
                for r in range(height):
                    z = conv_row(m, r, c0, ROWS_OUT, bias_b[0, m, cs])
                    z = xin[m, (1, 3, 2)[r], cs].astype(jnp.float32) + z
                    out_ref[m, r, cs] = jnp.where(r < height_own, z, 0.0).astype(jnp.bfloat16)

        wait_for(stat_lat, small_ss.at[1])
        for i in range(SUB):
            for j in range(3):
                wait_for(part.at[pl.ds(0, piece)], share_ss.at[j, i])
        for i in range(4 * SUB):
            wait_for(part.at[pl.ds(0, piece)], core_ss.at[i])
        for m in range(2):
            for kind in range(2):
                wait_edge(kind, lat.at[0, head_part], own_edge_ss, m)
                wait_edge(kind, lat.at[0, tail_part], far_edge_ss, m)

    for i in range(3):
        wait_for(lat.at[0], row_ss.at[i])
    for m in range(2):
        for kind in range(2):
            wait_edge(kind, lat.at[0], edge_ss, m)


def paired_call(patches, operands, height, channels, columns):
    bf16, f32 = jnp.bfloat16, jnp.float32
    local = channels * 2 // 5
    hbm = pl.BlockSpec(memory_space=pltpu.HBM)
    dma = pltpu.SemaphoreType.DMA
    return pl.pallas_call(
        functools.partial(paired_kernel, patches, local),
        out_shape=jax.ShapeDtypeStruct((2, height, channels, columns), bf16),
        in_specs=[hbm] * 6,
        out_specs=pl.BlockSpec(memory_space=pltpu.VMEM),
        scratch_shapes=[
            pltpu.VMEM((height, channels, columns), bf16),
            pltpu.VMEM((3, 3, channels, channels), bf16),
            pltpu.VMEM((3 * channels, 3 * channels), bf16),
            pltpu.VMEM((3 * local, 3 * channels), bf16),
            pltpu.VMEM((2, height + 2, channels, columns), bf16),
            pltpu.VMEM((2, height + 2, channels, columns), bf16),
            pltpu.VMEM((2, 2, channels, columns), bf16),
            pltpu.SMEM((patches,), jnp.int32),
            pltpu.VMEM((1, channels), bf16),
            pltpu.VMEM((1, channels), bf16),
            pltpu.VMEM((2, channels), bf16),
            pltpu.VMEM((8, channels), f32),
            pltpu.VMEM((8, channels), f32),
            pltpu.VMEM((1, 128), f32),
            pltpu.VMEM((1, 128), f32),
            pltpu.VMEM((2, patches, 1, 128), f32),
            pltpu.VMEM((2, 1, 128), f32),
            pltpu.VMEM((2, 1, 128), f32),
            pltpu.VMEM((2, 1, 128), f32),
            pltpu.VMEM((2, patches, 1, 128), f32),
            pltpu.VMEM((2, channels, 128), f32),
            pltpu.VMEM((2, channels, 128), f32),
            pltpu.VMEM((2, 2, channels, 128), f32),
            pltpu.VMEM((3 * channels, 2 * height * columns), bf16),
            pltpu.VMEM((3 * channels, 2 * height * columns), f32),
            pltpu.VMEM((channels, columns), f32),
            pltpu.VMEM((channels, columns), f32),
            dma((6,)),
            pltpu.SemaphoreType.REGULAR,
            dma((6,)),
            dma((6,)),
            dma((3,)),
            dma((3,)),
            dma((2, 2)),
            dma((2, 2)),
            dma((SUB,)),
            dma((SUB,)),
            dma((3, SUB)),
            dma((3, SUB)),
            dma((1,)),
            dma((4 * SUB,)),
            dma((2, 3)),
            dma((2, 3)),
            dma((2, 2)),
            dma((2, 2)),
            dma((2, 2)),
            dma((2, 2)),
            dma((2,)),
            dma((2,)),
        ],
        compiler_params=pltpu.CompilerParams(
            collective_id=0, has_side_effects=True, vmem_limit_bytes=48 * 1024 * 1024
        ),
    )(*operands)


def per_device(sections, patches, latent, conv_weight, norm_gain, norm_shift, step_bias, patch_rows):
    latent = jnp.transpose(latent[0], (1, 0, 2))
    weight = jnp.transpose(conv_weight[0], (0, 2, 1, 3))
    height, channels, columns = latent.shape
    bf16, f32 = jnp.bfloat16, jnp.float32
    hbm = pl.BlockSpec(memory_space=pltpu.HBM)
    dma = pltpu.SemaphoreType.DMA
    operands = [
        pltpu.with_memory_space_constraint(array, pltpu.HBM)
        for array in (patch_rows, latent, weight, norm_gain, norm_shift, step_bias[0])
    ]
    if sections == 2 and patches % 8 == 0:
        out = paired_call(patches, operands, height, channels, columns)
        return jnp.transpose(out, (0, 2, 1, 3))[None]
    out = pl.pallas_call(
        functools.partial(kernel, sections, patches),
        out_shape=jax.ShapeDtypeStruct((sections, height, channels, columns), bf16),
        in_specs=[hbm] * 6,
        out_specs=pl.BlockSpec(memory_space=pl.ANY),
        scratch_shapes=[
            pltpu.VMEM((height, channels, columns), bf16),
            pltpu.VMEM((3, 3, channels, channels), bf16),
            pltpu.VMEM((3 * channels, 3 * channels), bf16),
            pltpu.VMEM((sections, height + 2, channels, columns), bf16),
            pltpu.VMEM((sections, height, channels, columns), bf16),
            pltpu.VMEM((sections, height, channels, columns), bf16),
            pltpu.VMEM((channels, columns), bf16),
            pltpu.VMEM((sections, channels, columns), bf16),
            pltpu.SMEM((patches,), jnp.int32),
            pltpu.VMEM((1, channels), bf16),
            pltpu.VMEM((1, channels), bf16),
            pltpu.VMEM((sections, channels), bf16),
            pltpu.VMEM((1, 128), f32),
            pltpu.VMEM((sections, 1, 128), f32),
            pltpu.VMEM((sections, patches, 1, 128), f32),
            pltpu.VMEM((channels, 128), f32),
            pltpu.VMEM((channels, 128), f32),
            pltpu.VMEM((sections, channels, 128), f32),
            pltpu.VMEM((3 * channels, height * columns), bf16),
            pltpu.VMEM((3 * channels, height * columns), f32),
            pltpu.VMEM((channels, columns), f32),
            pltpu.VMEM((channels, columns), f32),
            dma((6,)),
            dma((4,)),
        ]
        + [dma((sections,)) for _ in range(13)],
        compiler_params=pltpu.CompilerParams(
            collective_id=0, has_side_effects=True, vmem_limit_bytes=48 * 1024 * 1024
        ),
    )(*operands)
    return jnp.transpose(out, (0, 2, 1, 3))[None]


def solution(mesh):
    placed = (
        P("section", None, "patch", None),
        P("section", None, None, None, None),
        P("section", None),
        P("section", None),
        P("section", None, None),
        P(),
    )
    return jax.shard_map(
        functools.partial(per_device, mesh.shape["section"], mesh.shape["patch"]),
        mesh=mesh,
        in_specs=placed,
        out_specs=P("section", None, None, "patch", None),
        check_vma=False,
    )
```

```python
import functools

import jax
import jax.numpy as jnp
from jax import lax
from jax.experimental import pallas as pl
from jax.experimental.pallas import tpu as pltpu
from jax.sharding import PartitionSpec as P

GROUPS = 32
EPS = 1e-05
MESH = pl.DeviceIdType.MESH
ROWS_OUT = 64
SUB = 3


def kernel(
    sections,
    patches,
    heights_in,
    latent_ref,
    weight_ref,
    gain_ref,
    shift_ref,
    bias_ref,
    out_ref,
    lat,
    weights,
    wall,
    xbuf,
    skip,
    obuf,
    edge_lat,
    edge_out,
    heights_ref,
    gain_v,
    shift_v,
    bias_v,
    stat_lat,
    stat_out,
    stat_in,
    gain_b,
    shift_b,
    bias_b,
    ybuf,
    tbuf,
    sum_b,
    sq_b,
    local_sem,
    first_sem,
    ends_rs,
    mid_rs,
    up_rs,
    low_rs,
    stat_rs,
    skip_rs,
    ends_ss,
    mid_ss,
    up_ss,
    low_ss,
    stat_ss,
    skip_ss,
    out_sem,
):
    k = lax.axis_index("section")
    p = lax.axis_index("patch")
    height, channels, columns = lat.shape
    per_group = channels // GROUPS
    is_odd = lax.rem(k, 2) == 1
    last = k == sections - 1
    has_far = jnp.logical_and(is_odd, k + 2 < sections)

    load_lat = pltpu.make_async_copy(latent_ref, lat, local_sem.at[0])
    load_w = pltpu.make_async_copy(weight_ref, weights, local_sem.at[1])
    load_h = pltpu.make_async_copy(heights_in, heights_ref, local_sem.at[2])
    load_g = pltpu.make_async_copy(gain_ref, gain_v, local_sem.at[3])
    load_s = pltpu.make_async_copy(shift_ref, shift_v, local_sem.at[4])
    load_b = pltpu.make_async_copy(bias_ref, bias_v, local_sem.at[5])
    load_h.start()
    load_lat.start()
    load_g.start()
    load_s.start()
    load_b.start()
    load_w.start()

    barrier = pltpu.get_barrier_semaphore()

    def signal(s, q):
        pl.semaphore_signal(barrier, inc=1, device_id=(s, q), device_id_type=MESH)

    @pl.when(k == 0)
    def _():
        def step(i, c):
            q = lax.rem(p + i, patches)
            for s in range(sections):
                if s == 0:
                    @pl.when(i > 0)
                    def _():
                        signal(0, q)
                else:
                    signal(s, q)
            return c

        lax.fori_loop(0, patches, step, 0)

    @pl.when(k > 0)
    def _():
        def step(i, c):
            signal(k - 1, lax.rem(p + i, patches))
            return c

        lax.fori_loop(0, patches, step, 0)

        @pl.when(p > 0)
        def _():
            signal(k, p - 1)

        @pl.when(p < patches - 1)
        def _():
            signal(k, p + 1)

    if sections > 2:
        @pl.when(k == 1)
        def _():
            for s in range(2, sections):
                signal(s, p)

        @pl.when(jnp.logical_and(is_odd, k >= 3))
        def _():
            signal(k - 2, p)

    load_h.wait()
    height_own = heights_ref[p]
    window_rows = heights_ref[0]
    for i in range(1, patches):
        window_rows = window_rows + heights_ref[i]
    inv_count = 1.0 / (
        jnp.full((1, 128), window_rows, jnp.int32).astype(jnp.float32)
        * (per_group * columns)
    )

    chan = lax.broadcasted_iota(jnp.int32, (channels, 128), 0)
    first = lax.broadcasted_iota(jnp.int32, (channels, 128), 1) * per_group
    group_mask = jnp.where(
        jnp.logical_and(chan >= first, chan < first + per_group), 1.0, 0.0
    ).astype(jnp.float32)

    def to_groups(per_chan):
        total = jnp.sum(per_chan, axis=1, keepdims=True)
        return jnp.sum(total * group_mask, axis=0, keepdims=True)

    def to_channels(per_group_row):
        return jnp.sum(per_group_row * group_mask, axis=1, keepdims=True)

    def write_stats(ref, sums, squares):
        ref[...] = to_groups(sums) + pltpu.roll(to_groups(squares), GROUPS, 1)

    load_lat.wait()
    rows = [
        jnp.where(r < height_own, lat[r].astype(jnp.float32), 0.0) for r in range(height)
    ]
    sums, squares, edge = rows[0], rows[0] * rows[0], lat[0]
    for r in range(1, height):
        sums = sums + rows[r]
        squares = squares + rows[r] * rows[r]
        edge = jnp.where(height_own == r + 1, lat[r], edge)
    edge_lat[...] = edge
    write_stats(stat_lat, sums, squares)

    sends_to = (
        patches
        - (k == 0).astype(jnp.int32)
        + jnp.where(last, 0, patches)
        + jnp.where(k > 0, (p > 0).astype(jnp.int32) + (p < patches - 1).astype(jnp.int32), 0)
        + (k >= 2).astype(jnp.int32)
        + has_far.astype(jnp.int32)
    )
    pl.semaphore_wait(barrier, sends_to)

    def remote(src, dst, ssem, rsem, s, q):
        return pltpu.make_async_remote_copy(
            src_ref=src, dst_ref=dst, send_sem=ssem, recv_sem=rsem,
            device_id=(s, q), device_id_type=MESH,
        )

    def send_stats(m, s, stat, ssem, own):
        def step(i, c):
            q = lax.rem(p + i, patches)
            remote(stat, stat_in.at[m, p], ssem, stat_rs.at[m], s, q).start()
            return c

        if own is None:
            lax.fori_loop(0, patches, step, 0)
        else:
            lax.fori_loop(1, patches, step, 0)

            @pl.when(own)
            def _():
                pltpu.make_async_copy(stat, stat_in.at[m, p], stat_rs.at[m]).start()

            @pl.when(jnp.logical_not(own))
            def _():
                step(0, 0)

    def send_rows(m, s, head, tail, mid, ssem_ends, ssem_mid):
        remote(head, xbuf.at[m, 1], ssem_ends, ends_rs.at[m], s, p).start()
        remote(tail, xbuf.at[m, 2], ssem_ends, ends_rs.at[m], s, p).start()
        remote(mid, xbuf.at[m, 3], ssem_mid, mid_rs.at[m], s, p).start()

    def pass_on(m, head, tail):
        @pl.when(p < patches - 1)
        def _():
            remote(tail, xbuf.at[m, 0], up_ss.at[m], up_rs.at[m], k, p + 1).start()

        @pl.when(p > 0)
        def _():
            remote(head, xbuf.at[m, 4], low_ss.at[m], low_rs.at[m], k, p - 1).start()

    send_stats(k, 0, stat_lat, first_sem.at[0], k == 0)

    @pl.when(k == 0)
    def _():
        pass_on(0, lat.at[0], edge_lat)
        pltpu.make_async_copy(lat.at[0], xbuf.at[0, 1], ends_rs.at[0]).start()
        pltpu.make_async_copy(edge_lat, xbuf.at[0, 2], ends_rs.at[0]).start()
        pltpu.make_async_copy(lat.at[1], xbuf.at[0, 3], mid_rs.at[0]).start()

    @pl.when(k > 0)
    def _():
        send_rows(k, 0, lat.at[0], edge_lat, lat.at[1], first_sem.at[1], first_sem.at[2])

    @pl.when(k == 1)
    def _():
        pltpu.make_async_copy(lat, skip.at[1], skip_rs.at[1]).start()

    @pl.when(k != 1)
    def _():
        remote(lat, skip.at[k], first_sem.at[3], skip_rs.at[k], 1, p).start()

    eye = jnp.where(
        lax.broadcasted_iota(jnp.int32, (channels, channels), 0)
        == lax.broadcasted_iota(jnp.int32, (channels, channels), 1),
        1.0,
        0.0,
    ).astype(jnp.bfloat16)

    def spread(row):
        wide = jnp.broadcast_to(row.astype(jnp.float32), (128, channels)).astype(jnp.bfloat16)
        return lax.dot_general(
            eye, wide, (((1,), (1,)), ((), ())), preferred_element_type=jnp.float32
        )

    load_g.wait()
    gain_b[...] = spread(gain_v[...])
    load_s.wait()
    shift_b[...] = spread(shift_v[...])
    load_b.wait()
    for m in range(sections):
        bias_b[m] = spread(bias_v[m : m + 1, :])

    load_w.wait()
    for b in range(3):
        for a in range(3):
            wall[b * channels : (b + 1) * channels, a * channels : (a + 1) * channels] = weights[b, a]

    def wait_for(ref, sem):
        pltpu.make_async_copy(ref, ref, sem).wait()

    lane = lax.broadcasted_iota(jnp.int32, (ROWS_OUT, columns), 1)

    def sample(m, carry):
        wait_for(xbuf.at[m, pl.ds(1, 2)], ends_rs.at[m])

        @pl.when(jnp.logical_or(k > 0, m > 0))
        def _():
            pass_on(m, xbuf.at[m, 1], xbuf.at[m, 2])

        wait_for(stat_in.at[m], stat_rs.at[m])
        total = jnp.sum(stat_in[m], axis=0)
        mean = total * inv_count
        var = pltpu.roll(mean, 128 - GROUPS, 1) - mean * mean
        inv = lax.rsqrt(jnp.maximum(var, 0.0) + EPS)
        scale = to_channels(inv) * gain_b[...]
        offset = shift_b[...] - to_channels(mean) * scale

        def activate(values):
            v = values.astype(jnp.float32) * scale + offset
            half = 0.5 * v
            return half + half * jnp.tanh(half)

        def put(j, value):
            value = value.astype(jnp.bfloat16)
            for a in range(3):
                r = j - a
                if 0 <= r < height:
                    ybuf[a * channels : (a + 1) * channels, r * columns : (r + 1) * columns] = value

        put(1, activate(xbuf[m, 1]))
        tail = activate(xbuf[m, 2])
        wait_for(xbuf.at[m, 3], mid_rs.at[m])
        mid = activate(xbuf[m, 3])

        @pl.when(p > 0)
        def _():
            wait_for(xbuf.at[m, 0], up_rs.at[m])

        @pl.when(p < patches - 1)
        def _():
            wait_for(xbuf.at[m, 4], low_rs.at[m])

        put(0, jnp.where(p > 0, activate(xbuf[m, 0]), 0.0))
        below = jnp.where(p < patches - 1, activate(xbuf[m, 4]), 0.0)
        one, two = height_own == 1, height_own == 2
        put(2, jnp.where(one, below, jnp.where(two, tail, mid)))
        put(3, jnp.where(one, 0.0, jnp.where(two, below, tail)))
        put(4, jnp.where(height_own == 3, below, 0.0))

        tbuf[...] = jnp.dot(wall[...], ybuf[...], preferred_element_type=jnp.float32)

        @pl.when(is_odd)
        def _():
            wait_for(skip.at[m], skip_rs.at[m])

        for c0 in range(0, channels, ROWS_OUT):
            cs = slice(c0, c0 + ROWS_OUT)
            sums = jnp.zeros((ROWS_OUT, columns), jnp.float32)
            squares = sums
            edge = None
            for r in range(height):
                ls = slice(r * columns, (r + 1) * columns)
                left = pltpu.roll(tbuf[c0 : c0 + ROWS_OUT, ls], 1, 1)
                mid = tbuf[channels + c0 : channels + c0 + ROWS_OUT, ls]
                right = pltpu.roll(
                    tbuf[2 * channels + c0 : 2 * channels + c0 + ROWS_OUT, ls], columns - 1, 1
                )
                z = (
                    jnp.where(lane > 0, left, 0.0)
                    + mid
                    + jnp.where(lane < columns - 1, right, 0.0)
                    + bias_b[m, cs]
                )
                z = jnp.where(is_odd, skip[m, r, cs].astype(jnp.float32) + z, z)
                value = jnp.where(r < height_own, z, 0.0).astype(jnp.bfloat16)
                obuf[m, r, cs] = value
                wide = value.astype(jnp.float32)
                sums = sums + wide
                squares = squares + wide * wide
                edge = value if r == 0 else jnp.where(height_own == r + 1, value, edge)
            edge_out[m, cs] = edge
            sum_b[cs] = sums
            sq_b[cs] = squares

        @pl.when(jnp.logical_not(last))
        def _():
            send_rows(
                m, k + 1, obuf.at[m, 0], edge_out.at[m], obuf.at[m, 1], ends_ss.at[m], mid_ss.at[m]
            )
            write_stats(stat_out.at[m], sum_b[...], sq_b[...])
            send_stats(m, k + 1, stat_out.at[m], stat_ss.at[m], None)

        if sections > 2:
            @pl.when(has_far)
            def _():
                remote(obuf.at[m], skip.at[m], skip_ss.at[m], skip_rs.at[m], k + 2, p).start()

        pltpu.make_async_copy(obuf.at[m], out_ref.at[m], out_sem.at[m]).start()
        return carry

    lax.fori_loop(0, sections, sample, 0)

    wait_for(stat_in.at[0, pl.ds(1, patches - 1)], first_sem.at[0])

    @pl.when(k > 0)
    def _():
        wait_for(stat_lat, first_sem.at[0])
        wait_for(xbuf.at[0, pl.ds(0, 2)], first_sem.at[1])
        wait_for(edge_lat, first_sem.at[2])

    @pl.when(k != 1)
    def _():
        wait_for(lat, first_sem.at[3])

    def drain(m, carry):
        @pl.when(p < patches - 1)
        def _():
            wait_for(edge_lat, up_ss.at[m])

        @pl.when(p > 0)
        def _():
            wait_for(edge_lat, low_ss.at[m])

        @pl.when(jnp.logical_not(last))
        def _():
            wait_for(xbuf.at[m, pl.ds(0, 2)], ends_ss.at[m])
            wait_for(edge_lat, mid_ss.at[m])
            wait_for(stat_in.at[m], stat_ss.at[m])

        if sections > 2:
            @pl.when(has_far)
            def _():
                wait_for(obuf.at[m], skip_ss.at[m])

        wait_for(obuf.at[m], out_sem.at[m])
        return carry

    lax.fori_loop(0, sections, drain, 0)


def paired_kernel(
    patches,
    local,
    heights_in,
    latent_ref,
    weight_ref,
    gain_ref,
    shift_ref,
    bias_ref,
    out_ref,
    lat,
    weights,
    wall,
    part,
    xin,
    xmid,
    ends,
    heights_ref,
    gain_v,
    shift_v,
    bias_v,
    params,
    params_in,
    stat_lat,
    stat_mate,
    stat_all,
    total_out,
    total_in,
    stat_mid,
    stat_mid_all,
    gain_b,
    shift_b,
    bias_b,
    ybuf,
    tbuf,
    sum_b,
    sq_b,
    load_sem,
    ready,
    greeted,
    small_rs,
    small_ss,
    row_rs,
    row_ss,
    edge_rs,
    edge_ss,
    seed_rs,
    seed_ss,
    share_rs,
    share_ss,
    core_rs,
    core_ss,
    mid_rs,
    mid_ss,
    own_edge_rs,
    own_edge_ss,
    far_edge_rs,
    far_edge_ss,
    stat_rs,
    stat_ss,
):
    k = lax.axis_index("section")
    p = lax.axis_index("patch")
    height, channels, columns = lat.shape
    per_group = channels // GROUPS
    rest = channels - local
    piece = part.shape[0] // (8 * SUB)

    core = lax.rem(p, 2)
    mate = p + 1 - 2 * core
    across = p - 1 + 2 * core
    has_across = jnp.logical_and(across >= 0, across < patches)
    member = lax.rem(p, 8)
    turn_y = 2 - 4 * lax.rem(member // 2, 2)
    turn_z = 4 - 8 * (member // 4)
    friends = (p + turn_y, p + turn_z, p + turn_y + turn_z)

    load_h = pltpu.make_async_copy(heights_in, heights_ref, load_sem.at[0])
    load_lat = pltpu.make_async_copy(latent_ref, lat, load_sem.at[1])
    load_g = pltpu.make_async_copy(gain_ref, gain_v, load_sem.at[2])
    load_s = pltpu.make_async_copy(shift_ref, shift_v, load_sem.at[3])
    load_b = pltpu.make_async_copy(bias_ref, bias_v, load_sem.at[4])
    load_w = pltpu.make_async_copy(weight_ref, weights, load_sem.at[5])
    for load in (load_h, load_lat, load_g, load_s, load_b, load_w):
        load.start()

    barrier = pltpu.get_barrier_semaphore()

    def signal(s, q):
        pl.semaphore_signal(barrier, inc=1, device_id=(s, q), device_id_type=MESH)

    @pl.when(k == 0)
    def _():
        signal(1, p)

        def step(i, carry):
            signal(0, lax.rem(p + i, patches))
            return carry

        lax.fori_loop(1, patches, step, 0)

    partners = [(q, True) for q in (mate, *friends)] + [(across, has_across)]

    def count(higher):
        total = 0
        for q, exists in partners:
            total = total + jnp.logical_and(exists, (q > p) == higher).astype(jnp.int32)
        return total

    @pl.when(k == 1)
    def _():
        for q, exists in partners:
            @pl.when(jnp.logical_and(exists, q > p))
            def _():
                signal(1, q)

        pl.semaphore_wait(barrier, 1 + count(False))
        pl.semaphore_signal(ready, inc=1, device_id=(0, p), device_id_type=MESH)
        for q, exists in partners:
            @pl.when(jnp.logical_and(exists, q < p))
            def _():
                pl.semaphore_signal(greeted, inc=1, device_id=(1, q), device_id_type=MESH)

    def remote(src, dst, ssem, rsem, s, q):
        return pltpu.make_async_remote_copy(
            src_ref=src, dst_ref=dst, send_sem=ssem, recv_sem=rsem,
            device_id=(s, q), device_id_type=MESH,
        )

    def wait_for(ref, sem):
        pltpu.make_async_copy(ref, ref, sem).wait()

    load_h.wait()
    height_own = heights_ref[p]
    window_rows = heights_ref[0]
    for i in range(1, patches):
        window_rows = window_rows + heights_ref[i]
    inv_count = 1.0 / (
        jnp.full((1, 128), window_rows, jnp.int32).astype(jnp.float32)
        * (per_group * columns)
    )

    chan = lax.broadcasted_iota(jnp.int32, (channels, 128), 0)
    first = lax.broadcasted_iota(jnp.int32, (channels, 128), 1) * per_group
    group_mask = jnp.where(
        jnp.logical_and(chan >= first, chan < first + per_group), 1.0, 0.0
    ).astype(jnp.float32)

    def to_groups(per_chan):
        total = jnp.sum(per_chan, axis=1, keepdims=True)
        return jnp.sum(total * group_mask, axis=0, keepdims=True)

    def to_channels(per_group_row):
        return jnp.sum(per_group_row * group_mask, axis=1, keepdims=True)

    def both(sums, squares):
        return to_groups(sums) + pltpu.roll(to_groups(squares), GROUPS, 1)

    load_lat.wait()
    rows = [
        jnp.where(r < height_own, lat[r].astype(jnp.float32), 0.0) for r in range(height)
    ]
    sums, squares, edge = rows[0], rows[0] * rows[0], lat[0]
    for r in range(1, height):
        sums = sums + rows[r]
        squares = squares + rows[r] * rows[r]
        edge = jnp.where(height_own == r + 1, lat[r], edge)
    xin[k, 1] = lat[0]
    xin[k, 2] = edge
    xin[k, 3] = lat[1]
    stat_lat[...] = both(sums, squares)

    def take_params():
        load_g.wait()
        load_s.wait()
        load_b.wait()
        params[0:1] = gain_v[...].astype(jnp.float32)
        params[1:2] = shift_v[...].astype(jnp.float32)
        params[2:4] = bias_v[...].astype(jnp.float32)

    eye = jnp.where(
        lax.broadcasted_iota(jnp.int32, (channels, channels), 0)
        == lax.broadcasted_iota(jnp.int32, (channels, channels), 1),
        1.0,
        0.0,
    ).astype(jnp.bfloat16)

    def spread(row):
        wide = jnp.broadcast_to(row, (128, channels)).astype(jnp.bfloat16)
        return lax.dot_general(
            eye, wide, (((1,), (1,)), ((), ())), preferred_element_type=jnp.float32
        )

    def spread_params(at, source):
        gain_b[at] = spread(source[0:1])
        shift_b[at] = spread(source[1:2])
        for m in range(2):
            bias_b[at, m] = spread(source[2 + m : 3 + m])

    def build(is_rest):
        for b in range(3):
            for a in range(3):
                cols = slice(a * channels, (a + 1) * channels)
                if is_rest:
                    start = 3 * local + b * rest
                    wall[start : start + rest, cols] = weights[b, a, local:]
                else:
                    wall[b * local : (b + 1) * local, cols] = weights[b, a, :local]

    cross_slot, other_slot = 1 + core, 2 - core

    def send_rows():
        for i, slot in enumerate((cross_slot, other_slot, 3)):
            remote(xin.at[k, slot], xin.at[k, slot], row_ss.at[i], row_rs.at[i], 1 - k, p).start()

    def wait_row(i):
        wait_for(lat.at[0], row_rs.at[i])

    def send_edge(kind, ref, m, span, ssem, rsem):
        src_slot = cross_slot if kind == 0 else other_slot
        dst_slot = 4 - 4 * core if kind == 0 else 4 * core
        q = across if kind == 0 else mate

        def go():
            remote(
                ref.at[m, src_slot, span], ref.at[m, dst_slot, span],
                ssem.at[m, kind], rsem.at[m, kind], k, q,
            ).start()

        if kind == 0:
            pl.when(has_across)(go)
        else:
            go()

    def wait_edge(kind, ref, sem, m):
        if kind == 0:
            @pl.when(has_across)
            def _():
                wait_for(ref, sem.at[m, kind])
        else:
            wait_for(ref, sem.at[m, kind])

    whole = pl.ds(0, channels)
    head_part = pl.ds(0, local)
    tail_part = pl.ds(local, rest)

    def pass_in(kind, m):
        send_edge(kind, xin, m, whole, edge_ss, edge_rs)

    def coefficients(total, at):
        mean = total * inv_count
        var = pltpu.roll(mean, 128 - GROUPS, 1) - mean * mean
        inv = lax.rsqrt(jnp.maximum(var, 0.0) + EPS)
        scale = to_channels(inv) * gain_b[at]
        return scale, shift_b[at] - to_channels(mean) * scale

    def fill(rows_of, m, scale, offset, before_edges):
        def activate(values):
            v = values.astype(jnp.float32) * scale + offset
            half = 0.5 * v
            return half + half * jnp.tanh(half)

        def put(j, value):
            value = value.astype(jnp.bfloat16)
            for a in range(3):
                r = j - a
                if 0 <= r < height:
                    at = (m * height + r) * columns
                    ybuf[a * channels : (a + 1) * channels, at : at + columns] = value

        put(1, activate(rows_of[m, 1]))
        tail = activate(rows_of[m, 2])
        mid = activate(rows_of[m, 3])
        before_edges()
        put(0, jnp.where(p > 0, activate(rows_of[m, 0]), 0.0))
        below = jnp.where(p < patches - 1, activate(rows_of[m, 4]), 0.0)
        one, two = height_own == 1, height_own == 2
        put(2, jnp.where(one, below, jnp.where(two, tail, mid)))
        put(3, jnp.where(one, 0.0, jnp.where(two, below, tail)))
        put(4, jnp.where(height_own == 3, below, 0.0))

    lane = lax.broadcasted_iota(jnp.int32, (ROWS_OUT, columns), 1)

    def conv_row(m, r, c0, count, bias):
        at = (m * height + r) * columns
        ls = slice(at, at + columns)

        def block(b):
            start = b * local + c0 if c0 < local else 3 * local + b * rest + c0 - local
            return tbuf[start : start + count, ls]

        return (
            jnp.where(lane > 0, pltpu.roll(block(0), 1, 1), 0.0)
            + block(1)
            + jnp.where(lane < columns - 1, pltpu.roll(block(2), columns - 1, 1), 0.0)
            + bias
        )

    def send_mid(i, m):
        src = (ends.at[m, core], ends.at[m, 1 - core], out_ref.at[m, 1])[i]
        slot = (cross_slot, other_slot, 3)[i]
        remote(
            src.at[tail_part], xmid.at[m, slot, tail_part], mid_ss.at[m, i], mid_rs.at[m, i], 1, p
        ).start()

    def multiply(count, m0, samples):
        cols = slice(m0 * height * columns, (m0 + samples) * height * columns)
        tbuf[:count, cols] = jnp.dot(
            wall[...] if count > 3 * local else part[...],
            ybuf[:, cols],
            preferred_element_type=jnp.float32,
        )

    @pl.when(k == 1)
    def _():
        remote(stat_lat, stat_mate, small_ss.at[1], small_rs.at[1], 0, p).start()
        send_rows()

        @pl.when(count(True) > 0)
        def _():
            pl.semaphore_wait(greeted, count(True))

        pass_in(0, 1)
        pass_in(1, 1)
        take_params()
        spread_params(0, params)
        load_w.wait()
        build(False)
        build(True)

    @pl.when(k == 0)
    def _():
        take_params()
        load_w.wait()
        build(False)
        pl.semaphore_wait(ready, 1)
        remote(params, params_in, small_ss.at[0], small_rs.at[0], 1, p).start()
        for i in range(SUB):
            at = pl.ds((member * SUB + i) * piece, piece)
            remote(wall.at[at], part.at[at], seed_ss.at[i], seed_rs.at[i], 1, p).start()
        send_rows()
        pl.semaphore_wait(barrier, patches - 1)

        def share_stats(m, source):
            def step(i, carry):
                q = lax.rem(p + i, patches)
                remote(
                    source, stat_all.at[m, p], small_ss.at[2 + m], small_rs.at[2 + m], 0, q
                ).start()
                return carry

            lax.fori_loop(1, patches, step, 0)
            stat_all[m, p] = source[...]

        def total_of(m):
            wait_for(stat_all.at[m, pl.ds(0, patches - 1)], small_rs.at[2 + m])
            total = jnp.sum(stat_all[m], axis=0)
            total_out[m] = total
            remote(
                total_out.at[m], total_in.at[m], small_ss.at[4 + m], small_rs.at[4 + m], 1, p
            ).start()
            return total

        share_stats(0, stat_lat)
        pass_in(0, 0)
        pass_in(1, 0)
        spread_params(0, params)
        build(True)
        wait_for(stat_lat, small_rs.at[1])
        share_stats(1, stat_mate)
        wait_row(0)
        pass_in(0, 1)

        total = total_of(0)
        for m in range(2):
            scale, offset = coefficients(total, 0)

            def before_edges():
                if m == 0:
                    wait_row(1)
                    pass_in(1, 1)
                for kind in range(2):
                    wait_edge(kind, lat.at[0], edge_rs, m)

            if m == 1:
                wait_row(2)
            fill(xin, m, scale, offset, before_edges)
            multiply(3 * channels, m, 1)
            for c0 in range(0, channels, ROWS_OUT):
                cs = slice(c0, c0 + ROWS_OUT)
                sums = jnp.zeros((ROWS_OUT, columns), jnp.float32)
                squares = sums
                edge = None
                for r in range(height):
                    z = conv_row(m, r, c0, ROWS_OUT, bias_b[0, m, cs])
                    value = jnp.where(r < height_own, z, 0.0).astype(jnp.bfloat16)
                    out_ref[m, r, cs] = value
                    wide = value.astype(jnp.float32)
                    sums = sums + wide
                    squares = squares + wide * wide
                    edge = value if r == 0 else jnp.where(height_own == r + 1, value, edge)
                    if r == 0:
                        ends[m, 0, cs] = value
                ends[m, 1, cs] = edge
                sum_b[cs] = sums
                sq_b[cs] = squares
            stat_mid[m] = both(sum_b[...], sq_b[...])

            def step(i, carry):
                q = lax.rem(p + i, patches)
                remote(stat_mid.at[m], stat_mid_all.at[m, p], stat_ss.at[m], stat_rs.at[m], 1, q).start()
                return carry

            if m == 1:
                @pl.when(has_across)
                def _():
                    remote(
                        ends.at[1, core, tail_part], xmid.at[1, 4 - 4 * core, tail_part],
                        far_edge_ss.at[1, 0], far_edge_rs.at[1, 0], 1, across,
                    ).start()

            send_mid(0, m)
            lax.fori_loop(0, patches, step, 0)
            if m == 0:
                total = total_of(1)
                send_mid(1, 0)
        send_mid(2, 0)
        send_mid(1, 1)
        send_mid(2, 1)

        wait_for(params, small_ss.at[0])
        for m in range(2):
            wait_for(stat_all.at[m, pl.ds(0, patches - 1)], small_ss.at[2 + m])
            wait_for(total_out.at[m], small_ss.at[4 + m])
        for i in range(SUB):
            wait_for(part.at[pl.ds(0, piece)], seed_ss.at[i])
        wait_edge(0, lat.at[0, tail_part], far_edge_ss, 1)
        for m in range(2):
            wait_for(stat_mid_all.at[m], stat_ss.at[m])
            for i in range(3):
                wait_for(out_ref.at[m, 1, tail_part], mid_ss.at[m, i])

    @pl.when(k == 1)
    def _():
        def to_mate(index, sem):
            at = pl.ds(index * piece, piece)
            remote(part.at[at], part.at[at], core_ss.at[sem], core_rs.at[0], 1, mate).start()

        def seed(i, carry):
            index = member * SUB + i
            at = pl.ds(index * piece, piece)
            wait_for(part.at[pl.ds(0, piece)], seed_rs.at[i])
            for j in range(3):
                remote(
                    part.at[at], part.at[at], share_ss.at[j, i], share_rs.at[j, i], 1, friends[j]
                ).start()
            to_mate(index, i)
            return carry

        lax.fori_loop(0, SUB, seed, 0)
        wait_for(params, small_rs.at[0])
        spread_params(1, params_in)
        wait_row(0)
        pass_in(0, 0)

        def shared(i, carry):
            for j in range(3):
                wait_for(part.at[pl.ds(0, piece)], share_rs.at[j, i])
                to_mate(lax.rem(friends[j], 8) * SUB + i, (1 + j) * SUB + i)
            return carry

        lax.fori_loop(0, SUB, shared, 0)
        wait_row(1)
        pass_in(1, 0)
        wait_row(2)

        def pass_far(kind, m):
            wait_for(out_ref.at[m, 1, tail_part], mid_rs.at[m, kind])
            if kind == 1 or m == 0:
                send_edge(kind, xmid, m, tail_part, far_edge_ss, far_edge_rs)

        for m in range(2):
            if m == 0:
                pass_far(0, 0)
            wait_for(total_out.at[m], small_rs.at[4 + m])
            scale, offset = coefficients(total_in[m], 1)

            def before_edges():
                for kind in range(2):
                    wait_edge(kind, lat.at[0], edge_rs, m)

            fill(xin, m, scale, offset, before_edges)
            if m == 0:
                wait_for(part.at[pl.ds(0, 4 * SUB * piece)], core_rs.at[0])
            multiply(3 * local, m, 1)
            for c0 in range(0, local, ROWS_OUT):
                cs = slice(c0, c0 + ROWS_OUT)
                edge = None
                for r in range(height):
                    value = conv_row(m, r, c0, ROWS_OUT, bias_b[1, m, cs]).astype(jnp.bfloat16)
                    edge = value if r == 0 else jnp.where(height_own == r + 1, value, edge)
                    if r == 0:
                        xmid[m, 1, cs] = value
                    if r == 1:
                        xmid[m, 3, cs] = value
                xmid[m, 2, cs] = edge
            for kind in range(2):
                send_edge(kind, xmid, m, head_part, own_edge_ss, own_edge_rs)
            if m == 0:
                pass_far(1, 0)

        for m in range(2):
            wait_for(stat_mid_all.at[m], stat_rs.at[m])
            scale, offset = coefficients(jnp.sum(stat_mid_all[m], axis=0), 0)
            wait_for(out_ref.at[m, 1, tail_part], mid_rs.at[m, 2])

            def before_edges():
                for kind in range(2):
                    wait_edge(kind, lat.at[0, head_part], own_edge_rs, m)
                    wait_edge(kind, lat.at[0, tail_part], far_edge_rs, m)

            if m == 1:
                pass_far(0, 1)
            fill(xmid, m, scale, offset, before_edges)
            multiply(3 * channels, m, 1)
            if m == 0:
                pass_far(1, 1)
            for c0 in range(0, channels, ROWS_OUT):
                cs = slice(c0, c0 + ROWS_OUT)
                for r in range(height):
                    z = conv_row(m, r, c0, ROWS_OUT, bias_b[0, m, cs])
                    z = xin[m, (1, 3, 2)[r], cs].astype(jnp.float32) + z
                    out_ref[m, r, cs] = jnp.where(r < height_own, z, 0.0).astype(jnp.bfloat16)

        wait_for(stat_lat, small_ss.at[1])
        for i in range(SUB):
            for j in range(3):
                wait_for(part.at[pl.ds(0, piece)], share_ss.at[j, i])
        for i in range(4 * SUB):
            wait_for(part.at[pl.ds(0, piece)], core_ss.at[i])
        for m in range(2):
            for kind in range(2):
                wait_edge(kind, lat.at[0, head_part], own_edge_ss, m)
                if kind == 1 or m == 0:
                    wait_edge(kind, lat.at[0, tail_part], far_edge_ss, m)

    for i in range(3):
        wait_for(lat.at[0], row_ss.at[i])
    for m in range(2):
        for kind in range(2):
            wait_edge(kind, lat.at[0], edge_ss, m)


def paired_call(patches, operands, height, channels, columns):
    bf16, f32 = jnp.bfloat16, jnp.float32
    local = channels * 2 // 5
    hbm = pl.BlockSpec(memory_space=pltpu.HBM)
    dma = pltpu.SemaphoreType.DMA
    return pl.pallas_call(
        functools.partial(paired_kernel, patches, local),
        out_shape=jax.ShapeDtypeStruct((2, height, channels, columns), bf16),
        in_specs=[hbm] * 6,
        out_specs=pl.BlockSpec(memory_space=pltpu.VMEM),
        scratch_shapes=[
            pltpu.VMEM((height, channels, columns), bf16),
            pltpu.VMEM((3, 3, channels, channels), bf16),
            pltpu.VMEM((3 * channels, 3 * channels), bf16),
            pltpu.VMEM((3 * local, 3 * channels), bf16),
            pltpu.VMEM((2, height + 2, channels, columns), bf16),
            pltpu.VMEM((2, height + 2, channels, columns), bf16),
            pltpu.VMEM((2, 2, channels, columns), bf16),
            pltpu.SMEM((patches,), jnp.int32),
            pltpu.VMEM((1, channels), bf16),
            pltpu.VMEM((1, channels), bf16),
            pltpu.VMEM((2, channels), bf16),
            pltpu.VMEM((8, channels), f32),
            pltpu.VMEM((8, channels), f32),
            pltpu.VMEM((1, 128), f32),
            pltpu.VMEM((1, 128), f32),
            pltpu.VMEM((2, patches, 1, 128), f32),
            pltpu.VMEM((2, 1, 128), f32),
            pltpu.VMEM((2, 1, 128), f32),
            pltpu.VMEM((2, 1, 128), f32),
            pltpu.VMEM((2, patches, 1, 128), f32),
            pltpu.VMEM((2, channels, 128), f32),
            pltpu.VMEM((2, channels, 128), f32),
            pltpu.VMEM((2, 2, channels, 128), f32),
            pltpu.VMEM((3 * channels, 2 * height * columns), bf16),
            pltpu.VMEM((3 * channels, 2 * height * columns), f32),
            pltpu.VMEM((channels, columns), f32),
            pltpu.VMEM((channels, columns), f32),
            dma((6,)),
            pltpu.SemaphoreType.REGULAR,
            pltpu.SemaphoreType.REGULAR,
            dma((6,)),
            dma((6,)),
            dma((3,)),
            dma((3,)),
            dma((2, 2)),
            dma((2, 2)),
            dma((SUB,)),
            dma((SUB,)),
            dma((3, SUB)),
            dma((3, SUB)),
            dma((1,)),
            dma((4 * SUB,)),
            dma((2, 3)),
            dma((2, 3)),
            dma((2, 2)),
            dma((2, 2)),
            dma((2, 2)),
            dma((2, 2)),
            dma((2,)),
            dma((2,)),
        ],
        compiler_params=pltpu.CompilerParams(
            collective_id=0, has_side_effects=True, vmem_limit_bytes=48 * 1024 * 1024
        ),
    )(*operands)


def per_device(sections, patches, latent, conv_weight, norm_gain, norm_shift, step_bias, patch_rows):
    latent = jnp.transpose(latent[0], (1, 0, 2))
    weight = jnp.transpose(conv_weight[0], (0, 2, 1, 3))
    height, channels, columns = latent.shape
    bf16, f32 = jnp.bfloat16, jnp.float32
    hbm = pl.BlockSpec(memory_space=pltpu.HBM)
    dma = pltpu.SemaphoreType.DMA
    operands = [
        pltpu.with_memory_space_constraint(array, pltpu.HBM)
        for array in (patch_rows, latent, weight, norm_gain, norm_shift, step_bias[0])
    ]
    if sections == 2 and patches % 8 == 0:
        out = paired_call(patches, operands, height, channels, columns)
        return jnp.transpose(out, (0, 2, 1, 3))[None]
    out = pl.pallas_call(
        functools.partial(kernel, sections, patches),
        out_shape=jax.ShapeDtypeStruct((sections, height, channels, columns), bf16),
        in_specs=[hbm] * 6,
        out_specs=pl.BlockSpec(memory_space=pl.ANY),
        scratch_shapes=[
            pltpu.VMEM((height, channels, columns), bf16),
            pltpu.VMEM((3, 3, channels, channels), bf16),
            pltpu.VMEM((3 * channels, 3 * channels), bf16),
            pltpu.VMEM((sections, height + 2, channels, columns), bf16),
            pltpu.VMEM((sections, height, channels, columns), bf16),
            pltpu.VMEM((sections, height, channels, columns), bf16),
            pltpu.VMEM((channels, columns), bf16),
            pltpu.VMEM((sections, channels, columns), bf16),
            pltpu.SMEM((patches,), jnp.int32),
            pltpu.VMEM((1, channels), bf16),
            pltpu.VMEM((1, channels), bf16),
            pltpu.VMEM((sections, channels), bf16),
            pltpu.VMEM((1, 128), f32),
            pltpu.VMEM((sections, 1, 128), f32),
            pltpu.VMEM((sections, patches, 1, 128), f32),
            pltpu.VMEM((channels, 128), f32),
            pltpu.VMEM((channels, 128), f32),
            pltpu.VMEM((sections, channels, 128), f32),
            pltpu.VMEM((3 * channels, height * columns), bf16),
            pltpu.VMEM((3 * channels, height * columns), f32),
            pltpu.VMEM((channels, columns), f32),
            pltpu.VMEM((channels, columns), f32),
            dma((6,)),
            dma((4,)),
        ]
        + [dma((sections,)) for _ in range(13)],
        compiler_params=pltpu.CompilerParams(
            collective_id=0, has_side_effects=True, vmem_limit_bytes=48 * 1024 * 1024
        ),
    )(*operands)
    return jnp.transpose(out, (0, 2, 1, 3))[None]


def solution(mesh):
    placed = (
        P("section", None, "patch", None),
        P("section", None, None, None, None),
        P("section", None),
        P("section", None),
        P("section", None, None),
        P(),
    )
    return jax.shard_map(
        functools.partial(per_device, mesh.shape["section"], mesh.shape["patch"]),
        mesh=mesh,
        in_specs=placed,
        out_specs=P("section", None, None, "patch", None),
        check_vma=False,
    )
```

```python
import functools

import jax
import jax.numpy as jnp
from jax import lax
from jax.experimental import pallas as pl
from jax.experimental.pallas import tpu as pltpu
from jax.sharding import PartitionSpec as P

GROUPS = 32
EPS = 1e-05
MESH = pl.DeviceIdType.MESH
ROWS_OUT = 64
SUB = 3


def kernel(
    sections,
    patches,
    heights_in,
    latent_ref,
    weight_ref,
    gain_ref,
    shift_ref,
    bias_ref,
    out_ref,
    lat,
    weights,
    wall,
    xbuf,
    skip,
    obuf,
    edge_lat,
    edge_out,
    heights_ref,
    gain_v,
    shift_v,
    bias_v,
    stat_lat,
    stat_out,
    stat_in,
    gain_b,
    shift_b,
    bias_b,
    ybuf,
    tbuf,
    sum_b,
    sq_b,
    local_sem,
    first_sem,
    ends_rs,
    mid_rs,
    up_rs,
    low_rs,
    stat_rs,
    skip_rs,
    ends_ss,
    mid_ss,
    up_ss,
    low_ss,
    stat_ss,
    skip_ss,
    out_sem,
):
    k = lax.axis_index("section")
    p = lax.axis_index("patch")
    height, channels, columns = lat.shape
    per_group = channels // GROUPS
    is_odd = lax.rem(k, 2) == 1
    last = k == sections - 1
    has_far = jnp.logical_and(is_odd, k + 2 < sections)

    load_lat = pltpu.make_async_copy(latent_ref, lat, local_sem.at[0])
    load_w = pltpu.make_async_copy(weight_ref, weights, local_sem.at[1])
    load_h = pltpu.make_async_copy(heights_in, heights_ref, local_sem.at[2])
    load_g = pltpu.make_async_copy(gain_ref, gain_v, local_sem.at[3])
    load_s = pltpu.make_async_copy(shift_ref, shift_v, local_sem.at[4])
    load_b = pltpu.make_async_copy(bias_ref, bias_v, local_sem.at[5])
    load_h.start()
    load_lat.start()
    load_g.start()
    load_s.start()
    load_b.start()
    load_w.start()

    barrier = pltpu.get_barrier_semaphore()

    def signal(s, q):
        pl.semaphore_signal(barrier, inc=1, device_id=(s, q), device_id_type=MESH)

    @pl.when(k == 0)
    def _():
        def step(i, c):
            q = lax.rem(p + i, patches)
            for s in range(sections):
                if s == 0:
                    @pl.when(i > 0)
                    def _():
                        signal(0, q)
                else:
                    signal(s, q)
            return c

        lax.fori_loop(0, patches, step, 0)

    @pl.when(k > 0)
    def _():
        def step(i, c):
            signal(k - 1, lax.rem(p + i, patches))
            return c

        lax.fori_loop(0, patches, step, 0)

        @pl.when(p > 0)
        def _():
            signal(k, p - 1)

        @pl.when(p < patches - 1)
        def _():
            signal(k, p + 1)

    if sections > 2:
        @pl.when(k == 1)
        def _():
            for s in range(2, sections):
                signal(s, p)

        @pl.when(jnp.logical_and(is_odd, k >= 3))
        def _():
            signal(k - 2, p)

    load_h.wait()
    height_own = heights_ref[p]
    window_rows = heights_ref[0]
    for i in range(1, patches):
        window_rows = window_rows + heights_ref[i]
    inv_count = 1.0 / (
        jnp.full((1, 128), window_rows, jnp.int32).astype(jnp.float32)
        * (per_group * columns)
    )

    chan = lax.broadcasted_iota(jnp.int32, (channels, 128), 0)
    first = lax.broadcasted_iota(jnp.int32, (channels, 128), 1) * per_group
    group_mask = jnp.where(
        jnp.logical_and(chan >= first, chan < first + per_group), 1.0, 0.0
    ).astype(jnp.float32)

    def to_groups(per_chan):
        total = jnp.sum(per_chan, axis=1, keepdims=True)
        return jnp.sum(total * group_mask, axis=0, keepdims=True)

    def to_channels(per_group_row):
        return jnp.sum(per_group_row * group_mask, axis=1, keepdims=True)

    def write_stats(ref, sums, squares):
        ref[...] = to_groups(sums) + pltpu.roll(to_groups(squares), GROUPS, 1)

    load_lat.wait()
    rows = [
        jnp.where(r < height_own, lat[r].astype(jnp.float32), 0.0) for r in range(height)
    ]
    sums, squares, edge = rows[0], rows[0] * rows[0], lat[0]
    for r in range(1, height):
        sums = sums + rows[r]
        squares = squares + rows[r] * rows[r]
        edge = jnp.where(height_own == r + 1, lat[r], edge)
    edge_lat[...] = edge
    write_stats(stat_lat, sums, squares)

    sends_to = (
        patches
        - (k == 0).astype(jnp.int32)
        + jnp.where(last, 0, patches)
        + jnp.where(k > 0, (p > 0).astype(jnp.int32) + (p < patches - 1).astype(jnp.int32), 0)
        + (k >= 2).astype(jnp.int32)
        + has_far.astype(jnp.int32)
    )
    pl.semaphore_wait(barrier, sends_to)

    def remote(src, dst, ssem, rsem, s, q):
        return pltpu.make_async_remote_copy(
            src_ref=src, dst_ref=dst, send_sem=ssem, recv_sem=rsem,
            device_id=(s, q), device_id_type=MESH,
        )

    def send_stats(m, s, stat, ssem, own):
        def step(i, c):
            q = lax.rem(p + i, patches)
            remote(stat, stat_in.at[m, p], ssem, stat_rs.at[m], s, q).start()
            return c

        if own is None:
            lax.fori_loop(0, patches, step, 0)
        else:
            lax.fori_loop(1, patches, step, 0)

            @pl.when(own)
            def _():
                pltpu.make_async_copy(stat, stat_in.at[m, p], stat_rs.at[m]).start()

            @pl.when(jnp.logical_not(own))
            def _():
                step(0, 0)

    def send_rows(m, s, head, tail, mid, ssem_ends, ssem_mid):
        remote(head, xbuf.at[m, 1], ssem_ends, ends_rs.at[m], s, p).start()
        remote(tail, xbuf.at[m, 2], ssem_ends, ends_rs.at[m], s, p).start()
        remote(mid, xbuf.at[m, 3], ssem_mid, mid_rs.at[m], s, p).start()

    def pass_on(m, head, tail):
        @pl.when(p < patches - 1)
        def _():
            remote(tail, xbuf.at[m, 0], up_ss.at[m], up_rs.at[m], k, p + 1).start()

        @pl.when(p > 0)
        def _():
            remote(head, xbuf.at[m, 4], low_ss.at[m], low_rs.at[m], k, p - 1).start()

    send_stats(k, 0, stat_lat, first_sem.at[0], k == 0)

    @pl.when(k == 0)
    def _():
        pass_on(0, lat.at[0], edge_lat)
        pltpu.make_async_copy(lat.at[0], xbuf.at[0, 1], ends_rs.at[0]).start()
        pltpu.make_async_copy(edge_lat, xbuf.at[0, 2], ends_rs.at[0]).start()
        pltpu.make_async_copy(lat.at[1], xbuf.at[0, 3], mid_rs.at[0]).start()

    @pl.when(k > 0)
    def _():
        send_rows(k, 0, lat.at[0], edge_lat, lat.at[1], first_sem.at[1], first_sem.at[2])

    @pl.when(k == 1)
    def _():
        pltpu.make_async_copy(lat, skip.at[1], skip_rs.at[1]).start()

    @pl.when(k != 1)
    def _():
        remote(lat, skip.at[k], first_sem.at[3], skip_rs.at[k], 1, p).start()

    eye = jnp.where(
        lax.broadcasted_iota(jnp.int32, (channels, channels), 0)
        == lax.broadcasted_iota(jnp.int32, (channels, channels), 1),
        1.0,
        0.0,
    ).astype(jnp.bfloat16)

    def spread(row):
        wide = jnp.broadcast_to(row.astype(jnp.float32), (128, channels)).astype(jnp.bfloat16)
        return lax.dot_general(
            eye, wide, (((1,), (1,)), ((), ())), preferred_element_type=jnp.float32
        )

    load_g.wait()
    gain_b[...] = spread(gain_v[...])
    load_s.wait()
    shift_b[...] = spread(shift_v[...])
    load_b.wait()
    for m in range(sections):
        bias_b[m] = spread(bias_v[m : m + 1, :])

    load_w.wait()
    for b in range(3):
        for a in range(3):
            wall[b * channels : (b + 1) * channels, a * channels : (a + 1) * channels] = weights[b, a]

    def wait_for(ref, sem):
        pltpu.make_async_copy(ref, ref, sem).wait()

    lane = lax.broadcasted_iota(jnp.int32, (ROWS_OUT, columns), 1)

    def sample(m, carry):
        wait_for(xbuf.at[m, pl.ds(1, 2)], ends_rs.at[m])

        @pl.when(jnp.logical_or(k > 0, m > 0))
        def _():
            pass_on(m, xbuf.at[m, 1], xbuf.at[m, 2])

        wait_for(stat_in.at[m], stat_rs.at[m])
        total = jnp.sum(stat_in[m], axis=0)
        mean = total * inv_count
        var = pltpu.roll(mean, 128 - GROUPS, 1) - mean * mean
        inv = lax.rsqrt(jnp.maximum(var, 0.0) + EPS)
        scale = to_channels(inv) * gain_b[...]
        offset = shift_b[...] - to_channels(mean) * scale

        def activate(values):
            v = values.astype(jnp.float32) * scale + offset
            half = 0.5 * v
            return half + half * jnp.tanh(half)

        def put(j, value):
            value = value.astype(jnp.bfloat16)
            for a in range(3):
                r = j - a
                if 0 <= r < height:
                    ybuf[a * channels : (a + 1) * channels, r * columns : (r + 1) * columns] = value

        put(1, activate(xbuf[m, 1]))
        tail = activate(xbuf[m, 2])
        wait_for(xbuf.at[m, 3], mid_rs.at[m])
        mid = activate(xbuf[m, 3])

        @pl.when(p > 0)
        def _():
            wait_for(xbuf.at[m, 0], up_rs.at[m])

        @pl.when(p < patches - 1)
        def _():
            wait_for(xbuf.at[m, 4], low_rs.at[m])

        put(0, jnp.where(p > 0, activate(xbuf[m, 0]), 0.0))
        below = jnp.where(p < patches - 1, activate(xbuf[m, 4]), 0.0)
        one, two = height_own == 1, height_own == 2
        put(2, jnp.where(one, below, jnp.where(two, tail, mid)))
        put(3, jnp.where(one, 0.0, jnp.where(two, below, tail)))
        put(4, jnp.where(height_own == 3, below, 0.0))

        tbuf[...] = jnp.dot(wall[...], ybuf[...], preferred_element_type=jnp.float32)

        @pl.when(is_odd)
        def _():
            wait_for(skip.at[m], skip_rs.at[m])

        for c0 in range(0, channels, ROWS_OUT):
            cs = slice(c0, c0 + ROWS_OUT)
            sums = jnp.zeros((ROWS_OUT, columns), jnp.float32)
            squares = sums
            edge = None
            for r in range(height):
                ls = slice(r * columns, (r + 1) * columns)
                left = pltpu.roll(tbuf[c0 : c0 + ROWS_OUT, ls], 1, 1)
                mid = tbuf[channels + c0 : channels + c0 + ROWS_OUT, ls]
                right = pltpu.roll(
                    tbuf[2 * channels + c0 : 2 * channels + c0 + ROWS_OUT, ls], columns - 1, 1
                )
                z = (
                    jnp.where(lane > 0, left, 0.0)
                    + mid
                    + jnp.where(lane < columns - 1, right, 0.0)
                    + bias_b[m, cs]
                )
                z = jnp.where(is_odd, skip[m, r, cs].astype(jnp.float32) + z, z)
                value = jnp.where(r < height_own, z, 0.0).astype(jnp.bfloat16)
                obuf[m, r, cs] = value
                wide = value.astype(jnp.float32)
                sums = sums + wide
                squares = squares + wide * wide
                edge = value if r == 0 else jnp.where(height_own == r + 1, value, edge)
            edge_out[m, cs] = edge
            sum_b[cs] = sums
            sq_b[cs] = squares

        @pl.when(jnp.logical_not(last))
        def _():
            send_rows(
                m, k + 1, obuf.at[m, 0], edge_out.at[m], obuf.at[m, 1], ends_ss.at[m], mid_ss.at[m]
            )
            write_stats(stat_out.at[m], sum_b[...], sq_b[...])
            send_stats(m, k + 1, stat_out.at[m], stat_ss.at[m], None)

        if sections > 2:
            @pl.when(has_far)
            def _():
                remote(obuf.at[m], skip.at[m], skip_ss.at[m], skip_rs.at[m], k + 2, p).start()

        pltpu.make_async_copy(obuf.at[m], out_ref.at[m], out_sem.at[m]).start()
        return carry

    lax.fori_loop(0, sections, sample, 0)

    wait_for(stat_in.at[0, pl.ds(1, patches - 1)], first_sem.at[0])

    @pl.when(k > 0)
    def _():
        wait_for(stat_lat, first_sem.at[0])
        wait_for(xbuf.at[0, pl.ds(0, 2)], first_sem.at[1])
        wait_for(edge_lat, first_sem.at[2])

    @pl.when(k != 1)
    def _():
        wait_for(lat, first_sem.at[3])

    def drain(m, carry):
        @pl.when(p < patches - 1)
        def _():
            wait_for(edge_lat, up_ss.at[m])

        @pl.when(p > 0)
        def _():
            wait_for(edge_lat, low_ss.at[m])

        @pl.when(jnp.logical_not(last))
        def _():
            wait_for(xbuf.at[m, pl.ds(0, 2)], ends_ss.at[m])
            wait_for(edge_lat, mid_ss.at[m])
            wait_for(stat_in.at[m], stat_ss.at[m])

        if sections > 2:
            @pl.when(has_far)
            def _():
                wait_for(obuf.at[m], skip_ss.at[m])

        wait_for(obuf.at[m], out_sem.at[m])
        return carry

    lax.fori_loop(0, sections, drain, 0)


def paired_kernel(
    patches,
    local,
    heights_in,
    latent_ref,
    weight_ref,
    gain_ref,
    shift_ref,
    bias_ref,
    out_ref,
    lat,
    weights,
    wall,
    part,
    xin,
    xmid,
    ends,
    heights_ref,
    gain_v,
    shift_v,
    bias_v,
    params,
    params_in,
    stat_lat,
    stat_mate,
    stat_all,
    total_out,
    total_in,
    stat_mid,
    stat_mid_all,
    gain_b,
    shift_b,
    bias_b,
    ybuf,
    tbuf,
    sum_b,
    sq_b,
    load_sem,
    ready,
    greeted,
    small_rs,
    small_ss,
    row_rs,
    row_ss,
    edge_rs,
    edge_ss,
    seed_rs,
    seed_ss,
    share_rs,
    share_ss,
    core_rs,
    core_ss,
    mid_rs,
    mid_ss,
    own_edge_rs,
    own_edge_ss,
    far_edge_rs,
    far_edge_ss,
    late_rs,
    late_ss,
    late_edge_rs,
    late_edge_ss,
    stat_rs,
    stat_ss,
):
    k = lax.axis_index("section")
    p = lax.axis_index("patch")
    height, channels, columns = lat.shape
    per_group = channels // GROUPS
    rest = channels - local
    lead = channels * 4 // 5
    lag = channels - lead
    piece = part.shape[0] // (8 * SUB)

    core = lax.rem(p, 2)
    mate = p + 1 - 2 * core
    across = p - 1 + 2 * core
    has_across = jnp.logical_and(across >= 0, across < patches)
    member = lax.rem(p, 8)
    turn_y = 2 - 4 * lax.rem(member // 2, 2)
    turn_z = 4 - 8 * (member // 4)
    friends = (p + turn_y, p + turn_z, p + turn_y + turn_z)

    load_h = pltpu.make_async_copy(heights_in, heights_ref, load_sem.at[0])
    load_lat = pltpu.make_async_copy(latent_ref, lat, load_sem.at[1])
    load_g = pltpu.make_async_copy(gain_ref, gain_v, load_sem.at[2])
    load_s = pltpu.make_async_copy(shift_ref, shift_v, load_sem.at[3])
    load_b = pltpu.make_async_copy(bias_ref, bias_v, load_sem.at[4])
    load_w = [
        pltpu.make_async_copy(
            weight_ref.at[:, :, span], weights.at[:, :, span], load_sem.at[5 + i]
        )
        for i, span in enumerate((pl.ds(0, local), pl.ds(local, rest)))
    ]
    for load in (load_h, load_lat, load_w[0], load_g, load_s, load_b, load_w[1]):
        load.start()

    barrier = pltpu.get_barrier_semaphore()

    def signal(s, q):
        pl.semaphore_signal(barrier, inc=1, device_id=(s, q), device_id_type=MESH)

    @pl.when(k == 0)
    def _():
        signal(1, p)

        def step(i, carry):
            signal(0, lax.rem(p + i, patches))
            return carry

        lax.fori_loop(1, patches, step, 0)

    partners = [(q, True) for q in (mate, *friends)] + [(across, has_across)]

    def count(higher):
        total = 0
        for q, exists in partners:
            total = total + jnp.logical_and(exists, (q > p) == higher).astype(jnp.int32)
        return total

    @pl.when(k == 1)
    def _():
        for q, exists in partners:
            @pl.when(jnp.logical_and(exists, q > p))
            def _():
                signal(1, q)

        pl.semaphore_wait(barrier, 1 + count(False))
        pl.semaphore_signal(ready, inc=1, device_id=(0, p), device_id_type=MESH)
        for q, exists in partners:
            @pl.when(jnp.logical_and(exists, q < p))
            def _():
                pl.semaphore_signal(greeted, inc=1, device_id=(1, q), device_id_type=MESH)

    def remote(src, dst, ssem, rsem, s, q):
        return pltpu.make_async_remote_copy(
            src_ref=src, dst_ref=dst, send_sem=ssem, recv_sem=rsem,
            device_id=(s, q), device_id_type=MESH,
        )

    def wait_for(ref, sem):
        pltpu.make_async_copy(ref, ref, sem).wait()

    load_h.wait()
    height_own = heights_ref[p]
    window_rows = heights_ref[0]
    for i in range(1, patches):
        window_rows = window_rows + heights_ref[i]
    inv_count = 1.0 / (
        jnp.full((1, 128), window_rows, jnp.int32).astype(jnp.float32)
        * (per_group * columns)
    )

    chan = lax.broadcasted_iota(jnp.int32, (channels, 128), 0)
    first = lax.broadcasted_iota(jnp.int32, (channels, 128), 1) * per_group
    group_mask = jnp.where(
        jnp.logical_and(chan >= first, chan < first + per_group), 1.0, 0.0
    ).astype(jnp.float32)

    def to_groups(per_chan):
        total = jnp.sum(per_chan, axis=1, keepdims=True)
        return jnp.sum(total * group_mask, axis=0, keepdims=True)

    def to_channels(per_group_row):
        return jnp.sum(per_group_row * group_mask, axis=1, keepdims=True)

    def both(sums, squares):
        return to_groups(sums) + pltpu.roll(to_groups(squares), GROUPS, 1)

    load_lat.wait()
    rows = [
        jnp.where(r < height_own, lat[r].astype(jnp.float32), 0.0) for r in range(height)
    ]
    sums, squares, edge = rows[0], rows[0] * rows[0], lat[0]
    for r in range(1, height):
        sums = sums + rows[r]
        squares = squares + rows[r] * rows[r]
        edge = jnp.where(height_own == r + 1, lat[r], edge)
    xin[k, 1] = lat[0]
    xin[k, 2] = edge
    xin[k, 3] = lat[1]
    stat_lat[...] = both(sums, squares)

    def take_params():
        load_g.wait()
        load_s.wait()
        load_b.wait()
        params[0:1] = gain_v[...].astype(jnp.float32)
        params[1:2] = shift_v[...].astype(jnp.float32)
        params[2:4] = bias_v[...].astype(jnp.float32)

    eye = jnp.where(
        lax.broadcasted_iota(jnp.int32, (channels, channels), 0)
        == lax.broadcasted_iota(jnp.int32, (channels, channels), 1),
        1.0,
        0.0,
    ).astype(jnp.bfloat16)

    def spread(row):
        wide = jnp.broadcast_to(row, (128, channels)).astype(jnp.bfloat16)
        return lax.dot_general(
            eye, wide, (((1,), (1,)), ((), ())), preferred_element_type=jnp.float32
        )

    def spread_params(at, source):
        gain_b[at] = spread(source[0:1])
        shift_b[at] = spread(source[1:2])
        for m in range(2):
            bias_b[at, m] = spread(source[2 + m : 3 + m])

    def depth(a, c):
        return a * lead + c if c < lead else 3 * lead + a * lag + c - lead

    def build(is_rest):
        for b in range(3):
            for a in range(3):
                for lo, hi in ((0, lead), (lead, channels)):
                    at = depth(a, lo)
                    cols = slice(at, at + hi - lo)
                    if is_rest:
                        start = 3 * local + b * rest
                        wall[start : start + rest, cols] = weights[b, a, local:, lo:hi]
                    else:
                        wall[b * local : (b + 1) * local, cols] = weights[b, a, :local, lo:hi]

    cross_slot, other_slot = 1 + core, 2 - core

    def send_rows():
        for i, slot in enumerate((cross_slot, other_slot, 3)):
            remote(xin.at[k, slot], xin.at[k, slot], row_ss.at[i], row_rs.at[i], 1 - k, p).start()

    def wait_row(i):
        wait_for(lat.at[0], row_rs.at[i])

    def send_edge(kind, ref, m, span, ssem, rsem):
        src_slot = cross_slot if kind == 0 else other_slot
        dst_slot = 4 - 4 * core if kind == 0 else 4 * core
        q = across if kind == 0 else mate

        def go():
            remote(
                ref.at[m, src_slot, span], ref.at[m, dst_slot, span],
                ssem.at[m, kind], rsem.at[m, kind], k, q,
            ).start()

        if kind == 0:
            pl.when(has_across)(go)
        else:
            go()

    def wait_edge(kind, ref, sem, m):
        if kind == 0:
            @pl.when(has_across)
            def _():
                wait_for(ref, sem.at[m, kind])
        else:
            wait_for(ref, sem.at[m, kind])

    whole = pl.ds(0, channels)
    head_part = pl.ds(0, local)
    tail_part = pl.ds(local, rest)
    early_part = pl.ds(local, lead - local)
    late_part = pl.ds(lead, lag)

    def pass_in(kind, m):
        send_edge(kind, xin, m, whole, edge_ss, edge_rs)

    def coefficients(total, at):
        mean = total * inv_count
        var = pltpu.roll(mean, 128 - GROUPS, 1) - mean * mean
        inv = lax.rsqrt(jnp.maximum(var, 0.0) + EPS)
        scale = to_channels(inv) * gain_b[at]
        return scale, shift_b[at] - to_channels(mean) * scale

    def fill(rows_of, m, scale, offset, before_edges, low=0, high=channels):
        def activate(slot):
            v = rows_of[m, slot, low:high].astype(jnp.float32) * scale[low:high] + offset[low:high]
            half = 0.5 * v
            return half + half * jnp.tanh(half)

        def put(j, value):
            value = value.astype(jnp.bfloat16)
            for a in range(3):
                r = j - a
                if 0 <= r < height:
                    at = (m * height + r) * columns
                    for lo, hi in ((low, min(high, lead)), (max(low, lead), high)):
                        if lo < hi:
                            start = depth(a, lo)
                            ybuf[start : start + hi - lo, at : at + columns] = value[lo - low : hi - low]

        put(1, activate(1))
        tail = activate(2)
        mid = activate(3)
        before_edges()
        put(0, jnp.where(p > 0, activate(0), 0.0))
        below = jnp.where(p < patches - 1, activate(4), 0.0)
        one, two = height_own == 1, height_own == 2
        put(2, jnp.where(one, below, jnp.where(two, tail, mid)))
        put(3, jnp.where(one, 0.0, jnp.where(two, below, tail)))
        put(4, jnp.where(height_own == 3, below, 0.0))

    lane = lax.broadcasted_iota(jnp.int32, (ROWS_OUT, columns), 1)

    def conv_row(m, r, c0, count, bias):
        at = (m * height + r) * columns
        ls = slice(at, at + columns)

        def block(b):
            start = b * local + c0 if c0 < local else 3 * local + b * rest + c0 - local
            return tbuf[start : start + count, ls]

        return (
            jnp.where(lane > 0, pltpu.roll(block(0), 1, 1), 0.0)
            + block(1)
            + jnp.where(lane < columns - 1, pltpu.roll(block(2), columns - 1, 1), 0.0)
            + bias
        )

    def far(m, is_late):
        if m == 0:
            return tail_part, mid_ss.at[0], mid_rs.at[0], far_edge_ss.at[0], far_edge_rs.at[0]
        if is_late:
            return late_part, late_ss, late_rs, late_edge_ss, late_edge_rs
        return early_part, mid_ss.at[1], mid_rs.at[1], far_edge_ss.at[1], far_edge_rs.at[1]

    def send_mid(i, m, is_late=False):
        span, ssem, rsem, _, _ = far(m, is_late)
        src = (ends.at[m, core], ends.at[m, 1 - core], out_ref.at[m, 1])[i]
        slot = (cross_slot, other_slot, 3)[i]
        remote(src.at[span], xmid.at[m, slot, span], ssem.at[i], rsem.at[i], 1, p).start()

    def send_across(is_late):
        span, _, _, ssem, rsem = far(1, is_late)

        @pl.when(has_across)
        def _():
            remote(
                ends.at[1, core, span], xmid.at[1, 4 - 4 * core, span],
                ssem.at[0], rsem.at[0], 1, across,
            ).start()

    def wait_far(i, m, is_late=False):
        span, _, rsem, _, _ = far(m, is_late)
        wait_for(out_ref.at[m, 1, span], rsem.at[i])

    def wait_far_edges(m, is_late=False):
        span, _, _, _, rsem = far(m, is_late)

        @pl.when(has_across)
        def _():
            wait_for(lat.at[0, span], rsem.at[0])

        wait_for(lat.at[0, span], rsem.at[1])

    def pass_far(kind, m, is_late=False):
        span, _, _, ssem, rsem = far(m, is_late)
        wait_far(kind, m, is_late)
        src_slot = cross_slot if kind == 0 else other_slot
        dst_slot = 4 - 4 * core if kind == 0 else 4 * core
        q = across if kind == 0 else mate

        def go():
            remote(
                xmid.at[m, src_slot, span], xmid.at[m, dst_slot, span],
                ssem.at[kind], rsem.at[kind], 1, q,
            ).start()

        if kind == 0:
            pl.when(has_across)(go)
        else:
            go()

    def multiply(count, m0, samples, low=0, high=3 * channels):
        cols = slice(m0 * height * columns, (m0 + samples) * height * columns)
        left = wall if count > 3 * local else part
        product = jnp.dot(
            left[:, low:high], ybuf[low:high, cols], preferred_element_type=jnp.float32
        )
        tbuf[:count, cols] = product if low == 0 else tbuf[:count, cols] + product

    @pl.when(k == 1)
    def _():
        remote(stat_lat, stat_mate, small_ss.at[1], small_rs.at[1], 0, p).start()
        send_rows()

        @pl.when(count(True) > 0)
        def _():
            pl.semaphore_wait(greeted, count(True))

        pass_in(0, 1)
        pass_in(1, 1)
        take_params()
        spread_params(0, params)
        load_w[0].wait()
        build(False)
        load_w[1].wait()
        build(True)

    @pl.when(k == 0)
    def _():
        take_params()
        load_w[0].wait()
        build(False)
        pl.semaphore_wait(ready, 1)
        remote(params, params_in, small_ss.at[0], small_rs.at[0], 1, p).start()
        for i in range(SUB):
            at = pl.ds((member * SUB + i) * piece, piece)
            remote(wall.at[at], part.at[at], seed_ss.at[i], seed_rs.at[i], 1, p).start()
        send_rows()
        pl.semaphore_wait(barrier, patches - 1)

        def share_stats(m, source):
            def step(i, carry):
                q = lax.rem(p + i, patches)
                remote(
                    source, stat_all.at[m, p], small_ss.at[2 + m], small_rs.at[2 + m], 0, q
                ).start()
                return carry

            lax.fori_loop(1, patches, step, 0)
            stat_all[m, p] = source[...]

        def total_of(m):
            wait_for(stat_all.at[m, pl.ds(0, patches - 1)], small_rs.at[2 + m])
            total = jnp.sum(stat_all[m], axis=0)
            total_out[m] = total
            remote(
                total_out.at[m], total_in.at[m], small_ss.at[4 + m], small_rs.at[4 + m], 1, p
            ).start()
            return total

        share_stats(0, stat_lat)
        pass_in(0, 0)
        pass_in(1, 0)
        spread_params(0, params)
        load_w[1].wait()
        build(True)
        wait_for(stat_lat, small_rs.at[1])
        share_stats(1, stat_mate)
        wait_row(0)
        pass_in(0, 1)

        total = total_of(0)
        for m in range(2):
            scale, offset = coefficients(total, 0)

            def before_edges():
                if m == 0:
                    wait_row(1)
                    pass_in(1, 1)
                for kind in range(2):
                    wait_edge(kind, lat.at[0], edge_rs, m)

            if m == 1:
                wait_row(2)
            fill(xin, m, scale, offset, before_edges)
            multiply(3 * channels, m, 1)
            for c0 in range(0, channels, ROWS_OUT):
                cs = slice(c0, c0 + ROWS_OUT)
                sums = jnp.zeros((ROWS_OUT, columns), jnp.float32)
                squares = sums
                edge = None
                for r in range(height):
                    z = conv_row(m, r, c0, ROWS_OUT, bias_b[0, m, cs])
                    value = jnp.where(r < height_own, z, 0.0).astype(jnp.bfloat16)
                    out_ref[m, r, cs] = value
                    wide = value.astype(jnp.float32)
                    sums = sums + wide
                    squares = squares + wide * wide
                    edge = value if r == 0 else jnp.where(height_own == r + 1, value, edge)
                    if r == 0:
                        ends[m, 0, cs] = value
                ends[m, 1, cs] = edge
                sum_b[cs] = sums
                sq_b[cs] = squares
            stat_mid[m] = both(sum_b[...], sq_b[...])

            def step(i, carry):
                q = lax.rem(p + i, patches)
                remote(stat_mid.at[m], stat_mid_all.at[m, p], stat_ss.at[m], stat_rs.at[m], 1, q).start()
                return carry

            if m == 0:
                send_mid(0, m)
            lax.fori_loop(0, patches, step, 0)
            if m == 1:
                send_across(False)
                send_mid(0, m)
            if m == 0:
                total = total_of(1)
                send_mid(1, 0)
        send_mid(2, 0)
        send_mid(1, 1)
        send_mid(2, 1)
        send_mid(1, 1, True)
        send_across(True)
        send_mid(0, 1, True)
        send_mid(2, 1, True)

        wait_for(params, small_ss.at[0])
        for m in range(2):
            wait_for(stat_all.at[m, pl.ds(0, patches - 1)], small_ss.at[2 + m])
            wait_for(total_out.at[m], small_ss.at[4 + m])
        for i in range(SUB):
            wait_for(part.at[pl.ds(0, piece)], seed_ss.at[i])
        for m, is_late in ((0, False), (1, False), (1, True)):
            span, ssem, _, edge_sem, _ = far(m, is_late)
            for i in range(3):
                wait_for(out_ref.at[m, 1, span], ssem.at[i])
            if m == 1:
                @pl.when(has_across)
                def _():
                    wait_for(lat.at[0, span], edge_sem.at[0])
        for m in range(2):
            wait_for(stat_mid_all.at[m], stat_ss.at[m])

    @pl.when(k == 1)
    def _():
        def to_mate(index, sem):
            at = pl.ds(index * piece, piece)
            remote(part.at[at], part.at[at], core_ss.at[sem], core_rs.at[0], 1, mate).start()

        def seed(i, carry):
            index = member * SUB + i
            at = pl.ds(index * piece, piece)
            wait_for(part.at[pl.ds(0, piece)], seed_rs.at[i])
            for j in range(3):
                remote(
                    part.at[at], part.at[at], share_ss.at[j, i], share_rs.at[j, i], 1, friends[j]
                ).start()
            to_mate(index, i)
            return carry

        lax.fori_loop(0, SUB, seed, 0)
        wait_for(params, small_rs.at[0])
        spread_params(1, params_in)
        wait_row(0)
        pass_in(0, 0)

        def shared(i, carry):
            for j in range(3):
                wait_for(part.at[pl.ds(0, piece)], share_rs.at[j, i])
                to_mate(lax.rem(friends[j], 8) * SUB + i, (1 + j) * SUB + i)
            return carry

        lax.fori_loop(0, SUB, shared, 0)
        wait_row(1)
        pass_in(1, 0)
        wait_row(2)

        for m in range(2):
            if m == 0:
                pass_far(0, 0)
            wait_for(total_out.at[m], small_rs.at[4 + m])
            scale, offset = coefficients(total_in[m], 1)

            def before_edges():
                for kind in range(2):
                    wait_edge(kind, lat.at[0], edge_rs, m)

            fill(xin, m, scale, offset, before_edges)
            if m == 0:
                wait_for(part.at[pl.ds(0, 4 * SUB * piece)], core_rs.at[0])
            multiply(3 * local, m, 1)
            for c0 in range(0, local, ROWS_OUT):
                cs = slice(c0, c0 + ROWS_OUT)
                edge = None
                for r in range(height):
                    value = conv_row(m, r, c0, ROWS_OUT, bias_b[1, m, cs]).astype(jnp.bfloat16)
                    edge = value if r == 0 else jnp.where(height_own == r + 1, value, edge)
                    if r == 0:
                        xmid[m, 1, cs] = value
                    if r == 1:
                        xmid[m, 3, cs] = value
                xmid[m, 2, cs] = edge
            for kind in range(2):
                send_edge(kind, xmid, m, head_part, own_edge_ss, own_edge_rs)
            if m == 0:
                pass_far(1, 0)

        for m in range(2):
            wait_for(stat_mid_all.at[m], stat_rs.at[m])
            scale, offset = coefficients(jnp.sum(stat_mid_all[m], axis=0), 0)

            def before_edges():
                if m == 0:
                    pass_far(1, 1)
                for kind in range(2):
                    wait_edge(kind, lat.at[0, head_part], own_edge_rs, m)
                wait_far_edges(m)

            wait_far(2, m)
            if m == 0:
                fill(xmid, 0, scale, offset, before_edges)
                multiply(3 * channels, 0, 1)
                pass_far(1, 1, True)
            else:
                wait_far(0, 1)
                fill(xmid, 1, scale, offset, before_edges, 0, lead)
                multiply(3 * channels, 1, 1, 0, 3 * lead)
                wait_far(0, 1, True)
                wait_far(2, 1, True)
                fill(xmid, 1, scale, offset, lambda: wait_far_edges(1, True), lead, channels)
                multiply(3 * channels, 1, 1, 3 * lead, 3 * channels)
            for c0 in range(0, channels, ROWS_OUT):
                cs = slice(c0, c0 + ROWS_OUT)
                for r in range(height):
                    z = conv_row(m, r, c0, ROWS_OUT, bias_b[0, m, cs])
                    z = xin[m, (1, 3, 2)[r], cs].astype(jnp.float32) + z
                    out_ref[m, r, cs] = jnp.where(r < height_own, z, 0.0).astype(jnp.bfloat16)

        wait_for(stat_lat, small_ss.at[1])
        for i in range(SUB):
            for j in range(3):
                wait_for(part.at[pl.ds(0, piece)], share_ss.at[j, i])
        for i in range(4 * SUB):
            wait_for(part.at[pl.ds(0, piece)], core_ss.at[i])
        for m in range(2):
            for kind in range(2):
                wait_edge(kind, lat.at[0, head_part], own_edge_ss, m)
        wait_edge(0, lat.at[0, tail_part], far_edge_ss, 0)
        for m, is_late in ((0, False), (1, False), (1, True)):
            span, _, _, sem, _ = far(m, is_late)
            wait_for(lat.at[0, span], sem.at[1])

    for i in range(3):
        wait_for(lat.at[0], row_ss.at[i])
    for m in range(2):
        for kind in range(2):
            wait_edge(kind, lat.at[0], edge_ss, m)


def paired_call(patches, operands, height, channels, columns):
    bf16, f32 = jnp.bfloat16, jnp.float32
    local = channels * 2 // 5
    hbm = pl.BlockSpec(memory_space=pltpu.HBM)
    dma = pltpu.SemaphoreType.DMA
    return pl.pallas_call(
        functools.partial(paired_kernel, patches, local),
        out_shape=jax.ShapeDtypeStruct((2, height, channels, columns), bf16),
        in_specs=[hbm] * 6,
        out_specs=pl.BlockSpec(memory_space=pltpu.VMEM),
        scratch_shapes=[
            pltpu.VMEM((height, channels, columns), bf16),
            pltpu.VMEM((3, 3, channels, channels), bf16),
            pltpu.VMEM((3 * channels, 3 * channels), bf16),
            pltpu.VMEM((3 * local, 3 * channels), bf16),
            pltpu.VMEM((2, height + 2, channels, columns), bf16),
            pltpu.VMEM((2, height + 2, channels, columns), bf16),
            pltpu.VMEM((2, 2, channels, columns), bf16),
            pltpu.SMEM((patches,), jnp.int32),
            pltpu.VMEM((1, channels), bf16),
            pltpu.VMEM((1, channels), bf16),
            pltpu.VMEM((2, channels), bf16),
            pltpu.VMEM((8, channels), f32),
            pltpu.VMEM((8, channels), f32),
            pltpu.VMEM((1, 128), f32),
            pltpu.VMEM((1, 128), f32),
            pltpu.VMEM((2, patches, 1, 128), f32),
            pltpu.VMEM((2, 1, 128), f32),
            pltpu.VMEM((2, 1, 128), f32),
            pltpu.VMEM((2, 1, 128), f32),
            pltpu.VMEM((2, patches, 1, 128), f32),
            pltpu.VMEM((2, channels, 128), f32),
            pltpu.VMEM((2, channels, 128), f32),
            pltpu.VMEM((2, 2, channels, 128), f32),
            pltpu.VMEM((3 * channels, 2 * height * columns), bf16),
            pltpu.VMEM((3 * channels, 2 * height * columns), f32),
            pltpu.VMEM((channels, columns), f32),
            pltpu.VMEM((channels, columns), f32),
            dma((7,)),
            pltpu.SemaphoreType.REGULAR,
            pltpu.SemaphoreType.REGULAR,
            dma((6,)),
            dma((6,)),
            dma((3,)),
            dma((3,)),
            dma((2, 2)),
            dma((2, 2)),
            dma((SUB,)),
            dma((SUB,)),
            dma((3, SUB)),
            dma((3, SUB)),
            dma((1,)),
            dma((4 * SUB,)),
            dma((2, 3)),
            dma((2, 3)),
            dma((2, 2)),
            dma((2, 2)),
            dma((2, 2)),
            dma((2, 2)),
            dma((3,)),
            dma((3,)),
            dma((2,)),
            dma((2,)),
            dma((2,)),
            dma((2,)),
        ],
        compiler_params=pltpu.CompilerParams(
            collective_id=0, has_side_effects=True, vmem_limit_bytes=48 * 1024 * 1024
        ),
    )(*operands)


def per_device(sections, patches, latent, conv_weight, norm_gain, norm_shift, step_bias, patch_rows):
    latent = jnp.transpose(latent[0], (1, 0, 2))
    weight = jnp.transpose(conv_weight[0], (0, 2, 1, 3))
    height, channels, columns = latent.shape
    bf16, f32 = jnp.bfloat16, jnp.float32
    hbm = pl.BlockSpec(memory_space=pltpu.HBM)
    dma = pltpu.SemaphoreType.DMA
    operands = [
        pltpu.with_memory_space_constraint(array, pltpu.HBM)
        for array in (patch_rows, latent, weight, norm_gain, norm_shift, step_bias[0])
    ]
    if sections == 2 and patches % 8 == 0:
        out = paired_call(patches, operands, height, channels, columns)
        return jnp.transpose(out, (0, 2, 1, 3))[None]
    out = pl.pallas_call(
        functools.partial(kernel, sections, patches),
        out_shape=jax.ShapeDtypeStruct((sections, height, channels, columns), bf16),
        in_specs=[hbm] * 6,
        out_specs=pl.BlockSpec(memory_space=pl.ANY),
        scratch_shapes=[
            pltpu.VMEM((height, channels, columns), bf16),
            pltpu.VMEM((3, 3, channels, channels), bf16),
            pltpu.VMEM((3 * channels, 3 * channels), bf16),
            pltpu.VMEM((sections, height + 2, channels, columns), bf16),
            pltpu.VMEM((sections, height, channels, columns), bf16),
            pltpu.VMEM((sections, height, channels, columns), bf16),
            pltpu.VMEM((channels, columns), bf16),
            pltpu.VMEM((sections, channels, columns), bf16),
            pltpu.SMEM((patches,), jnp.int32),
            pltpu.VMEM((1, channels), bf16),
            pltpu.VMEM((1, channels), bf16),
            pltpu.VMEM((sections, channels), bf16),
            pltpu.VMEM((1, 128), f32),
            pltpu.VMEM((sections, 1, 128), f32),
            pltpu.VMEM((sections, patches, 1, 128), f32),
            pltpu.VMEM((channels, 128), f32),
            pltpu.VMEM((channels, 128), f32),
            pltpu.VMEM((sections, channels, 128), f32),
            pltpu.VMEM((3 * channels, height * columns), bf16),
            pltpu.VMEM((3 * channels, height * columns), f32),
            pltpu.VMEM((channels, columns), f32),
            pltpu.VMEM((channels, columns), f32),
            dma((6,)),
            dma((4,)),
        ]
        + [dma((sections,)) for _ in range(13)],
        compiler_params=pltpu.CompilerParams(
            collective_id=0, has_side_effects=True, vmem_limit_bytes=48 * 1024 * 1024
        ),
    )(*operands)
    return jnp.transpose(out, (0, 2, 1, 3))[None]


def solution(mesh):
    placed = (
        P("section", None, "patch", None),
        P("section", None, None, None, None),
        P("section", None),
        P("section", None),
        P("section", None, None),
        P(),
    )
    return jax.shard_map(
        functools.partial(per_device, mesh.shape["section"], mesh.shape["patch"]),
        mesh=mesh,
        in_specs=placed,
        out_specs=P("section", None, None, "patch", None),
        check_vma=False,
    )
```

```python
import functools

import jax
import jax.numpy as jnp
from jax import lax
from jax.experimental import pallas as pl
from jax.experimental.pallas import tpu as pltpu
from jax.sharding import PartitionSpec as P

GROUPS = 32
EPS = 1e-05
MESH = pl.DeviceIdType.MESH
ROWS_OUT = 32
SUB = 3


def kernel(
    sections,
    patches,
    heights_in,
    latent_ref,
    weight_ref,
    gain_ref,
    shift_ref,
    bias_ref,
    out_ref,
    lat,
    weights,
    wall,
    xbuf,
    skip,
    obuf,
    edge_lat,
    edge_out,
    heights_ref,
    gain_v,
    shift_v,
    bias_v,
    stat_lat,
    stat_out,
    stat_in,
    gain_b,
    shift_b,
    bias_b,
    ybuf,
    tbuf,
    sum_b,
    sq_b,
    local_sem,
    first_sem,
    ends_rs,
    mid_rs,
    up_rs,
    low_rs,
    stat_rs,
    skip_rs,
    ends_ss,
    mid_ss,
    up_ss,
    low_ss,
    stat_ss,
    skip_ss,
    out_sem,
):
    k = lax.axis_index("section")
    p = lax.axis_index("patch")
    height, channels, columns = lat.shape
    per_group = channels // GROUPS
    is_odd = lax.rem(k, 2) == 1
    last = k == sections - 1
    has_far = jnp.logical_and(is_odd, k + 2 < sections)

    load_lat = pltpu.make_async_copy(latent_ref, lat, local_sem.at[0])
    load_w = pltpu.make_async_copy(weight_ref, weights, local_sem.at[1])
    load_h = pltpu.make_async_copy(heights_in, heights_ref, local_sem.at[2])
    load_g = pltpu.make_async_copy(gain_ref, gain_v, local_sem.at[3])
    load_s = pltpu.make_async_copy(shift_ref, shift_v, local_sem.at[4])
    load_b = pltpu.make_async_copy(bias_ref, bias_v, local_sem.at[5])
    load_h.start()
    load_lat.start()
    load_g.start()
    load_s.start()
    load_b.start()
    load_w.start()

    barrier = pltpu.get_barrier_semaphore()

    def signal(s, q):
        pl.semaphore_signal(barrier, inc=1, device_id=(s, q), device_id_type=MESH)

    @pl.when(k == 0)
    def _():
        def step(i, c):
            q = lax.rem(p + i, patches)
            for s in range(sections):
                if s == 0:
                    @pl.when(i > 0)
                    def _():
                        signal(0, q)
                else:
                    signal(s, q)
            return c

        lax.fori_loop(0, patches, step, 0)

    @pl.when(k > 0)
    def _():
        def step(i, c):
            signal(k - 1, lax.rem(p + i, patches))
            return c

        lax.fori_loop(0, patches, step, 0)

        @pl.when(p > 0)
        def _():
            signal(k, p - 1)

        @pl.when(p < patches - 1)
        def _():
            signal(k, p + 1)

    if sections > 2:
        @pl.when(k == 1)
        def _():
            for s in range(2, sections):
                signal(s, p)

        @pl.when(jnp.logical_and(is_odd, k >= 3))
        def _():
            signal(k - 2, p)

    load_h.wait()
    height_own = heights_ref[p]
    window_rows = heights_ref[0]
    for i in range(1, patches):
        window_rows = window_rows + heights_ref[i]
    inv_count = 1.0 / (
        jnp.full((1, 128), window_rows, jnp.int32).astype(jnp.float32)
        * (per_group * columns)
    )

    chan = lax.broadcasted_iota(jnp.int32, (channels, 128), 0)
    first = lax.broadcasted_iota(jnp.int32, (channels, 128), 1) * per_group
    group_mask = jnp.where(
        jnp.logical_and(chan >= first, chan < first + per_group), 1.0, 0.0
    ).astype(jnp.float32)

    def to_groups(per_chan):
        total = jnp.sum(per_chan, axis=1, keepdims=True)
        return jnp.sum(total * group_mask, axis=0, keepdims=True)

    def to_channels(per_group_row):
        return jnp.sum(per_group_row * group_mask, axis=1, keepdims=True)

    def write_stats(ref, sums, squares):
        ref[...] = to_groups(sums) + pltpu.roll(to_groups(squares), GROUPS, 1)

    load_lat.wait()
    rows = [
        jnp.where(r < height_own, lat[r].astype(jnp.float32), 0.0) for r in range(height)
    ]
    sums, squares, edge = rows[0], rows[0] * rows[0], lat[0]
    for r in range(1, height):
        sums = sums + rows[r]
        squares = squares + rows[r] * rows[r]
        edge = jnp.where(height_own == r + 1, lat[r], edge)
    edge_lat[...] = edge
    write_stats(stat_lat, sums, squares)

    sends_to = (
        patches
        - (k == 0).astype(jnp.int32)
        + jnp.where(last, 0, patches)
        + jnp.where(k > 0, (p > 0).astype(jnp.int32) + (p < patches - 1).astype(jnp.int32), 0)
        + (k >= 2).astype(jnp.int32)
        + has_far.astype(jnp.int32)
    )
    pl.semaphore_wait(barrier, sends_to)

    def remote(src, dst, ssem, rsem, s, q):
        return pltpu.make_async_remote_copy(
            src_ref=src, dst_ref=dst, send_sem=ssem, recv_sem=rsem,
            device_id=(s, q), device_id_type=MESH,
        )

    def send_stats(m, s, stat, ssem, own):
        def step(i, c):
            q = lax.rem(p + i, patches)
            remote(stat, stat_in.at[m, p], ssem, stat_rs.at[m], s, q).start()
            return c

        if own is None:
            lax.fori_loop(0, patches, step, 0)
        else:
            lax.fori_loop(1, patches, step, 0)

            @pl.when(own)
            def _():
                pltpu.make_async_copy(stat, stat_in.at[m, p], stat_rs.at[m]).start()

            @pl.when(jnp.logical_not(own))
            def _():
                step(0, 0)

    def send_rows(m, s, head, tail, mid, ssem_ends, ssem_mid):
        remote(head, xbuf.at[m, 1], ssem_ends, ends_rs.at[m], s, p).start()
        remote(tail, xbuf.at[m, 2], ssem_ends, ends_rs.at[m], s, p).start()
        remote(mid, xbuf.at[m, 3], ssem_mid, mid_rs.at[m], s, p).start()

    def pass_on(m, head, tail):
        @pl.when(p < patches - 1)
        def _():
            remote(tail, xbuf.at[m, 0], up_ss.at[m], up_rs.at[m], k, p + 1).start()

        @pl.when(p > 0)
        def _():
            remote(head, xbuf.at[m, 4], low_ss.at[m], low_rs.at[m], k, p - 1).start()

    send_stats(k, 0, stat_lat, first_sem.at[0], k == 0)

    @pl.when(k == 0)
    def _():
        pass_on(0, lat.at[0], edge_lat)
        pltpu.make_async_copy(lat.at[0], xbuf.at[0, 1], ends_rs.at[0]).start()
        pltpu.make_async_copy(edge_lat, xbuf.at[0, 2], ends_rs.at[0]).start()
        pltpu.make_async_copy(lat.at[1], xbuf.at[0, 3], mid_rs.at[0]).start()

    @pl.when(k > 0)
    def _():
        send_rows(k, 0, lat.at[0], edge_lat, lat.at[1], first_sem.at[1], first_sem.at[2])

    @pl.when(k == 1)
    def _():
        pltpu.make_async_copy(lat, skip.at[1], skip_rs.at[1]).start()

    @pl.when(k != 1)
    def _():
        remote(lat, skip.at[k], first_sem.at[3], skip_rs.at[k], 1, p).start()

    eye = jnp.where(
        lax.broadcasted_iota(jnp.int32, (channels, channels), 0)
        == lax.broadcasted_iota(jnp.int32, (channels, channels), 1),
        1.0,
        0.0,
    ).astype(jnp.bfloat16)

    def spread(row):
        wide = jnp.broadcast_to(row.astype(jnp.float32), (128, channels)).astype(jnp.bfloat16)
        return lax.dot_general(
            eye, wide, (((1,), (1,)), ((), ())), preferred_element_type=jnp.float32
        )

    load_g.wait()
    gain_b[...] = spread(gain_v[...])
    load_s.wait()
    shift_b[...] = spread(shift_v[...])
    load_b.wait()
    for m in range(sections):
        bias_b[m] = spread(bias_v[m : m + 1, :])

    load_w.wait()
    for b in range(3):
        for a in range(3):
            wall[b * channels : (b + 1) * channels, a * channels : (a + 1) * channels] = weights[b, a]

    def wait_for(ref, sem):
        pltpu.make_async_copy(ref, ref, sem).wait()

    lane = lax.broadcasted_iota(jnp.int32, (ROWS_OUT, columns), 1)

    def sample(m, carry):
        wait_for(xbuf.at[m, pl.ds(1, 2)], ends_rs.at[m])

        @pl.when(jnp.logical_or(k > 0, m > 0))
        def _():
            pass_on(m, xbuf.at[m, 1], xbuf.at[m, 2])

        wait_for(stat_in.at[m], stat_rs.at[m])
        total = jnp.sum(stat_in[m], axis=0)
        mean = total * inv_count
        var = pltpu.roll(mean, 128 - GROUPS, 1) - mean * mean
        inv = lax.rsqrt(jnp.maximum(var, 0.0) + EPS)
        scale = to_channels(inv) * gain_b[...]
        offset = shift_b[...] - to_channels(mean) * scale

        def activate(values):
            v = values.astype(jnp.float32) * scale + offset
            half = 0.5 * v
            return half + half * jnp.tanh(half)

        def put(j, value):
            value = value.astype(jnp.bfloat16)
            for a in range(3):
                r = j - a
                if 0 <= r < height:
                    ybuf[a * channels : (a + 1) * channels, r * columns : (r + 1) * columns] = value

        put(1, activate(xbuf[m, 1]))
        tail = activate(xbuf[m, 2])
        wait_for(xbuf.at[m, 3], mid_rs.at[m])
        mid = activate(xbuf[m, 3])

        @pl.when(p > 0)
        def _():
            wait_for(xbuf.at[m, 0], up_rs.at[m])

        @pl.when(p < patches - 1)
        def _():
            wait_for(xbuf.at[m, 4], low_rs.at[m])

        put(0, jnp.where(p > 0, activate(xbuf[m, 0]), 0.0))
        below = jnp.where(p < patches - 1, activate(xbuf[m, 4]), 0.0)
        one, two = height_own == 1, height_own == 2
        put(2, jnp.where(one, below, jnp.where(two, tail, mid)))
        put(3, jnp.where(one, 0.0, jnp.where(two, below, tail)))
        put(4, jnp.where(height_own == 3, below, 0.0))

        tbuf[...] = jnp.dot(wall[...], ybuf[...], preferred_element_type=jnp.float32)

        @pl.when(is_odd)
        def _():
            wait_for(skip.at[m], skip_rs.at[m])

        for c0 in range(0, channels, ROWS_OUT):
            cs = slice(c0, c0 + ROWS_OUT)
            sums = jnp.zeros((ROWS_OUT, columns), jnp.float32)
            squares = sums
            edge = None
            for r in range(height):
                ls = slice(r * columns, (r + 1) * columns)
                left = pltpu.roll(tbuf[c0 : c0 + ROWS_OUT, ls], 1, 1)
                mid = tbuf[channels + c0 : channels + c0 + ROWS_OUT, ls]
                right = pltpu.roll(
                    tbuf[2 * channels + c0 : 2 * channels + c0 + ROWS_OUT, ls], columns - 1, 1
                )
                z = (
                    jnp.where(lane > 0, left, 0.0)
                    + mid
                    + jnp.where(lane < columns - 1, right, 0.0)
                    + bias_b[m, cs]
                )
                z = jnp.where(is_odd, skip[m, r, cs].astype(jnp.float32) + z, z)
                value = jnp.where(r < height_own, z, 0.0).astype(jnp.bfloat16)
                obuf[m, r, cs] = value
                wide = value.astype(jnp.float32)
                sums = sums + wide
                squares = squares + wide * wide
                edge = value if r == 0 else jnp.where(height_own == r + 1, value, edge)
            edge_out[m, cs] = edge
            sum_b[cs] = sums
            sq_b[cs] = squares

        @pl.when(jnp.logical_not(last))
        def _():
            send_rows(
                m, k + 1, obuf.at[m, 0], edge_out.at[m], obuf.at[m, 1], ends_ss.at[m], mid_ss.at[m]
            )
            write_stats(stat_out.at[m], sum_b[...], sq_b[...])
            send_stats(m, k + 1, stat_out.at[m], stat_ss.at[m], None)

        if sections > 2:
            @pl.when(has_far)
            def _():
                remote(obuf.at[m], skip.at[m], skip_ss.at[m], skip_rs.at[m], k + 2, p).start()

        pltpu.make_async_copy(obuf.at[m], out_ref.at[m], out_sem.at[m]).start()
        return carry

    lax.fori_loop(0, sections, sample, 0)

    wait_for(stat_in.at[0, pl.ds(1, patches - 1)], first_sem.at[0])

    @pl.when(k > 0)
    def _():
        wait_for(stat_lat, first_sem.at[0])
        wait_for(xbuf.at[0, pl.ds(0, 2)], first_sem.at[1])
        wait_for(edge_lat, first_sem.at[2])

    @pl.when(k != 1)
    def _():
        wait_for(lat, first_sem.at[3])

    def drain(m, carry):
        @pl.when(p < patches - 1)
        def _():
            wait_for(edge_lat, up_ss.at[m])

        @pl.when(p > 0)
        def _():
            wait_for(edge_lat, low_ss.at[m])

        @pl.when(jnp.logical_not(last))
        def _():
            wait_for(xbuf.at[m, pl.ds(0, 2)], ends_ss.at[m])
            wait_for(edge_lat, mid_ss.at[m])
            wait_for(stat_in.at[m], stat_ss.at[m])

        if sections > 2:
            @pl.when(has_far)
            def _():
                wait_for(obuf.at[m], skip_ss.at[m])

        wait_for(obuf.at[m], out_sem.at[m])
        return carry

    lax.fori_loop(0, sections, drain, 0)


def paired_kernel(
    patches,
    local,
    heights_in,
    latent_ref,
    weight_ref,
    gain_ref,
    shift_ref,
    bias_ref,
    out_ref,
    lat,
    weights,
    wall,
    part,
    xin,
    xmid,
    ends,
    heights_ref,
    gain_v,
    shift_v,
    bias_v,
    params,
    params_in,
    stat_lat,
    stat_mate,
    stat_all,
    total_out,
    total_in,
    stat_mid,
    stat_mid_all,
    gain_b,
    shift_b,
    bias_b,
    ybuf,
    tbuf,
    sum_b,
    sq_b,
    load_sem,
    ready,
    greeted,
    small_rs,
    small_ss,
    row_rs,
    row_ss,
    edge_rs,
    edge_ss,
    seed_rs,
    seed_ss,
    share_rs,
    share_ss,
    core_rs,
    core_ss,
    mid_rs,
    mid_ss,
    own_edge_rs,
    own_edge_ss,
    far_edge_rs,
    far_edge_ss,
    late_rs,
    late_ss,
    late_edge_rs,
    late_edge_ss,
    stat_rs,
    stat_ss,
):
    k = lax.axis_index("section")
    p = lax.axis_index("patch")
    height, channels, columns = lat.shape
    per_group = channels // GROUPS
    rest = channels - local
    lead = channels * 4 // 5
    lag = channels - lead
    piece = part.shape[0] // (8 * SUB)

    core = lax.rem(p, 2)
    mate = p + 1 - 2 * core
    across = p - 1 + 2 * core
    has_across = jnp.logical_and(across >= 0, across < patches)
    member = lax.rem(p, 8)
    turn_y = 2 - 4 * lax.rem(member // 2, 2)
    turn_z = 4 - 8 * (member // 4)
    friends = (p + turn_y, p + turn_z, p + turn_y + turn_z)

    load_h = pltpu.make_async_copy(heights_in, heights_ref, load_sem.at[0])
    load_lat = pltpu.make_async_copy(latent_ref, lat, load_sem.at[1])
    load_g = pltpu.make_async_copy(gain_ref, gain_v, load_sem.at[2])
    load_s = pltpu.make_async_copy(shift_ref, shift_v, load_sem.at[3])
    load_b = pltpu.make_async_copy(bias_ref, bias_v, load_sem.at[4])
    load_w = [
        pltpu.make_async_copy(
            weight_ref.at[:, :, span], weights.at[:, :, span], load_sem.at[5 + i]
        )
        for i, span in enumerate((pl.ds(0, local), pl.ds(local, rest)))
    ]

    barrier = pltpu.get_barrier_semaphore()

    def signal(s, q):
        pl.semaphore_signal(barrier, inc=1, device_id=(s, q), device_id_type=MESH)

    load_h.start()
    load_lat.start()
    load_w[0].start()

    @pl.when(k == 0)
    def _():
        signal(1, p)

        def step(i, carry):
            signal(0, lax.rem(p + i, patches))
            return carry

        lax.fori_loop(1, patches, step, 0)

    partners = [(q, True) for q in (mate, *friends)] + [(across, has_across)]

    def count(higher):
        total = 0
        for q, exists in partners:
            total = total + jnp.logical_and(exists, (q > p) == higher).astype(jnp.int32)
        return total

    @pl.when(k == 1)
    def _():
        for q, exists in partners:
            @pl.when(jnp.logical_and(exists, q > p))
            def _():
                signal(1, q)

        pl.semaphore_wait(barrier, 1 + count(False))
        pl.semaphore_signal(ready, inc=1, device_id=(0, p), device_id_type=MESH)
        for q, exists in partners:
            @pl.when(jnp.logical_and(exists, q < p))
            def _():
                pl.semaphore_signal(greeted, inc=1, device_id=(1, q), device_id_type=MESH)

    for load in (load_g, load_s, load_b, load_w[1]):
        load.start()

    def remote(src, dst, ssem, rsem, s, q):
        return pltpu.make_async_remote_copy(
            src_ref=src, dst_ref=dst, send_sem=ssem, recv_sem=rsem,
            device_id=(s, q), device_id_type=MESH,
        )

    def wait_for(ref, sem):
        pltpu.make_async_copy(ref, ref, sem).wait()

    load_h.wait()
    height_own = heights_ref[p]
    window_rows = heights_ref[0]
    for i in range(1, patches):
        window_rows = window_rows + heights_ref[i]
    inv_count = 1.0 / (
        jnp.full((1, 128), window_rows, jnp.int32).astype(jnp.float32)
        * (per_group * columns)
    )

    chan = lax.broadcasted_iota(jnp.int32, (channels, 128), 0)
    first = lax.broadcasted_iota(jnp.int32, (channels, 128), 1) * per_group
    group_mask = jnp.where(
        jnp.logical_and(chan >= first, chan < first + per_group), 1.0, 0.0
    ).astype(jnp.float32)

    def to_groups(per_chan):
        total = jnp.sum(per_chan, axis=1, keepdims=True)
        return jnp.sum(total * group_mask, axis=0, keepdims=True)

    def to_channels(per_group_row):
        return jnp.sum(per_group_row * group_mask, axis=1, keepdims=True)

    def both(sums, squares):
        return to_groups(sums) + pltpu.roll(to_groups(squares), GROUPS, 1)

    load_lat.wait()
    rows = [
        jnp.where(r < height_own, lat[r].astype(jnp.float32), 0.0) for r in range(height)
    ]
    sums, squares, edge = rows[0], rows[0] * rows[0], lat[0]
    for r in range(1, height):
        sums = sums + rows[r]
        squares = squares + rows[r] * rows[r]
        edge = jnp.where(height_own == r + 1, lat[r], edge)
    xin[k, 1] = lat[0]
    xin[k, 2] = edge
    xin[k, 3] = lat[1]
    stat_lat[...] = both(sums, squares)

    def take_params():
        load_g.wait()
        load_s.wait()
        load_b.wait()
        params[0:1] = gain_v[...].astype(jnp.float32)
        params[1:2] = shift_v[...].astype(jnp.float32)
        params[2:4] = bias_v[...].astype(jnp.float32)

    eye = jnp.where(
        lax.broadcasted_iota(jnp.int32, (channels, channels), 0)
        == lax.broadcasted_iota(jnp.int32, (channels, channels), 1),
        1.0,
        0.0,
    ).astype(jnp.bfloat16)

    def spread(row):
        wide = jnp.broadcast_to(row, (128, channels)).astype(jnp.bfloat16)
        return lax.dot_general(
            eye, wide, (((1,), (1,)), ((), ())), preferred_element_type=jnp.float32
        )

    def spread_params(at, source):
        gain_b[at] = spread(source[0:1])
        shift_b[at] = spread(source[1:2])
        for m in range(2):
            bias_b[at, m] = spread(source[2 + m : 3 + m])

    def depth(a, c):
        return a * lead + c if c < lead else 3 * lead + a * lag + c - lead

    def build(is_rest):
        for b in range(3):
            for a in range(3):
                for lo, hi in ((0, lead), (lead, channels)):
                    at = depth(a, lo)
                    cols = slice(at, at + hi - lo)
                    if is_rest:
                        start = 3 * local + b * rest
                        wall[start : start + rest, cols] = weights[b, a, local:, lo:hi]
                    else:
                        wall[b * local : (b + 1) * local, cols] = weights[b, a, :local, lo:hi]

    cross_slot, other_slot = 1 + core, 2 - core

    def send_rows():
        for i, slot in enumerate((cross_slot, other_slot, 3)):
            remote(xin.at[k, slot], xin.at[k, slot], row_ss.at[i], row_rs.at[i], 1 - k, p).start()

    def wait_row(i):
        wait_for(lat.at[0], row_rs.at[i])

    def send_edge(kind, ref, m, span, ssem, rsem):
        src_slot = cross_slot if kind == 0 else other_slot
        dst_slot = 4 - 4 * core if kind == 0 else 4 * core
        q = across if kind == 0 else mate

        def go():
            remote(
                ref.at[m, src_slot, span], ref.at[m, dst_slot, span],
                ssem.at[m, kind], rsem.at[m, kind], k, q,
            ).start()

        if kind == 0:
            pl.when(has_across)(go)
        else:
            go()

    def wait_edge(kind, ref, sem, m):
        if kind == 0:
            @pl.when(has_across)
            def _():
                wait_for(ref, sem.at[m, kind])
        else:
            wait_for(ref, sem.at[m, kind])

    whole = pl.ds(0, channels)
    head_part = pl.ds(0, local)
    tail_part = pl.ds(local, rest)
    early_part = pl.ds(local, lead - local)
    late_part = pl.ds(lead, lag)

    def pass_in(kind, m):
        send_edge(kind, xin, m, whole, edge_ss, edge_rs)

    def coefficients(total, at):
        mean = total * inv_count
        var = pltpu.roll(mean, 128 - GROUPS, 1) - mean * mean
        inv = lax.rsqrt(jnp.maximum(var, 0.0) + EPS)
        scale = to_channels(inv) * gain_b[at]
        return scale, shift_b[at] - to_channels(mean) * scale

    def fill(rows_of, m, scale, offset, before_edges, low=0, high=channels):
        def activate(slot):
            v = rows_of[m, slot, low:high].astype(jnp.float32) * scale[low:high] + offset[low:high]
            half = 0.5 * v
            return half + half * jnp.tanh(half)

        def put(j, value):
            value = value.astype(jnp.bfloat16)
            for a in range(3):
                r = j - a
                if 0 <= r < height:
                    at = (m * height + r) * columns
                    for lo, hi in ((low, min(high, lead)), (max(low, lead), high)):
                        if lo < hi:
                            start = depth(a, lo)
                            ybuf[start : start + hi - lo, at : at + columns] = value[lo - low : hi - low]

        put(1, activate(1))
        tail = activate(2)
        mid = activate(3)
        before_edges()
        put(0, jnp.where(p > 0, activate(0), 0.0))
        below = jnp.where(p < patches - 1, activate(4), 0.0)
        one, two = height_own == 1, height_own == 2
        put(2, jnp.where(one, below, jnp.where(two, tail, mid)))
        put(3, jnp.where(one, 0.0, jnp.where(two, below, tail)))
        put(4, jnp.where(height_own == 3, below, 0.0))

    lane = lax.broadcasted_iota(jnp.int32, (ROWS_OUT, columns), 1)

    def conv_row(m, r, c0, count, bias):
        at = (m * height + r) * columns
        ls = slice(at, at + columns)

        def block(b):
            start = b * local + c0 if c0 < local else 3 * local + b * rest + c0 - local
            return tbuf[start : start + count, ls]

        return (
            jnp.where(lane > 0, pltpu.roll(block(0), 1, 1), 0.0)
            + block(1)
            + jnp.where(lane < columns - 1, pltpu.roll(block(2), columns - 1, 1), 0.0)
            + bias
        )

    def far(m, is_late):
        if m == 0:
            return tail_part, mid_ss.at[0], mid_rs.at[0], far_edge_ss.at[0], far_edge_rs.at[0]
        if is_late:
            return late_part, late_ss, late_rs, late_edge_ss, late_edge_rs
        return early_part, mid_ss.at[1], mid_rs.at[1], far_edge_ss.at[1], far_edge_rs.at[1]

    def send_mid(i, m, is_late=False):
        span, ssem, rsem, _, _ = far(m, is_late)
        src = (ends.at[m, core], ends.at[m, 1 - core], out_ref.at[m, 1])[i]
        slot = (cross_slot, other_slot, 3)[i]
        remote(src.at[span], xmid.at[m, slot, span], ssem.at[i], rsem.at[i], 1, p).start()

    def send_across(is_late):
        span, _, _, ssem, rsem = far(1, is_late)

        @pl.when(has_across)
        def _():
            remote(
                ends.at[1, core, span], xmid.at[1, 4 - 4 * core, span],
                ssem.at[0], rsem.at[0], 1, across,
            ).start()

    def wait_far(i, m, is_late=False):
        span, _, rsem, _, _ = far(m, is_late)
        wait_for(out_ref.at[m, 1, span], rsem.at[i])

    def wait_far_edges(m, is_late=False):
        span, _, _, _, rsem = far(m, is_late)

        @pl.when(has_across)
        def _():
            wait_for(lat.at[0, span], rsem.at[0])

        wait_for(lat.at[0, span], rsem.at[1])

    def pass_far(kind, m, is_late=False):
        span, _, _, ssem, rsem = far(m, is_late)
        wait_far(kind, m, is_late)
        src_slot = cross_slot if kind == 0 else other_slot
        dst_slot = 4 - 4 * core if kind == 0 else 4 * core
        q = across if kind == 0 else mate

        def go():
            remote(
                xmid.at[m, src_slot, span], xmid.at[m, dst_slot, span],
                ssem.at[kind], rsem.at[kind], 1, q,
            ).start()

        if kind == 0:
            pl.when(has_across)(go)
        else:
            go()

    def multiply(count, m0, samples, low=0, high=3 * channels):
        cols = slice(m0 * height * columns, (m0 + samples) * height * columns)
        left = wall if count > 3 * local else part
        product = jnp.dot(
            left[:, low:high], ybuf[low:high, cols], preferred_element_type=jnp.float32
        )
        tbuf[:count, cols] = product if low == 0 else tbuf[:count, cols] + product

    @pl.when(k == 1)
    def _():
        remote(stat_lat, stat_mate, small_ss.at[1], small_rs.at[1], 0, p).start()
        send_rows()

        @pl.when(count(True) > 0)
        def _():
            pl.semaphore_wait(greeted, count(True))

        pass_in(0, 1)
        pass_in(1, 1)
        take_params()
        spread_params(0, params)
        load_w[0].wait()
        build(False)
        load_w[1].wait()
        build(True)

    @pl.when(k == 0)
    def _():
        take_params()
        load_w[0].wait()
        build(False)
        pl.semaphore_wait(ready, 1)
        remote(params, params_in, small_ss.at[0], small_rs.at[0], 1, p).start()
        for i in range(SUB):
            at = pl.ds((member * SUB + i) * piece, piece)
            remote(wall.at[at], part.at[at], seed_ss.at[i], seed_rs.at[i], 1, p).start()
        send_rows()
        pl.semaphore_wait(barrier, patches - 1)

        def share_stats(m, source):
            def step(i, carry):
                q = lax.rem(p + i, patches)
                remote(
                    source, stat_all.at[m, p], small_ss.at[2 + m], small_rs.at[2 + m], 0, q
                ).start()
                return carry

            lax.fori_loop(1, patches, step, 0)
            stat_all[m, p] = source[...]

        def total_of(m):
            wait_for(stat_all.at[m, pl.ds(0, patches - 1)], small_rs.at[2 + m])
            total = jnp.sum(stat_all[m], axis=0)
            total_out[m] = total
            remote(
                total_out.at[m], total_in.at[m], small_ss.at[4 + m], small_rs.at[4 + m], 1, p
            ).start()
            return total

        share_stats(0, stat_lat)
        pass_in(0, 0)
        pass_in(1, 0)
        spread_params(0, params)
        load_w[1].wait()
        build(True)
        wait_for(stat_lat, small_rs.at[1])
        share_stats(1, stat_mate)
        wait_row(0)
        pass_in(0, 1)

        total = total_of(0)
        for m in range(2):
            scale, offset = coefficients(total, 0)

            def before_edges():
                if m == 0:
                    wait_row(1)
                    pass_in(1, 1)
                for kind in range(2):
                    wait_edge(kind, lat.at[0], edge_rs, m)

            if m == 1:
                wait_row(2)
            fill(xin, m, scale, offset, before_edges)
            multiply(3 * channels, m, 1)
            for c0 in range(0, channels, ROWS_OUT):
                cs = slice(c0, c0 + ROWS_OUT)
                sums = jnp.zeros((ROWS_OUT, columns), jnp.float32)
                squares = sums
                edge = None
                for r in range(height):
                    z = conv_row(m, r, c0, ROWS_OUT, bias_b[0, m, cs])
                    value = jnp.where(r < height_own, z, 0.0).astype(jnp.bfloat16)
                    out_ref[m, r, cs] = value
                    wide = value.astype(jnp.float32)
                    sums = sums + wide
                    squares = squares + wide * wide
                    edge = value if r == 0 else jnp.where(height_own == r + 1, value, edge)
                    if r == 0:
                        ends[m, 0, cs] = value
                ends[m, 1, cs] = edge
                sum_b[cs] = sums
                sq_b[cs] = squares
            stat_mid[m] = both(sum_b[...], sq_b[...])

            def step(i, carry):
                q = lax.rem(p + i, patches)
                remote(stat_mid.at[m], stat_mid_all.at[m, p], stat_ss.at[m], stat_rs.at[m], 1, q).start()
                return carry

            if m == 0:
                send_mid(0, m)
            lax.fori_loop(0, patches, step, 0)
            if m == 1:
                send_across(False)
                send_mid(0, m)
            if m == 0:
                total = total_of(1)
                send_mid(1, 0)
        send_mid(2, 0)
        send_mid(1, 1)
        send_mid(2, 1)
        send_mid(1, 1, True)
        send_across(True)
        send_mid(0, 1, True)
        send_mid(2, 1, True)

        wait_for(params, small_ss.at[0])
        for m in range(2):
            wait_for(stat_all.at[m, pl.ds(0, patches - 1)], small_ss.at[2 + m])
            wait_for(total_out.at[m], small_ss.at[4 + m])
        for i in range(SUB):
            wait_for(part.at[pl.ds(0, piece)], seed_ss.at[i])
        for m, is_late in ((0, False), (1, False), (1, True)):
            span, ssem, _, edge_sem, _ = far(m, is_late)
            for i in range(3):
                wait_for(out_ref.at[m, 1, span], ssem.at[i])
            if m == 1:
                @pl.when(has_across)
                def _():
                    wait_for(lat.at[0, span], edge_sem.at[0])
        for m in range(2):
            wait_for(stat_mid_all.at[m], stat_ss.at[m])

    @pl.when(k == 1)
    def _():
        def to_mate(index, sem):
            at = pl.ds(index * piece, piece)
            remote(part.at[at], part.at[at], core_ss.at[sem], core_rs.at[0], 1, mate).start()

        def seed(i, carry):
            index = member * SUB + i
            at = pl.ds(index * piece, piece)
            wait_for(part.at[pl.ds(0, piece)], seed_rs.at[i])
            for j in range(3):
                remote(
                    part.at[at], part.at[at], share_ss.at[j, i], share_rs.at[j, i], 1, friends[j]
                ).start()
            to_mate(index, i)
            return carry

        lax.fori_loop(0, SUB, seed, 0)
        wait_for(params, small_rs.at[0])
        spread_params(1, params_in)
        wait_row(0)
        pass_in(0, 0)

        def shared(i, carry):
            for j in range(3):
                wait_for(part.at[pl.ds(0, piece)], share_rs.at[j, i])
                to_mate(lax.rem(friends[j], 8) * SUB + i, (1 + j) * SUB + i)
            return carry

        lax.fori_loop(0, SUB, shared, 0)
        wait_row(1)
        pass_in(1, 0)
        wait_row(2)

        for m in range(2):
            if m == 0:
                pass_far(0, 0)
            wait_for(total_out.at[m], small_rs.at[4 + m])
            scale, offset = coefficients(total_in[m], 1)

            def before_edges():
                for kind in range(2):
                    wait_edge(kind, lat.at[0], edge_rs, m)

            fill(xin, m, scale, offset, before_edges)
            if m == 0:
                wait_for(part.at[pl.ds(0, 4 * SUB * piece)], core_rs.at[0])
            multiply(3 * local, m, 1)
            for c0 in range(0, local, ROWS_OUT):
                cs = slice(c0, c0 + ROWS_OUT)
                edge = None
                for r in range(height):
                    value = conv_row(m, r, c0, ROWS_OUT, bias_b[1, m, cs]).astype(jnp.bfloat16)
                    edge = value if r == 0 else jnp.where(height_own == r + 1, value, edge)
                    if r == 0:
                        xmid[m, 1, cs] = value
                    if r == 1:
                        xmid[m, 3, cs] = value
                xmid[m, 2, cs] = edge
            for kind in range(2):
                send_edge(kind, xmid, m, head_part, own_edge_ss, own_edge_rs)
            if m == 0:
                pass_far(1, 0)

        for m in range(2):
            wait_for(stat_mid_all.at[m], stat_rs.at[m])
            scale, offset = coefficients(jnp.sum(stat_mid_all[m], axis=0), 0)

            def before_edges():
                if m == 0:
                    pass_far(1, 1)
                for kind in range(2):
                    wait_edge(kind, lat.at[0, head_part], own_edge_rs, m)
                wait_far_edges(m)

            wait_far(2, m)
            if m == 0:
                fill(xmid, 0, scale, offset, before_edges)
                multiply(3 * channels, 0, 1)
                pass_far(1, 1, True)
            else:
                wait_far(0, 1)
                fill(xmid, 1, scale, offset, before_edges, 0, lead)
                multiply(3 * channels, 1, 1, 0, 3 * lead)
                wait_far(0, 1, True)
                wait_far(2, 1, True)
                fill(xmid, 1, scale, offset, lambda: wait_far_edges(1, True), lead, channels)
                multiply(3 * channels, 1, 1, 3 * lead, 3 * channels)
            for c0 in range(0, channels, ROWS_OUT):
                cs = slice(c0, c0 + ROWS_OUT)
                for r in range(height):
                    z = conv_row(m, r, c0, ROWS_OUT, bias_b[0, m, cs])
                    z = xin[m, (1, 3, 2)[r], cs].astype(jnp.float32) + z
                    out_ref[m, r, cs] = jnp.where(r < height_own, z, 0.0).astype(jnp.bfloat16)

        wait_for(stat_lat, small_ss.at[1])
        for i in range(SUB):
            for j in range(3):
                wait_for(part.at[pl.ds(0, piece)], share_ss.at[j, i])
        for i in range(4 * SUB):
            wait_for(part.at[pl.ds(0, piece)], core_ss.at[i])
        for m in range(2):
            for kind in range(2):
                wait_edge(kind, lat.at[0, head_part], own_edge_ss, m)
        wait_edge(0, lat.at[0, tail_part], far_edge_ss, 0)
        for m, is_late in ((0, False), (1, False), (1, True)):
            span, _, _, sem, _ = far(m, is_late)
            wait_for(lat.at[0, span], sem.at[1])

    for i in range(3):
        wait_for(lat.at[0], row_ss.at[i])
    for m in range(2):
        for kind in range(2):
            wait_edge(kind, lat.at[0], edge_ss, m)


def paired_call(patches, operands, height, channels, columns):
    bf16, f32 = jnp.bfloat16, jnp.float32
    local = channels * 2 // 5
    hbm = pl.BlockSpec(memory_space=pltpu.HBM)
    dma = pltpu.SemaphoreType.DMA
    return pl.pallas_call(
        functools.partial(paired_kernel, patches, local),
        out_shape=jax.ShapeDtypeStruct((2, height, channels, columns), bf16),
        in_specs=[hbm] * 6,
        out_specs=pl.BlockSpec(memory_space=pltpu.VMEM),
        scratch_shapes=[
            pltpu.VMEM((height, channels, columns), bf16),
            pltpu.VMEM((3, 3, channels, channels), bf16),
            pltpu.VMEM((3 * channels, 3 * channels), bf16),
            pltpu.VMEM((3 * local, 3 * channels), bf16),
            pltpu.VMEM((2, height + 2, channels, columns), bf16),
            pltpu.VMEM((2, height + 2, channels, columns), bf16),
            pltpu.VMEM((2, 2, channels, columns), bf16),
            pltpu.SMEM((patches,), jnp.int32),
            pltpu.VMEM((1, channels), bf16),
            pltpu.VMEM((1, channels), bf16),
            pltpu.VMEM((2, channels), bf16),
            pltpu.VMEM((8, channels), f32),
            pltpu.VMEM((8, channels), f32),
            pltpu.VMEM((1, 128), f32),
            pltpu.VMEM((1, 128), f32),
            pltpu.VMEM((2, patches, 1, 128), f32),
            pltpu.VMEM((2, 1, 128), f32),
            pltpu.VMEM((2, 1, 128), f32),
            pltpu.VMEM((2, 1, 128), f32),
            pltpu.VMEM((2, patches, 1, 128), f32),
            pltpu.VMEM((2, channels, 128), f32),
            pltpu.VMEM((2, channels, 128), f32),
            pltpu.VMEM((2, 2, channels, 128), f32),
            pltpu.VMEM((3 * channels, 2 * height * columns), bf16),
            pltpu.VMEM((3 * channels, 2 * height * columns), f32),
            pltpu.VMEM((channels, columns), f32),
            pltpu.VMEM((channels, columns), f32),
            dma((7,)),
            pltpu.SemaphoreType.REGULAR,
            pltpu.SemaphoreType.REGULAR,
            dma((6,)),
            dma((6,)),
            dma((3,)),
            dma((3,)),
            dma((2, 2)),
            dma((2, 2)),
            dma((SUB,)),
            dma((SUB,)),
            dma((3, SUB)),
            dma((3, SUB)),
            dma((1,)),
            dma((4 * SUB,)),
            dma((2, 3)),
            dma((2, 3)),
            dma((2, 2)),
            dma((2, 2)),
            dma((2, 2)),
            dma((2, 2)),
            dma((3,)),
            dma((3,)),
            dma((2,)),
            dma((2,)),
            dma((2,)),
            dma((2,)),
        ],
        compiler_params=pltpu.CompilerParams(
            collective_id=0, has_side_effects=True, vmem_limit_bytes=48 * 1024 * 1024
        ),
    )(*operands)


def per_device(sections, patches, latent, conv_weight, norm_gain, norm_shift, step_bias, patch_rows):
    latent = jnp.transpose(latent[0], (1, 0, 2))
    weight = jnp.transpose(conv_weight[0], (0, 2, 1, 3))
    height, channels, columns = latent.shape
    bf16, f32 = jnp.bfloat16, jnp.float32
    hbm = pl.BlockSpec(memory_space=pltpu.HBM)
    dma = pltpu.SemaphoreType.DMA
    operands = [
        pltpu.with_memory_space_constraint(array, pltpu.HBM)
        for array in (patch_rows, latent, weight, norm_gain, norm_shift, step_bias[0])
    ]
    if sections == 2 and patches % 8 == 0:
        out = paired_call(patches, operands, height, channels, columns)
        return jnp.transpose(out, (0, 2, 1, 3))[None]
    out = pl.pallas_call(
        functools.partial(kernel, sections, patches),
        out_shape=jax.ShapeDtypeStruct((sections, height, channels, columns), bf16),
        in_specs=[hbm] * 6,
        out_specs=pl.BlockSpec(memory_space=pl.ANY),
        scratch_shapes=[
            pltpu.VMEM((height, channels, columns), bf16),
            pltpu.VMEM((3, 3, channels, channels), bf16),
            pltpu.VMEM((3 * channels, 3 * channels), bf16),
            pltpu.VMEM((sections, height + 2, channels, columns), bf16),
            pltpu.VMEM((sections, height, channels, columns), bf16),
            pltpu.VMEM((sections, height, channels, columns), bf16),
            pltpu.VMEM((channels, columns), bf16),
            pltpu.VMEM((sections, channels, columns), bf16),
            pltpu.SMEM((patches,), jnp.int32),
            pltpu.VMEM((1, channels), bf16),
            pltpu.VMEM((1, channels), bf16),
            pltpu.VMEM((sections, channels), bf16),
            pltpu.VMEM((1, 128), f32),
            pltpu.VMEM((sections, 1, 128), f32),
            pltpu.VMEM((sections, patches, 1, 128), f32),
            pltpu.VMEM((channels, 128), f32),
            pltpu.VMEM((channels, 128), f32),
            pltpu.VMEM((sections, channels, 128), f32),
            pltpu.VMEM((3 * channels, height * columns), bf16),
            pltpu.VMEM((3 * channels, height * columns), f32),
            pltpu.VMEM((channels, columns), f32),
            pltpu.VMEM((channels, columns), f32),
            dma((6,)),
            dma((4,)),
        ]
        + [dma((sections,)) for _ in range(13)],
        compiler_params=pltpu.CompilerParams(
            collective_id=0, has_side_effects=True, vmem_limit_bytes=48 * 1024 * 1024
        ),
    )(*operands)
    return jnp.transpose(out, (0, 2, 1, 3))[None]


def solution(mesh):
    placed = (
        P("section", None, "patch", None),
        P("section", None, None, None, None),
        P("section", None),
        P("section", None),
        P("section", None, None),
        P(),
    )
    return jax.shard_map(
        functools.partial(per_device, mesh.shape["section"], mesh.shape["patch"]),
        mesh=mesh,
        in_specs=placed,
        out_specs=P("section", None, None, "patch", None),
        check_vma=False,
    )
```

```python
import functools

import jax
import jax.numpy as jnp
from jax import lax
from jax.experimental import pallas as pl
from jax.experimental.pallas import tpu as pltpu
from jax.sharding import PartitionSpec as P

GROUPS = 32
EPS = 1e-05
MESH = pl.DeviceIdType.MESH
ROWS_OUT = 32
SUB = 3


def kernel(
    sections,
    patches,
    heights_in,
    latent_ref,
    weight_ref,
    gain_ref,
    shift_ref,
    bias_ref,
    out_ref,
    lat,
    weights,
    wall,
    xbuf,
    skip,
    obuf,
    edge_lat,
    edge_out,
    heights_ref,
    gain_v,
    shift_v,
    bias_v,
    stat_lat,
    stat_out,
    stat_in,
    gain_b,
    shift_b,
    bias_b,
    ybuf,
    tbuf,
    sum_b,
    sq_b,
    local_sem,
    first_sem,
    ends_rs,
    mid_rs,
    up_rs,
    low_rs,
    stat_rs,
    skip_rs,
    ends_ss,
    mid_ss,
    up_ss,
    low_ss,
    stat_ss,
    skip_ss,
    out_sem,
):
    k = lax.axis_index("section")
    p = lax.axis_index("patch")
    height, channels, columns = lat.shape
    per_group = channels // GROUPS
    is_odd = lax.rem(k, 2) == 1
    last = k == sections - 1
    has_far = jnp.logical_and(is_odd, k + 2 < sections)

    load_lat = pltpu.make_async_copy(latent_ref, lat, local_sem.at[0])
    load_w = pltpu.make_async_copy(weight_ref, weights, local_sem.at[1])
    load_h = pltpu.make_async_copy(heights_in, heights_ref, local_sem.at[2])
    load_g = pltpu.make_async_copy(gain_ref, gain_v, local_sem.at[3])
    load_s = pltpu.make_async_copy(shift_ref, shift_v, local_sem.at[4])
    load_b = pltpu.make_async_copy(bias_ref, bias_v, local_sem.at[5])
    load_h.start()
    load_lat.start()
    load_g.start()
    load_s.start()
    load_b.start()
    load_w.start()

    barrier = pltpu.get_barrier_semaphore()

    def signal(s, q):
        pl.semaphore_signal(barrier, inc=1, device_id=(s, q), device_id_type=MESH)

    @pl.when(k == 0)
    def _():
        def step(i, c):
            q = lax.rem(p + i, patches)
            for s in range(sections):
                if s == 0:
                    @pl.when(i > 0)
                    def _():
                        signal(0, q)
                else:
                    signal(s, q)
            return c

        lax.fori_loop(0, patches, step, 0)

    @pl.when(k > 0)
    def _():
        def step(i, c):
            signal(k - 1, lax.rem(p + i, patches))
            return c

        lax.fori_loop(0, patches, step, 0)

        @pl.when(p > 0)
        def _():
            signal(k, p - 1)

        @pl.when(p < patches - 1)
        def _():
            signal(k, p + 1)

    if sections > 2:
        @pl.when(k == 1)
        def _():
            for s in range(2, sections):
                signal(s, p)

        @pl.when(jnp.logical_and(is_odd, k >= 3))
        def _():
            signal(k - 2, p)

    load_h.wait()
    height_own = heights_ref[p]
    window_rows = heights_ref[0]
    for i in range(1, patches):
        window_rows = window_rows + heights_ref[i]
    inv_count = 1.0 / (
        jnp.full((1, 128), window_rows, jnp.int32).astype(jnp.float32)
        * (per_group * columns)
    )

    chan = lax.broadcasted_iota(jnp.int32, (channels, 128), 0)
    first = lax.broadcasted_iota(jnp.int32, (channels, 128), 1) * per_group
    group_mask = jnp.where(
        jnp.logical_and(chan >= first, chan < first + per_group), 1.0, 0.0
    ).astype(jnp.float32)

    def to_groups(per_chan):
        total = jnp.sum(per_chan, axis=1, keepdims=True)
        return jnp.sum(total * group_mask, axis=0, keepdims=True)

    def to_channels(per_group_row):
        return jnp.sum(per_group_row * group_mask, axis=1, keepdims=True)

    def write_stats(ref, sums, squares):
        ref[...] = to_groups(sums) + pltpu.roll(to_groups(squares), GROUPS, 1)

    load_lat.wait()
    rows = [
        jnp.where(r < height_own, lat[r].astype(jnp.float32), 0.0) for r in range(height)
    ]
    sums, squares, edge = rows[0], rows[0] * rows[0], lat[0]
    for r in range(1, height):
        sums = sums + rows[r]
        squares = squares + rows[r] * rows[r]
        edge = jnp.where(height_own == r + 1, lat[r], edge)
    edge_lat[...] = edge
    write_stats(stat_lat, sums, squares)

    sends_to = (
        patches
        - (k == 0).astype(jnp.int32)
        + jnp.where(last, 0, patches)
        + jnp.where(k > 0, (p > 0).astype(jnp.int32) + (p < patches - 1).astype(jnp.int32), 0)
        + (k >= 2).astype(jnp.int32)
        + has_far.astype(jnp.int32)
    )
    pl.semaphore_wait(barrier, sends_to)

    def remote(src, dst, ssem, rsem, s, q):
        return pltpu.make_async_remote_copy(
            src_ref=src, dst_ref=dst, send_sem=ssem, recv_sem=rsem,
            device_id=(s, q), device_id_type=MESH,
        )

    def send_stats(m, s, stat, ssem, own):
        def step(i, c):
            q = lax.rem(p + i, patches)
            remote(stat, stat_in.at[m, p], ssem, stat_rs.at[m], s, q).start()
            return c

        if own is None:
            lax.fori_loop(0, patches, step, 0)
        else:
            lax.fori_loop(1, patches, step, 0)

            @pl.when(own)
            def _():
                pltpu.make_async_copy(stat, stat_in.at[m, p], stat_rs.at[m]).start()

            @pl.when(jnp.logical_not(own))
            def _():
                step(0, 0)

    def send_rows(m, s, head, tail, mid, ssem_ends, ssem_mid):
        remote(head, xbuf.at[m, 1], ssem_ends, ends_rs.at[m], s, p).start()
        remote(tail, xbuf.at[m, 2], ssem_ends, ends_rs.at[m], s, p).start()
        remote(mid, xbuf.at[m, 3], ssem_mid, mid_rs.at[m], s, p).start()

    def pass_on(m, head, tail):
        @pl.when(p < patches - 1)
        def _():
            remote(tail, xbuf.at[m, 0], up_ss.at[m], up_rs.at[m], k, p + 1).start()

        @pl.when(p > 0)
        def _():
            remote(head, xbuf.at[m, 4], low_ss.at[m], low_rs.at[m], k, p - 1).start()

    send_stats(k, 0, stat_lat, first_sem.at[0], k == 0)

    @pl.when(k == 0)
    def _():
        pass_on(0, lat.at[0], edge_lat)
        pltpu.make_async_copy(lat.at[0], xbuf.at[0, 1], ends_rs.at[0]).start()
        pltpu.make_async_copy(edge_lat, xbuf.at[0, 2], ends_rs.at[0]).start()
        pltpu.make_async_copy(lat.at[1], xbuf.at[0, 3], mid_rs.at[0]).start()

    @pl.when(k > 0)
    def _():
        send_rows(k, 0, lat.at[0], edge_lat, lat.at[1], first_sem.at[1], first_sem.at[2])

    @pl.when(k == 1)
    def _():
        pltpu.make_async_copy(lat, skip.at[1], skip_rs.at[1]).start()

    @pl.when(k != 1)
    def _():
        remote(lat, skip.at[k], first_sem.at[3], skip_rs.at[k], 1, p).start()

    eye = jnp.where(
        lax.broadcasted_iota(jnp.int32, (channels, channels), 0)
        == lax.broadcasted_iota(jnp.int32, (channels, channels), 1),
        1.0,
        0.0,
    ).astype(jnp.bfloat16)

    def spread(row):
        wide = jnp.broadcast_to(row.astype(jnp.float32), (128, channels)).astype(jnp.bfloat16)
        return lax.dot_general(
            eye, wide, (((1,), (1,)), ((), ())), preferred_element_type=jnp.float32
        )

    load_g.wait()
    gain_b[...] = spread(gain_v[...])
    load_s.wait()
    shift_b[...] = spread(shift_v[...])
    load_b.wait()
    for m in range(sections):
        bias_b[m] = spread(bias_v[m : m + 1, :])

    load_w.wait()
    for b in range(3):
        for a in range(3):
            wall[b * channels : (b + 1) * channels, a * channels : (a + 1) * channels] = weights[b, a]

    def wait_for(ref, sem):
        pltpu.make_async_copy(ref, ref, sem).wait()

    lane = lax.broadcasted_iota(jnp.int32, (ROWS_OUT, columns), 1)

    def sample(m, carry):
        wait_for(xbuf.at[m, pl.ds(1, 2)], ends_rs.at[m])

        @pl.when(jnp.logical_or(k > 0, m > 0))
        def _():
            pass_on(m, xbuf.at[m, 1], xbuf.at[m, 2])

        wait_for(stat_in.at[m], stat_rs.at[m])
        total = jnp.sum(stat_in[m], axis=0)
        mean = total * inv_count
        var = pltpu.roll(mean, 128 - GROUPS, 1) - mean * mean
        inv = lax.rsqrt(jnp.maximum(var, 0.0) + EPS)
        scale = to_channels(inv) * gain_b[...]
        offset = shift_b[...] - to_channels(mean) * scale

        def activate(values):
            v = values.astype(jnp.float32) * scale + offset
            half = 0.5 * v
            return half + half * jnp.tanh(half)

        def put(j, value):
            value = value.astype(jnp.bfloat16)
            for a in range(3):
                r = j - a
                if 0 <= r < height:
                    ybuf[a * channels : (a + 1) * channels, r * columns : (r + 1) * columns] = value

        put(1, activate(xbuf[m, 1]))
        tail = activate(xbuf[m, 2])
        wait_for(xbuf.at[m, 3], mid_rs.at[m])
        mid = activate(xbuf[m, 3])

        @pl.when(p > 0)
        def _():
            wait_for(xbuf.at[m, 0], up_rs.at[m])

        @pl.when(p < patches - 1)
        def _():
            wait_for(xbuf.at[m, 4], low_rs.at[m])

        put(0, jnp.where(p > 0, activate(xbuf[m, 0]), 0.0))
        below = jnp.where(p < patches - 1, activate(xbuf[m, 4]), 0.0)
        one, two = height_own == 1, height_own == 2
        put(2, jnp.where(one, below, jnp.where(two, tail, mid)))
        put(3, jnp.where(one, 0.0, jnp.where(two, below, tail)))
        put(4, jnp.where(height_own == 3, below, 0.0))

        tbuf[...] = jnp.dot(wall[...], ybuf[...], preferred_element_type=jnp.float32)

        @pl.when(is_odd)
        def _():
            wait_for(skip.at[m], skip_rs.at[m])

        for c0 in range(0, channels, ROWS_OUT):
            cs = slice(c0, c0 + ROWS_OUT)
            sums = jnp.zeros((ROWS_OUT, columns), jnp.float32)
            squares = sums
            edge = None
            for r in range(height):
                ls = slice(r * columns, (r + 1) * columns)
                left = pltpu.roll(tbuf[c0 : c0 + ROWS_OUT, ls], 1, 1)
                mid = tbuf[channels + c0 : channels + c0 + ROWS_OUT, ls]
                right = pltpu.roll(
                    tbuf[2 * channels + c0 : 2 * channels + c0 + ROWS_OUT, ls], columns - 1, 1
                )
                z = (
                    jnp.where(lane > 0, left, 0.0)
                    + mid
                    + jnp.where(lane < columns - 1, right, 0.0)
                    + bias_b[m, cs]
                )
                z = jnp.where(is_odd, skip[m, r, cs].astype(jnp.float32) + z, z)
                value = jnp.where(r < height_own, z, 0.0).astype(jnp.bfloat16)
                obuf[m, r, cs] = value
                wide = value.astype(jnp.float32)
                sums = sums + wide
                squares = squares + wide * wide
                edge = value if r == 0 else jnp.where(height_own == r + 1, value, edge)
            edge_out[m, cs] = edge
            sum_b[cs] = sums
            sq_b[cs] = squares

        @pl.when(jnp.logical_not(last))
        def _():
            send_rows(
                m, k + 1, obuf.at[m, 0], edge_out.at[m], obuf.at[m, 1], ends_ss.at[m], mid_ss.at[m]
            )
            write_stats(stat_out.at[m], sum_b[...], sq_b[...])
            send_stats(m, k + 1, stat_out.at[m], stat_ss.at[m], None)

        if sections > 2:
            @pl.when(has_far)
            def _():
                remote(obuf.at[m], skip.at[m], skip_ss.at[m], skip_rs.at[m], k + 2, p).start()

        pltpu.make_async_copy(obuf.at[m], out_ref.at[m], out_sem.at[m]).start()
        return carry

    lax.fori_loop(0, sections, sample, 0)

    wait_for(stat_in.at[0, pl.ds(1, patches - 1)], first_sem.at[0])

    @pl.when(k > 0)
    def _():
        wait_for(stat_lat, first_sem.at[0])
        wait_for(xbuf.at[0, pl.ds(0, 2)], first_sem.at[1])
        wait_for(edge_lat, first_sem.at[2])

    @pl.when(k != 1)
    def _():
        wait_for(lat, first_sem.at[3])

    def drain(m, carry):
        @pl.when(p < patches - 1)
        def _():
            wait_for(edge_lat, up_ss.at[m])

        @pl.when(p > 0)
        def _():
            wait_for(edge_lat, low_ss.at[m])

        @pl.when(jnp.logical_not(last))
        def _():
            wait_for(xbuf.at[m, pl.ds(0, 2)], ends_ss.at[m])
            wait_for(edge_lat, mid_ss.at[m])
            wait_for(stat_in.at[m], stat_ss.at[m])

        if sections > 2:
            @pl.when(has_far)
            def _():
                wait_for(obuf.at[m], skip_ss.at[m])

        wait_for(obuf.at[m], out_sem.at[m])
        return carry

    lax.fori_loop(0, sections, drain, 0)


def paired_kernel(
    patches,
    local,
    heights_in,
    latent_ref,
    weight_ref,
    gain_ref,
    shift_ref,
    bias_ref,
    out_ref,
    lat,
    weights,
    wall,
    part,
    xin,
    xmid,
    ends,
    heights_ref,
    gain_v,
    shift_v,
    bias_v,
    params,
    params_in,
    stat_lat,
    stat_mate,
    stat_all,
    total_out,
    total_in,
    stat_mid,
    stat_mid_all,
    gain_b,
    shift_b,
    bias_b,
    ybuf,
    tbuf,
    sum_b,
    sq_b,
    load_sem,
    ready,
    greeted,
    small_rs,
    small_ss,
    row_rs,
    row_ss,
    edge_rs,
    edge_ss,
    seed_rs,
    seed_ss,
    share_rs,
    share_ss,
    core_rs,
    core_ss,
    mid_rs,
    mid_ss,
    own_edge_rs,
    own_edge_ss,
    far_edge_rs,
    far_edge_ss,
    late_rs,
    late_ss,
    late_edge_rs,
    late_edge_ss,
    stat_rs,
    stat_ss,
):
    k = lax.axis_index("section")
    p = lax.axis_index("patch")
    height, channels, columns = lat.shape
    per_group = channels // GROUPS
    rest = channels - local
    lead = channels * 4 // 5
    lag = channels - lead
    piece = part.shape[0] // (8 * SUB)

    core = lax.rem(p, 2)
    mate = p + 1 - 2 * core
    across = p - 1 + 2 * core
    has_across = jnp.logical_and(across >= 0, across < patches)
    member = lax.rem(p, 8)
    turn_y = 2 - 4 * lax.rem(member // 2, 2)
    turn_z = 4 - 8 * (member // 4)
    friends = (p + turn_y, p + turn_z, p + turn_y + turn_z)

    load_h = pltpu.make_async_copy(heights_in, heights_ref, load_sem.at[0])
    load_lat = pltpu.make_async_copy(latent_ref, lat, load_sem.at[1])
    load_g = pltpu.make_async_copy(gain_ref, gain_v, load_sem.at[2])
    load_s = pltpu.make_async_copy(shift_ref, shift_v, load_sem.at[3])
    load_b = pltpu.make_async_copy(bias_ref, bias_v, load_sem.at[4])
    load_w = [
        pltpu.make_async_copy(
            weight_ref.at[:, :, span], weights.at[:, :, span], load_sem.at[5 + i]
        )
        for i, span in enumerate((pl.ds(0, local), pl.ds(local, rest)))
    ]

    barrier = pltpu.get_barrier_semaphore()

    def signal(s, q):
        pl.semaphore_signal(barrier, inc=1, device_id=(s, q), device_id_type=MESH)

    load_h.start()
    load_lat.start()
    load_w[0].start()

    @pl.when(k == 0)
    def _():
        signal(1, p)

        def step(i, carry):
            signal(0, lax.rem(p + i, patches))
            return carry

        lax.fori_loop(1, patches, step, 0)

    partners = [(q, True) for q in (mate, *friends)] + [(across, has_across)]

    def count(higher):
        total = 0
        for q, exists in partners:
            total = total + jnp.logical_and(exists, (q > p) == higher).astype(jnp.int32)
        return total

    @pl.when(k == 1)
    def _():
        for q, exists in partners:
            @pl.when(jnp.logical_and(exists, q > p))
            def _():
                signal(1, q)

        pl.semaphore_wait(barrier, 1 + count(False))
        pl.semaphore_signal(ready, inc=1, device_id=(0, p), device_id_type=MESH)
        for q, exists in partners:
            @pl.when(jnp.logical_and(exists, q < p))
            def _():
                pl.semaphore_signal(greeted, inc=1, device_id=(1, q), device_id_type=MESH)

    for load in (load_g, load_s, load_b, load_w[1]):
        load.start()

    def remote(src, dst, ssem, rsem, s, q):
        return pltpu.make_async_remote_copy(
            src_ref=src, dst_ref=dst, send_sem=ssem, recv_sem=rsem,
            device_id=(s, q), device_id_type=MESH,
        )

    def wait_for(ref, sem):
        pltpu.make_async_copy(ref, ref, sem).wait()

    load_h.wait()
    height_own = heights_ref[p]
    window_rows = heights_ref[0]
    for i in range(1, patches):
        window_rows = window_rows + heights_ref[i]
    inv_count = 1.0 / (
        jnp.full((1, 128), window_rows, jnp.int32).astype(jnp.float32)
        * (per_group * columns)
    )

    chan = lax.broadcasted_iota(jnp.int32, (channels, 128), 0)
    first = lax.broadcasted_iota(jnp.int32, (channels, 128), 1) * per_group
    group_mask = jnp.where(
        jnp.logical_and(chan >= first, chan < first + per_group), 1.0, 0.0
    ).astype(jnp.float32)

    def to_groups(per_chan):
        total = jnp.sum(per_chan, axis=1, keepdims=True)
        return jnp.sum(total * group_mask, axis=0, keepdims=True)

    def to_channels(per_group_row):
        return jnp.sum(per_group_row * group_mask, axis=1, keepdims=True)

    def both(sums, squares):
        return to_groups(sums) + pltpu.roll(to_groups(squares), GROUPS, 1)

    load_lat.wait()
    rows = [
        jnp.where(r < height_own, lat[r].astype(jnp.float32), 0.0) for r in range(height)
    ]
    sums, squares, edge = rows[0], rows[0] * rows[0], lat[0]
    for r in range(1, height):
        sums = sums + rows[r]
        squares = squares + rows[r] * rows[r]
        edge = jnp.where(height_own == r + 1, lat[r], edge)
    xin[k, 1] = lat[0]
    xin[k, 2] = edge
    xin[k, 3] = lat[1]
    stat_lat[...] = both(sums, squares)

    def take_params():
        load_g.wait()
        load_s.wait()
        load_b.wait()
        params[0:1] = gain_v[...].astype(jnp.float32)
        params[1:2] = shift_v[...].astype(jnp.float32)
        params[2:4] = bias_v[...].astype(jnp.float32)

    eye = jnp.where(
        lax.broadcasted_iota(jnp.int32, (channels, channels), 0)
        == lax.broadcasted_iota(jnp.int32, (channels, channels), 1),
        1.0,
        0.0,
    ).astype(jnp.bfloat16)

    def spread(row):
        wide = jnp.broadcast_to(row, (128, channels)).astype(jnp.bfloat16)
        return lax.dot_general(
            eye, wide, (((1,), (1,)), ((), ())), preferred_element_type=jnp.float32
        )

    def spread_params(at, source):
        gain_b[at] = spread(source[0:1])
        shift_b[at] = spread(source[1:2])
        for m in range(2):
            bias_b[at, m] = spread(source[2 + m : 3 + m])

    def depth(a, c):
        return a * lead + c if c < lead else 3 * lead + a * lag + c - lead

    def build(is_rest):
        for b in range(3):
            for a in range(3):
                for lo, hi in ((0, lead), (lead, channels)):
                    at = depth(a, lo)
                    cols = slice(at, at + hi - lo)
                    if is_rest:
                        start = 3 * local + b * rest
                        wall[start : start + rest, cols] = weights[b, a, local:, lo:hi]
                    else:
                        wall[b * local : (b + 1) * local, cols] = weights[b, a, :local, lo:hi]

    cross_slot, other_slot = 1 + core, 2 - core

    def send_rows():
        for i, slot in enumerate((cross_slot, other_slot, 3)):
            remote(xin.at[k, slot], xin.at[k, slot], row_ss.at[i], row_rs.at[i], 1 - k, p).start()

    def wait_row(i):
        wait_for(lat.at[0], row_rs.at[i])

    def send_edge(kind, ref, m, span, ssem, rsem):
        src_slot = cross_slot if kind == 0 else other_slot
        dst_slot = 4 - 4 * core if kind == 0 else 4 * core
        q = across if kind == 0 else mate

        def go():
            remote(
                ref.at[m, src_slot, span], ref.at[m, dst_slot, span],
                ssem.at[m, kind], rsem.at[m, kind], k, q,
            ).start()

        if kind == 0:
            pl.when(has_across)(go)
        else:
            go()

    def wait_edge(kind, ref, sem, m):
        if kind == 0:
            @pl.when(has_across)
            def _():
                wait_for(ref, sem.at[m, kind])
        else:
            wait_for(ref, sem.at[m, kind])

    whole = pl.ds(0, channels)
    head_part = pl.ds(0, local)
    tail_part = pl.ds(local, rest)
    early_part = pl.ds(local, lead - local)
    late_part = pl.ds(lead, lag)

    def pass_in(kind, m):
        send_edge(kind, xin, m, whole, edge_ss, edge_rs)

    def coefficients(total, at):
        mean = total * inv_count
        var = pltpu.roll(mean, 128 - GROUPS, 1) - mean * mean
        inv = lax.rsqrt(jnp.maximum(var, 0.0) + EPS)
        scale = to_channels(inv) * gain_b[at]
        return scale, shift_b[at] - to_channels(mean) * scale

    def fill(rows_of, m, scale, offset, before_edges, low=0, high=channels):
        def activate(slot):
            v = rows_of[m, slot, low:high].astype(jnp.float32) * scale[low:high] + offset[low:high]
            half = 0.5 * v
            return half + half * jnp.tanh(half)

        def put(j, value):
            value = value.astype(jnp.bfloat16)
            for a in range(3):
                r = j - a
                if 0 <= r < height:
                    at = (m * height + r) * columns
                    for lo, hi in ((low, min(high, lead)), (max(low, lead), high)):
                        if lo < hi:
                            start = depth(a, lo)
                            ybuf[start : start + hi - lo, at : at + columns] = value[lo - low : hi - low]

        put(1, activate(1))
        tail = activate(2)
        mid = activate(3)
        before_edges()
        put(0, jnp.where(p > 0, activate(0), 0.0))
        below = jnp.where(p < patches - 1, activate(4), 0.0)
        one, two = height_own == 1, height_own == 2
        put(2, jnp.where(one, below, jnp.where(two, tail, mid)))
        put(3, jnp.where(one, 0.0, jnp.where(two, below, tail)))
        put(4, jnp.where(height_own == 3, below, 0.0))

    lane = lax.broadcasted_iota(jnp.int32, (ROWS_OUT, columns), 1)

    def conv_row(m, r, c0, count, bias):
        at = (m * height + r) * columns
        ls = slice(at, at + columns)

        def block(b):
            start = b * local + c0 if c0 < local else 3 * local + b * rest + c0 - local
            return tbuf[start : start + count, ls]

        return (
            jnp.where(lane > 0, pltpu.roll(block(0), 1, 1), 0.0)
            + block(1)
            + jnp.where(lane < columns - 1, pltpu.roll(block(2), columns - 1, 1), 0.0)
            + bias
        )

    def far(m, is_late):
        if m == 0:
            return tail_part, mid_ss.at[0], mid_rs.at[0], far_edge_ss.at[0], far_edge_rs.at[0]
        if is_late:
            return late_part, late_ss, late_rs, late_edge_ss, late_edge_rs
        return early_part, mid_ss.at[1], mid_rs.at[1], far_edge_ss.at[1], far_edge_rs.at[1]

    def send_mid(i, m, is_late=False):
        span, ssem, rsem, _, _ = far(m, is_late)
        src = (ends.at[m, core], ends.at[m, 1 - core], out_ref.at[m, 1])[i]
        slot = (cross_slot, other_slot, 3)[i]
        remote(src.at[span], xmid.at[m, slot, span], ssem.at[i], rsem.at[i], 1, p).start()

    def send_across(is_late):
        span, _, _, ssem, rsem = far(1, is_late)

        @pl.when(has_across)
        def _():
            remote(
                ends.at[1, core, span], xmid.at[1, 4 - 4 * core, span],
                ssem.at[0], rsem.at[0], 1, across,
            ).start()

    def wait_far(i, m, is_late=False):
        span, _, rsem, _, _ = far(m, is_late)
        wait_for(out_ref.at[m, 1, span], rsem.at[i])

    def wait_far_edges(m, is_late=False):
        span, _, _, _, rsem = far(m, is_late)

        @pl.when(has_across)
        def _():
            wait_for(lat.at[0, span], rsem.at[0])

        wait_for(lat.at[0, span], rsem.at[1])

    def pass_far(kind, m, is_late=False):
        span, _, _, ssem, rsem = far(m, is_late)
        wait_far(kind, m, is_late)
        src_slot = cross_slot if kind == 0 else other_slot
        dst_slot = 4 - 4 * core if kind == 0 else 4 * core
        q = across if kind == 0 else mate

        def go():
            remote(
                xmid.at[m, src_slot, span], xmid.at[m, dst_slot, span],
                ssem.at[kind], rsem.at[kind], 1, q,
            ).start()

        if kind == 0:
            pl.when(has_across)(go)
        else:
            go()

    def multiply(count, m0, samples, low=0, high=3 * channels):
        cols = slice(m0 * height * columns, (m0 + samples) * height * columns)
        left = wall if count > 3 * local else part
        product = jnp.dot(
            left[:, low:high], ybuf[low:high, cols], preferred_element_type=jnp.float32
        )
        tbuf[:count, cols] = product if low == 0 else tbuf[:count, cols] + product

    @pl.when(k == 1)
    def _():
        remote(stat_lat, stat_mate, small_ss.at[1], small_rs.at[1], 0, p).start()
        send_rows()

        @pl.when(count(True) > 0)
        def _():
            pl.semaphore_wait(greeted, count(True))

        pass_in(0, 1)
        pass_in(1, 1)
        take_params()
        spread_params(0, params)
        load_w[0].wait()
        build(False)
        load_w[1].wait()
        build(True)

    @pl.when(k == 0)
    def _():
        take_params()
        load_w[0].wait()
        build(False)
        pl.semaphore_wait(ready, 1)
        remote(params, params_in, small_ss.at[0], small_rs.at[0], 1, p).start()
        for i in range(SUB):
            at = pl.ds((member * SUB + i) * piece, piece)
            remote(wall.at[at], part.at[at], seed_ss.at[i], seed_rs.at[i], 1, p).start()
        send_rows()
        pl.semaphore_wait(barrier, patches - 1)

        def share_stats(m, source):
            def step(i, carry):
                q = lax.rem(p + i, patches)
                remote(
                    source, stat_all.at[m, p], small_ss.at[2 + m], small_rs.at[2 + m], 0, q
                ).start()
                return carry

            lax.fori_loop(1, patches, step, 0)
            stat_all[m, p] = source[...]

        def total_of(m):
            wait_for(stat_all.at[m, pl.ds(0, patches - 1)], small_rs.at[2 + m])
            total = jnp.sum(stat_all[m], axis=0)
            total_out[m] = total
            remote(
                total_out.at[m], total_in.at[m], small_ss.at[4 + m], small_rs.at[4 + m], 1, p
            ).start()
            return total

        share_stats(0, stat_lat)
        pass_in(0, 0)
        pass_in(1, 0)
        spread_params(0, params)
        load_w[1].wait()
        build(True)
        wait_for(stat_lat, small_rs.at[1])
        share_stats(1, stat_mate)
        wait_row(0)
        pass_in(0, 1)

        total = total_of(0)
        for m in range(2):
            scale, offset = coefficients(total, 0)

            def before_edges():
                if m == 0:
                    wait_row(1)
                    pass_in(1, 1)
                for kind in range(2):
                    wait_edge(kind, lat.at[0], edge_rs, m)

            if m == 1:
                wait_row(2)
            fill(xin, m, scale, offset, before_edges)
            multiply(3 * channels, m, 1)
            for c0 in range(0, channels, ROWS_OUT):
                cs = slice(c0, c0 + ROWS_OUT)
                sums = jnp.zeros((ROWS_OUT, columns), jnp.float32)
                squares = sums
                edge = None
                for r in range(height):
                    z = conv_row(m, r, c0, ROWS_OUT, bias_b[0, m, cs])
                    value = jnp.where(r < height_own, z, 0.0).astype(jnp.bfloat16)
                    out_ref[m, r, cs] = value
                    wide = value.astype(jnp.float32)
                    sums = sums + wide
                    squares = squares + wide * wide
                    edge = value if r == 0 else jnp.where(height_own == r + 1, value, edge)
                    if r == 0:
                        ends[m, 0, cs] = value
                ends[m, 1, cs] = edge
                sum_b[cs] = sums
                sq_b[cs] = squares
            stat_mid[m] = both(sum_b[...], sq_b[...])

            def step(i, carry):
                q = lax.rem(p + i, patches)
                remote(stat_mid.at[m], stat_mid_all.at[m, p], stat_ss.at[m], stat_rs.at[m], 1, q).start()
                return carry

            if m == 0:
                send_mid(0, m)
            lax.fori_loop(0, patches, step, 0)
            if m == 1:
                send_across(False)
                send_mid(0, m)
            if m == 0:
                total = total_of(1)
                send_mid(1, 0)
        send_mid(2, 0)
        send_mid(1, 1)
        send_mid(2, 1)
        send_across(True)
        send_mid(1, 1, True)
        send_mid(0, 1, True)
        send_mid(2, 1, True)

        wait_for(params, small_ss.at[0])
        for m in range(2):
            wait_for(stat_all.at[m, pl.ds(0, patches - 1)], small_ss.at[2 + m])
            wait_for(total_out.at[m], small_ss.at[4 + m])
        for i in range(SUB):
            wait_for(part.at[pl.ds(0, piece)], seed_ss.at[i])
        for m, is_late in ((0, False), (1, False), (1, True)):
            span, ssem, _, edge_sem, _ = far(m, is_late)
            for i in range(3):
                wait_for(out_ref.at[m, 1, span], ssem.at[i])
            if m == 1:
                @pl.when(has_across)
                def _():
                    wait_for(lat.at[0, span], edge_sem.at[0])
        for m in range(2):
            wait_for(stat_mid_all.at[m], stat_ss.at[m])

    @pl.when(k == 1)
    def _():
        def to_mate(index, sem):
            at = pl.ds(index * piece, piece)
            remote(part.at[at], part.at[at], core_ss.at[sem], core_rs.at[0], 1, mate).start()

        def seed(i, carry):
            index = member * SUB + i
            at = pl.ds(index * piece, piece)
            wait_for(part.at[pl.ds(0, piece)], seed_rs.at[i])
            for j in range(3):
                remote(
                    part.at[at], part.at[at], share_ss.at[j, i], share_rs.at[j, i], 1, friends[j]
                ).start()
            to_mate(index, i)
            return carry

        lax.fori_loop(0, SUB, seed, 0)
        wait_for(params, small_rs.at[0])
        spread_params(1, params_in)
        wait_row(0)
        pass_in(0, 0)

        def shared(i, carry):
            for j in range(3):
                wait_for(part.at[pl.ds(0, piece)], share_rs.at[j, i])
                to_mate(lax.rem(friends[j], 8) * SUB + i, (1 + j) * SUB + i)
            return carry

        lax.fori_loop(0, SUB, shared, 0)
        wait_row(1)
        pass_in(1, 0)
        wait_row(2)

        for m in range(2):
            if m == 0:
                pass_far(0, 0)
            wait_for(total_out.at[m], small_rs.at[4 + m])
            scale, offset = coefficients(total_in[m], 1)

            def before_edges():
                for kind in range(2):
                    wait_edge(kind, lat.at[0], edge_rs, m)

            fill(xin, m, scale, offset, before_edges)
            if m == 0:
                wait_for(part.at[pl.ds(0, 4 * SUB * piece)], core_rs.at[0])
            multiply(3 * local, m, 1)
            for c0 in range(0, local, ROWS_OUT):
                cs = slice(c0, c0 + ROWS_OUT)
                edge = None
                for r in range(height):
                    value = conv_row(m, r, c0, ROWS_OUT, bias_b[1, m, cs]).astype(jnp.bfloat16)
                    edge = value if r == 0 else jnp.where(height_own == r + 1, value, edge)
                    if r == 0:
                        xmid[m, 1, cs] = value
                    if r == 1:
                        xmid[m, 3, cs] = value
                xmid[m, 2, cs] = edge
            for kind in range(2):
                send_edge(kind, xmid, m, head_part, own_edge_ss, own_edge_rs)
            if m == 0:
                pass_far(1, 0)

        for m in range(2):
            wait_for(stat_mid_all.at[m], stat_rs.at[m])
            scale, offset = coefficients(jnp.sum(stat_mid_all[m], axis=0), 0)

            def before_edges():
                if m == 0:
                    pass_far(1, 1)
                for kind in range(2):
                    wait_edge(kind, lat.at[0, head_part], own_edge_rs, m)
                wait_far_edges(m)

            wait_far(2, m)
            if m == 0:
                fill(xmid, 0, scale, offset, before_edges)
                multiply(3 * channels, 0, 1)
                pass_far(1, 1, True)
            else:
                wait_far(0, 1)
                fill(xmid, 1, scale, offset, before_edges, 0, lead)
                multiply(3 * channels, 1, 1, 0, 3 * lead)
                wait_far(0, 1, True)
                wait_far(2, 1, True)
                fill(xmid, 1, scale, offset, lambda: wait_far_edges(1, True), lead, channels)
                multiply(3 * channels, 1, 1, 3 * lead, 3 * channels)
            for c0 in range(0, channels, ROWS_OUT):
                cs = slice(c0, c0 + ROWS_OUT)
                for r in range(height):
                    z = conv_row(m, r, c0, ROWS_OUT, bias_b[0, m, cs])
                    z = xin[m, (1, 3, 2)[r], cs].astype(jnp.float32) + z
                    out_ref[m, r, cs] = jnp.where(r < height_own, z, 0.0).astype(jnp.bfloat16)

        wait_for(stat_lat, small_ss.at[1])
        for i in range(SUB):
            for j in range(3):
                wait_for(part.at[pl.ds(0, piece)], share_ss.at[j, i])
        for i in range(4 * SUB):
            wait_for(part.at[pl.ds(0, piece)], core_ss.at[i])
        for m in range(2):
            for kind in range(2):
                wait_edge(kind, lat.at[0, head_part], own_edge_ss, m)
        wait_edge(0, lat.at[0, tail_part], far_edge_ss, 0)
        for m, is_late in ((0, False), (1, False), (1, True)):
            span, _, _, sem, _ = far(m, is_late)
            wait_for(lat.at[0, span], sem.at[1])

    for i in range(3):
        wait_for(lat.at[0], row_ss.at[i])
    for m in range(2):
        for kind in range(2):
            wait_edge(kind, lat.at[0], edge_ss, m)


def paired_call(patches, operands, height, channels, columns):
    bf16, f32 = jnp.bfloat16, jnp.float32
    local = channels * 2 // 5
    hbm = pl.BlockSpec(memory_space=pltpu.HBM)
    dma = pltpu.SemaphoreType.DMA
    return pl.pallas_call(
        functools.partial(paired_kernel, patches, local),
        out_shape=jax.ShapeDtypeStruct((2, height, channels, columns), bf16),
        in_specs=[hbm] * 6,
        out_specs=pl.BlockSpec(memory_space=pltpu.VMEM),
        scratch_shapes=[
            pltpu.VMEM((height, channels, columns), bf16),
            pltpu.VMEM((3, 3, channels, channels), bf16),
            pltpu.VMEM((3 * channels, 3 * channels), bf16),
            pltpu.VMEM((3 * local, 3 * channels), bf16),
            pltpu.VMEM((2, height + 2, channels, columns), bf16),
            pltpu.VMEM((2, height + 2, channels, columns), bf16),
            pltpu.VMEM((2, 2, channels, columns), bf16),
            pltpu.SMEM((patches,), jnp.int32),
            pltpu.VMEM((1, channels), bf16),
            pltpu.VMEM((1, channels), bf16),
            pltpu.VMEM((2, channels), bf16),
            pltpu.VMEM((8, channels), f32),
            pltpu.VMEM((8, channels), f32),
            pltpu.VMEM((1, 128), f32),
            pltpu.VMEM((1, 128), f32),
            pltpu.VMEM((2, patches, 1, 128), f32),
            pltpu.VMEM((2, 1, 128), f32),
            pltpu.VMEM((2, 1, 128), f32),
            pltpu.VMEM((2, 1, 128), f32),
            pltpu.VMEM((2, patches, 1, 128), f32),
            pltpu.VMEM((2, channels, 128), f32),
            pltpu.VMEM((2, channels, 128), f32),
            pltpu.VMEM((2, 2, channels, 128), f32),
            pltpu.VMEM((3 * channels, 2 * height * columns), bf16),
            pltpu.VMEM((3 * channels, 2 * height * columns), f32),
            pltpu.VMEM((channels, columns), f32),
            pltpu.VMEM((channels, columns), f32),
            dma((7,)),
            pltpu.SemaphoreType.REGULAR,
            pltpu.SemaphoreType.REGULAR,
            dma((6,)),
            dma((6,)),
            dma((3,)),
            dma((3,)),
            dma((2, 2)),
            dma((2, 2)),
            dma((SUB,)),
            dma((SUB,)),
            dma((3, SUB)),
            dma((3, SUB)),
            dma((1,)),
            dma((4 * SUB,)),
            dma((2, 3)),
            dma((2, 3)),
            dma((2, 2)),
            dma((2, 2)),
            dma((2, 2)),
            dma((2, 2)),
            dma((3,)),
            dma((3,)),
            dma((2,)),
            dma((2,)),
            dma((2,)),
            dma((2,)),
        ],
        compiler_params=pltpu.CompilerParams(
            collective_id=0, has_side_effects=True, vmem_limit_bytes=48 * 1024 * 1024
        ),
    )(*operands)


def per_device(sections, patches, latent, conv_weight, norm_gain, norm_shift, step_bias, patch_rows):
    latent = jnp.transpose(latent[0], (1, 0, 2))
    weight = jnp.transpose(conv_weight[0], (0, 2, 1, 3))
    height, channels, columns = latent.shape
    bf16, f32 = jnp.bfloat16, jnp.float32
    hbm = pl.BlockSpec(memory_space=pltpu.HBM)
    dma = pltpu.SemaphoreType.DMA
    operands = [
        pltpu.with_memory_space_constraint(array, pltpu.HBM)
        for array in (patch_rows, latent, weight, norm_gain, norm_shift, step_bias[0])
    ]
    if sections == 2 and patches % 8 == 0:
        out = paired_call(patches, operands, height, channels, columns)
        return jnp.transpose(out, (0, 2, 1, 3))[None]
    out = pl.pallas_call(
        functools.partial(kernel, sections, patches),
        out_shape=jax.ShapeDtypeStruct((sections, height, channels, columns), bf16),
        in_specs=[hbm] * 6,
        out_specs=pl.BlockSpec(memory_space=pl.ANY),
        scratch_shapes=[
            pltpu.VMEM((height, channels, columns), bf16),
            pltpu.VMEM((3, 3, channels, channels), bf16),
            pltpu.VMEM((3 * channels, 3 * channels), bf16),
            pltpu.VMEM((sections, height + 2, channels, columns), bf16),
            pltpu.VMEM((sections, height, channels, columns), bf16),
            pltpu.VMEM((sections, height, channels, columns), bf16),
            pltpu.VMEM((channels, columns), bf16),
            pltpu.VMEM((sections, channels, columns), bf16),
            pltpu.SMEM((patches,), jnp.int32),
            pltpu.VMEM((1, channels), bf16),
            pltpu.VMEM((1, channels), bf16),
            pltpu.VMEM((sections, channels), bf16),
            pltpu.VMEM((1, 128), f32),
            pltpu.VMEM((sections, 1, 128), f32),
            pltpu.VMEM((sections, patches, 1, 128), f32),
            pltpu.VMEM((channels, 128), f32),
            pltpu.VMEM((channels, 128), f32),
            pltpu.VMEM((sections, channels, 128), f32),
            pltpu.VMEM((3 * channels, height * columns), bf16),
            pltpu.VMEM((3 * channels, height * columns), f32),
            pltpu.VMEM((channels, columns), f32),
            pltpu.VMEM((channels, columns), f32),
            dma((6,)),
            dma((4,)),
        ]
        + [dma((sections,)) for _ in range(13)],
        compiler_params=pltpu.CompilerParams(
            collective_id=0, has_side_effects=True, vmem_limit_bytes=48 * 1024 * 1024
        ),
    )(*operands)
    return jnp.transpose(out, (0, 2, 1, 3))[None]


def solution(mesh):
    placed = (
        P("section", None, "patch", None),
        P("section", None, None, None, None),
        P("section", None),
        P("section", None),
        P("section", None, None),
        P(),
    )
    return jax.shard_map(
        functools.partial(per_device, mesh.shape["section"], mesh.shape["patch"]),
        mesh=mesh,
        in_specs=placed,
        out_specs=P("section", None, None, "patch", None),
        check_vma=False,
    )
```
